32 devices in a mesh: rep: 4 (over y, x), shard: 8 (over z, core).
Axes of the slice: x: 2, y: 2, z: 4, core: 2. Of those that a mesh axis runs over, the one named last changes fastest.
Arguments:
- tokens: bfloat16 [32, 1024, 768], P(('rep', 'shard')), may hold values from -6 to 6
- segment_ids: int32 [32, 1024], P(('rep', 'shard')), may hold values from 0 to 15, never falling along the last dimension, each value on 1 to 512 neighbouring positions
- qkv_weight: bfloat16 [768, 2304], P(None, 'shard'), may hold values from -0.15605632 to 0.15605632
- out_weight: bfloat16 [768, 768], P('shard'), may hold values from -0.4375 to 0.4375
- up_weight: bfloat16 [768, 3072], P(None, 'shard'), may hold values from -0.21875 to 0.21875
- down_weight: bfloat16 [3072, 768], P('shard'), may hold values from -0.109375 to 0.109375
- norm1_gain: bfloat16 [768], P('shard'), may hold values from 0.5 to 1.5
- norm1_shift: bfloat16 [768], P('shard'), may hold values from -2.5 to 2.5
- norm2_gain: bfloat16 [768], P('shard'), may hold values from 0.5 to 1.5
- norm2_shift: bfloat16 [768], P('shard'), may hold values from -2.5 to 2.5
- cotangent: bfloat16 [32, 1024, 768], P(('rep', 'shard')), may hold values from -6 to 6
Outputs:
- output: bfloat16 [32, 1024, 768], P(('rep', 'shard'))
- tokens_grad: bfloat16 [32, 1024, 768], P(('rep', 'shard'))
- qkv_weight_grad: float32 [768, 2304], P(None, 'shard')
- out_weight_grad: float32 [768, 768], P('shard')
- up_weight_grad: float32 [768, 3072], P(None, 'shard')
- down_weight_grad: float32 [3072, 768], P('shard')
- norm1_gain_grad: float32 [768], P('shard')
- norm1_shift_grad: float32 [768], P('shard')
- norm2_gain_grad: float32 [768], P('shard')
- norm2_shift_grad: float32 [768], P('shard')
The draws below stay inside these ranges and needn't reach their ends.
Inputs may be any that keep to these rules, and one draw needn't show every extreme that they name: `segment_ids`: within each sequence the ids never fall, every id of 0 to 15 is used, each document is a run of 1 to 512 slots, and the longest document of a draw has exactly 512 slots.
All inputs are finite; a program needn't handle non-finite values.
Results may differ from the reference program's by a relative error of at most 0.015.
Values may be sent and summed in bfloat16 or wider, within the bound.
A program may use at most 256 MiB of HBM per device.

```python
import math
import jax
import jax.numpy as jnp
import numpy as np
from jax import lax

HEADS = 12
HEAD_DIM = 64
D = 768
FF = 3072
TOK_DEV = 1024
SEQS = 32
DOCS = 16
DOC_MOST = 512


def shift_vector(key):
    shift_key = jax.random.fold_in(key, 7101)
    return 0.5 * jax.random.truncated_normal(shift_key, -5.0, 5.0, (D,), jnp.float32)


def draw_norm1_shift(key, part):
    return shift_vector(key).astype(jnp.bfloat16)


def draw_qkv_weight(key, part):
    shift_row = shift_vector(key)
    base_key = jax.random.fold_in(key, 7102)
    sign_key = jax.random.fold_in(key, 7103)
    weights = jax.random.truncated_normal(base_key, -4.0, 4.0, (D, 3 * D), jnp.float32) * D ** (-0.5)
    sign_row = jnp.where(jax.random.bernoulli(sign_key, 0.5, (HEAD_DIM,)), 1.0, -1.0).astype(jnp.float32)
    rank_term = shift_row[:, None] * sign_row[None, :] * (3.5 / D)
    weights = weights.at[:, 0:HEAD_DIM].add(rank_term)
    weights = weights.at[:, D:D + HEAD_DIM].add(-rank_term)
    return weights.astype(jnp.bfloat16)


def block_levels(key, dims, pieces, smallest, top_value):
    def one(dim, parts):
        steps = jax.random.uniform(jax.random.fold_in(jax.random.fold_in(key, 6), dim), (parts,), jnp.float32, smallest / len(pieces), top_value / len(pieces))
        return jnp.repeat(jnp.exp(steps), dims[dim] // parts).reshape((-1,) + (1,) * (len(dims) - dim - 1))

    factor_of = one(*pieces[0])
    for cut in pieces[1:]:
        factor_of = factor_of * one(*cut)
    return factor_of


def profile(count, total, bound, slope):
    portions = [(1 << 20) // math.isqrt(grade ** slope) + 1 for grade in range(2, count + 1)]
    spare, given = total - bound - (count - 1), [1] * (count - 1)
    while spare > 0:
        movable = [i for i in range(count - 1) if given[i] < bound]
        mass, budget = sum([portions[i] for i in movable]), spare
        for i in movable:
            addition = min(bound - given[i], max(1, budget * portions[i] // mass), spare)
            given[i] = given[i] + addition
            spare = spare - addition
    return np.array([bound] + given)


def uneven(own_key, number_of, total, limit, skew):
    if number_of == 2:
        one = jax.random.randint(own_key, (), max(1, total - limit), min(limit, total - 1) + 1)
        return jnp.stack([one, total - one])
    lengths = jnp.asarray(profile(number_of, total, limit, skew), jnp.int32)
    pairs = (number_of - 1) // 2
    giver, receiver = lengths[1:1 + 2 * pairs:2], lengths[2:2 + 2 * pairs:2]
    room = jnp.minimum(giver - 1, limit - receiver)
    moved = jax.random.randint(jax.random.fold_in(own_key, 1), (pairs,), 0, 1 << 20) % (room + 1)
    lengths = lengths.at[1:1 + 2 * pairs:2].set(giver - moved).at[2:2 + 2 * pairs:2].set(receiver + moved)
    return lengths[jax.random.permutation(jax.random.fold_in(own_key, 2), number_of)]


def centred(own_key, extent, deviation, bound, cuts=(), held_as=jnp.bfloat16):
    values = jax.random.normal(own_key, extent, jnp.float32) * deviation
    if len(cuts) > 0:
        values = block_levels(own_key, extent, cuts, -0.22, 0.18) * values
    return jnp.clip(values, min=-bound, max=bound).astype(held_as)


def setup_inputs(seed: int = 0) -> dict:
    key_list = jax.random.split(jax.random.key(seed), 12)
    return {
        "tokens": centred(key_list[0], (SEQS, TOK_DEV, D), 1.0, 6.0, ((0, 32),)),
        "segment_ids": jax.vmap(lambda own: jnp.searchsorted(jnp.cumsum(uneven(own, DOCS, TOK_DEV, DOC_MOST, 2)), jnp.arange(TOK_DEV), side="right"))(jax.random.split(key_list[1], SEQS)).reshape((SEQS, TOK_DEV)).astype(jnp.int32),
        "qkv_weight": draw_qkv_weight(jax.random.fold_in(key_list[11], 71), 0),
        "out_weight": centred(key_list[3], (D, D), (D // 4) ** -0.5, 0.4375, ((0, 8),)),
        "up_weight": centred(key_list[4], (D, FF), D ** -0.5, 0.21875, ((1, 8),)),
        "down_weight": centred(key_list[5], (FF, D), FF ** -0.5, 0.109375, ((0, 8),)),
        "norm1_gain": jnp.clip(1.0 + 0.1 * jax.random.normal(key_list[6], (D,), jnp.float32), 0.5, 1.5).astype(jnp.bfloat16),
        "norm1_shift": draw_norm1_shift(jax.random.fold_in(key_list[11], 71), 0),
        "norm2_gain": jnp.clip(1.0 + 0.1 * jax.random.normal(key_list[8], (D,), jnp.float32), 0.5, 1.5).astype(jnp.bfloat16),
        "norm2_shift": centred(key_list[9], (D,), 0.5, 2.5, ((0, 8),)),
        "cotangent": centred(key_list[10], (SEQS, TOK_DEV, D), 1.0, 6.0, ((0, 32),)),
    }


@jax.custom_vjp
def low(v):
    return lax.optimization_barrier(v.astype(jnp.bfloat16)).astype(jnp.float32)

@jax.custom_vjp
def low_back(v):
    return v

def low_keep(v):
    return (low(v), None)

def low_pass(kept, grad):
    return (grad,)

def back_keep(v):
    return (v, None)

def back_low(kept, grad):
    return (low(grad),)
low.defvjp(low_keep, low_pass)
low_back.defvjp(back_keep, back_low)
highest = lax.Precision.HIGHEST
norm_eps = 1e-05
masked_value = -1e+30

def layer_norm(inputs, gain_vec, shift_vec):
    average = lax.optimization_barrier(jnp.mean(inputs, axis=-1, keepdims=True))
    center = inputs - average
    variance = lax.optimization_barrier(jnp.mean(center * center, axis=-1, keepdims=True))
    return center * lax.rsqrt(variance + norm_eps) * gain_vec + shift_vec

def attend(projected, segment):
    length = segment.shape[0]
    heads_view = projected.reshape(length, 3, HEADS, HEAD_DIM)
    queries = heads_view[:, 0]
    key_heads = heads_view[:, 1]
    values = heads_view[:, 2]
    scores = jnp.einsum('qhd,khd->hqk', queries, key_heads, precision=highest) * HEAD_DIM ** (-0.5)
    scores = low_back(scores)
    position = jnp.arange(length, dtype=jnp.int32)
    same_doc = segment[:, None] == segment[None, :]
    allowed = same_doc & (position[None, :] <= position[:, None])
    starts = jnp.concatenate([jnp.ones((1,), dtype=bool), segment[1:] != segment[:-1]])
    chosen = same_doc & (position[None, :] < position[:, None]) & jnp.logical_not(starts)[None, :]
    select = jnp.where(chosen, jax.nn.softplus(scores[0]), 0.0)
    running = jnp.cumsum(select, axis=0)
    penalty = jnp.concatenate([jnp.zeros((1, length), jnp.float32), running[:-1]], axis=0)
    logits = jnp.where(allowed[None], scores - penalty[None], masked_value)
    attention = low(jax.nn.softmax(logits, axis=-1))
    attended = jnp.einsum('hqk,khd->qhd', attention, values, precision=highest)
    return attended.reshape(length, HEADS * HEAD_DIM)

def attend_pair(seq_pair):
    return attend(seq_pair[0], seq_pair[1])

def forward(tokens, qkv_weight, out_weight, up_weight, down_weight, gain_one, shift_one, gain_two, shift_two, segment_ids):
    normed_one = low(layer_norm(tokens, gain_one, shift_one))
    projected = jnp.einsum('std,de->ste', normed_one, qkv_weight, precision=highest)
    projected = low(low_back(projected))
    attended = lax.map(jax.checkpoint(attend_pair), (projected, segment_ids))
    attended = low(low_back(attended))
    branch_out = jnp.einsum('std,de->ste', attended, out_weight, precision=highest)
    residual = tokens + low_back(branch_out)
    normed_two = low(layer_norm(residual, gain_two, shift_two))
    hidden = low_back(jnp.einsum('std,df->stf', normed_two, up_weight, precision=highest))
    active = low(jax.nn.gelu(hidden, approximate=True))
    return residual + jnp.einsum('stf,fd->std', active, down_weight, precision=highest)

def reference(tokens, segment_ids, qkv_weight, out_weight, up_weight, down_weight, norm1_gain, norm1_shift, norm2_gain, norm2_shift, cotangent):
    floats = tuple((array_in.astype(jnp.float32) for array_in in (tokens, qkv_weight, out_weight, up_weight, down_weight, norm1_gain, norm1_shift, norm2_gain, norm2_shift)))

    def closure(*params):
        return forward(*params, segment_ids)
    result, pullback = jax.vjp(closure, *floats)
    gradients = pullback(cotangent.astype(jnp.float32))
    return (result.astype(jnp.bfloat16), gradients[0].astype(jnp.bfloat16), gradients[1], gradients[2], gradients[3], gradients[4], gradients[5], gradients[6], gradients[7], gradients[8])
```

```python
import functools

import jax
import jax.numpy as jnp
from jax import lax
from jax.experimental import pallas as pl
from jax.experimental.pallas import tpu as pltpu
from jax.sharding import PartitionSpec as P

F32=jnp.float32; BF=jnp.bfloat16
NEG=-1e30
def nt(a,b):
    return lax.dot_general(a,b,(((1,),(1,)),((),())),preferred_element_type=F32)
def nn(a,b):
    return lax.dot_general(a,b,(((1,),(0,)),((),())),preferred_element_type=F32)
def tn(a,b):
    return lax.dot_general(a,b,(((0,),(0,)),((),())),preferred_element_type=F32)
def split2(x):
    hi=x.astype(BF)
    lo=(x-hi.astype(F32)).astype(BF)
    return hi,lo

def attn_fwd_kernel(BQ,G,NW,HP,unroll, nblk_ref, qkv_ref, segc_ref, segr_ref, nst_ref, o_ref, lse_ref, bias_ref, sig_ref, cs_ref):
    i=pl.program_id(0)
    D=HP*128
    @pl.when(i==0)
    def _():
        cs_ref[...]=jnp.zeros_like(cs_ref)
    row0=pl.multiple_of(i*BQ,BQ)
    nb=nblk_ref[i]
    lane=lax.broadcasted_iota(jnp.int32,(BQ,128),1)
    left=lane<64
    def variant(n):
        W=n*G
        k0=pl.multiple_of(row0+BQ-W,G)
        kw=pl.ds(k0,W)
        segq=segc_ref[pl.ds(row0,BQ),:]
        segk=segr_ref[:,kw]
        same=segq==segk
        qi=lax.broadcasted_iota(jnp.int32,(BQ,W),0)+(W-BQ)
        ki=lax.broadcasted_iota(jnp.int32,(BQ,W),1)
        allowed=same&(ki<=qi)
        chosen=same&(ki<qi)&(nst_ref[:,kw]>0)
        def qpair(p):
            return qkv_ref[pl.ds(row0,BQ),pl.ds(p,128)]*jnp.asarray(0.125,BF)
        q=qpair(0)
        k=qkv_ref[kw,pl.ds(D,128)]
        s0=nt(jnp.where(left,q,jnp.zeros_like(q)),k)
        e=jnp.exp(-jnp.abs(s0))
        sp=jnp.maximum(s0,0.0)+jnp.log1p(e)
        sg=jnp.where(s0>=0,1.0,e)/(1.0+e)
        sel=jnp.where(chosen,sp,0.0)
        sig_ref[0,:,:W]=jnp.where(chosen,sg,0.0).astype(BF)
        hi,lo=split2(sel)
        ri=lax.broadcasted_iota(jnp.int32,(BQ,BQ),0); ci=lax.broadcasted_iota(jnp.int32,(BQ,BQ),1)
        L=(ri>ci).astype(BF)
        pen=nn(L,hi)+nn(L,lo)+cs_ref[:,kw]
        cs_ref[:,kw]=cs_ref[:,kw]+jnp.sum(sel,axis=0,keepdims=True)
        bias_ref[0,:,:W]=jnp.where(allowed,-pen,NEG)
        def pair(j,lse_acc):
            off=pl.multiple_of(j*128,128)
            q=qkv_ref[pl.ds(row0,BQ),pl.ds(off,128)]*jnp.asarray(0.125,BF)
            z=jnp.zeros_like(q)
            k=qkv_ref[kw,pl.ds(D+off,128)]
            v=qkv_ref[kw,pl.ds(2*D+off,128)]
            b=bias_ref[0,:,:W]
            outs=[]
            for hh in range(2):
                qm=jnp.where(left,q,z) if hh==0 else jnp.where(left,z,q)
                s=nt(qm,k)+b
                m=jnp.max(s,axis=1,keepdims=True)
                p=jnp.exp(s-m)
                l=jnp.sum(p,axis=1,keepdims=True)
                o=nn(p.astype(BF),v)*(1.0/l)
                lse_acc=jnp.where(lane==2*j+hh,m+jnp.log(l),lse_acc)
                outs.append(o)
            o_ref[:,pl.ds(off,128)]=jnp.where(left,outs[0],outs[1]).astype(BF)
            return lse_acc
        lse_ref[...]=lax.fori_loop(0,HP,pair,jnp.zeros((BQ,128),F32),unroll=unroll)
    for n in range(1,NW+1):
        pl.when(nb==n)(functools.partial(variant,n))

def attn_fwd(qkv,segc,segr,nst,nblk,BQ=128,G=128,unroll=2):
    T,D3=qkv.shape; D=D3//3; HP=D//128
    NW=min(T//G,-(-(511+BQ)//G)) if BQ%G==0 else None
    NB=T//BQ
    whole=lambda shape: pl.BlockSpec(shape,lambda i,*_:(0,0),pipeline_mode=pl.Buffered(1))
    gs=pltpu.PrefetchScalarGridSpec(num_scalar_prefetch=1,grid=(NB,),
      in_specs=[whole((T,D3)),whole((T,1)),whole((1,T)),whole((1,T))],
      out_specs=[pl.BlockSpec((BQ,D),lambda i,*_:(i,0)),pl.BlockSpec((BQ,128),lambda i,*_:(i,0)),
        pl.BlockSpec((1,BQ,NW*G),lambda i,*_:(i,0,0)),pl.BlockSpec((1,BQ,NW*G),lambda i,*_:(i,0,0))],
      scratch_shapes=[pltpu.VMEM((1,T),F32)])
    return pl.pallas_call(functools.partial(attn_fwd_kernel,BQ,G,NW,HP,unroll),grid_spec=gs,
      out_shape=[jax.ShapeDtypeStruct((T,D),BF),jax.ShapeDtypeStruct((T,128),F32),
        jax.ShapeDtypeStruct((NB,BQ,NW*G),F32),jax.ShapeDtypeStruct((NB,BQ,NW*G),BF)],
      compiler_params=pltpu.CompilerParams(vmem_limit_bytes=40<<20),name="attn_fwd")(nblk,qkv,segc,segr,nst)

def attn_bwd_kernel(BQ,G,NW,HP,unroll,NB, nblk_ref, qkv_ref, do_ref, o_ref, lse_ref, bias_ref, sig_ref, out_ref, dk_ref, dv_ref, gp_ref, ls_ref):
    step=pl.program_id(0)
    i=NB-1-step
    D=HP*128
    @pl.when(step==0)
    def _():
        dk_ref[...]=jnp.zeros_like(dk_ref)
        dv_ref[...]=jnp.zeros_like(dv_ref)
        ls_ref[...]=jnp.zeros_like(ls_ref)
    row0=pl.multiple_of(i*BQ,BQ)
    nb=nblk_ref[i]
    lane=lax.broadcasted_iota(jnp.int32,(BQ,128),1)
    left=lane<64
    def variant(n):
        W=n*G
        k0=pl.multiple_of(row0+BQ-W,G)
        kw=pl.ds(k0,W)
        gp_ref[:,:W]=jnp.zeros((BQ,W),F32)
        ones=jnp.ones((W,128),BF)
        lse=lse_ref[...]
        def work(j,first):
            off=pl.multiple_of(j*128,128)
            q=qkv_ref[pl.ds(row0,BQ),pl.ds(off,128)]*jnp.asarray(0.125,BF)
            k=qkv_ref[kw,pl.ds(D+off,128)]
            v=qkv_ref[kw,pl.ds(2*D+off,128)]
            do=do_ref[:,pl.ds(off,128)]
            z=jnp.zeros_like(q)
            b=bias_ref[0,:,:W]
            prod=do.astype(F32)*o_ref[:,pl.ds(off,128)].astype(F32)
            qs=[jnp.where(left,q,z),jnp.where(left,z,q)]
            dos=[jnp.where(left,do,z),jnp.where(left,z,do)]
            ps=[];dss=[]
            for hh in range(2):
                lh=jnp.sum(jnp.where(lane==2*j+hh,lse,0.0),axis=1,keepdims=True)
                delta=jnp.sum(jnp.where(left,prod,0.0) if hh==0 else jnp.where(left,0.0,prod),axis=1,keepdims=True)
                s=nt(qs[hh],k)
                p=jnp.exp(s+b-lh)
                dp=nt(dos[hh],v)
                ps.append(p); dss.append(p*(dp-delta))
            if not first:
                gp_ref[:,:W]=gp_ref[:,:W]+(dss[0]+dss[1])
            else:
                gp=gp_ref[:,:W]+(dss[0]+dss[1])
                hi,lo=split2(gp)
                ri=lax.broadcasted_iota(jnp.int32,(BQ,BQ),0); ci=lax.broadcasted_iota(jnp.int32,(BQ,BQ),1)
                U=(ci>ri).astype(BF)
                gsel=nn(U,hi)+nn(U,lo)+ls_ref[:,kw]
                ls_ref[:,kw]=ls_ref[:,kw]+jnp.sum(gp,axis=0,keepdims=True)
                dss[0]=dss[0]-gsel*sig_ref[0,:,:W].astype(F32)
            dsb=[x.astype(BF) for x in dss]
            pb=[x.astype(BF) for x in ps]
            dq=jnp.where(left,nn(dsb[0],k),nn(dsb[1],k))*0.125
            out_ref[pl.ds(row0,BQ),pl.ds(off,128)]=dq.astype(BF)
            dk_ref[kw,pl.ds(off,128)]+=tn(dsb[0],qs[0])+tn(dsb[1],qs[1])
            dv_ref[kw,pl.ds(off,128)]+=tn(pb[0],dos[0])+tn(pb[1],dos[1])
        def body(j,c):
            work(j,False)
            return c
        lax.fori_loop(1,HP,body,0,unroll=unroll)
        work(0,True)
    for n in range(1,NW+1):
        pl.when(nb==n)(functools.partial(variant,n))
    @pl.when(step==NB-1)
    def _():
        out_ref[:,D:2*D]=dk_ref[...].astype(BF)
        out_ref[:,2*D:]=dv_ref[...].astype(BF)

def attn_bwd(qkv,do,o,lse,bias,sig,nblk,BQ=128,G=128,unroll=1):
    T,D3=qkv.shape; D=D3//3; HP=D//128
    NW=bias.shape[2]//G
    NB=T//BQ
    whole=lambda shape: pl.BlockSpec(shape,lambda i,*_:(0,0),pipeline_mode=pl.Buffered(1))
    rb=lambda w: pl.BlockSpec((BQ,w),lambda i,*_:(NB-1-i,0))
    r3=pl.BlockSpec((1,BQ,NW*G),lambda i,*_:(NB-1-i,0,0))
    gs=pltpu.PrefetchScalarGridSpec(num_scalar_prefetch=1,grid=(NB,),
      in_specs=[whole((T,D3)),rb(D),rb(D),rb(128),r3,r3],
      out_specs=whole((T,D3)),
      scratch_shapes=[pltpu.VMEM((T,D),F32),pltpu.VMEM((T,D),F32),pltpu.VMEM((BQ,NW*G),F32),pltpu.VMEM((1,T),F32)])
    return pl.pallas_call(functools.partial(attn_bwd_kernel,BQ,G,NW,HP,unroll,NB),grid_spec=gs,
      out_shape=jax.ShapeDtypeStruct((T,D3),BF),
      compiler_params=pltpu.CompilerParams(vmem_limit_bytes=50<<20),name="attn_bwd")(nblk,qkv,do,o,lse,bias,sig)

def prep(seg,BQ=128,G=128):
    T=seg.shape[0]
    NB=T//BQ
    at=seg[::BQ]
    first=jnp.sum((seg[None,:]<at[:,None]).astype(jnp.int32),axis=1)
    ends=(jnp.arange(NB,dtype=jnp.int32)+1)*BQ
    nblk=(ends-(first//G)*G)//G
    starts=jnp.concatenate([jnp.ones((1,),bool),seg[1:]!=seg[:-1]])
    nst=jnp.logical_not(starts).astype(jnp.int32)[None,:]
    return seg[:,None],seg[None,:],nst,nblk

EPS=1e-5
GC=0.7978845608028654; GA=0.044715
def rowmean(x): return jnp.mean(x,axis=-1,keepdims=True)
def ln_unit(x):
    m=rowmean(x); c=x-m; v=rowmean(c*c); r=lax.rsqrt(v+EPS)
    return c*r, r

def qkv_kernel(tok_ref,w_ref,vec_ref,n_ref,o_ref):
    u,_=ln_unit(tok_ref[...].astype(F32))
    n=(u*vec_ref[0:1,:]+vec_ref[1:2,:]).astype(BF)
    n_ref[...]=n
    o_ref[...]=nt(n,w_ref[...]).astype(BF)
def qkv_proj(tok,wT,vec,R=256):
    T,D=tok.shape; E=wT.shape[0]
    c=lambda s: pl.BlockSpec(s,lambda i:(0,0),pipeline_mode=pl.Buffered(1))
    return pl.pallas_call(qkv_kernel,grid=(T//R,),in_specs=[pl.BlockSpec((R,D),lambda i:(i,0)),c((E,D)),c(vec.shape)],
      out_specs=[pl.BlockSpec((R,D),lambda i:(i,0)),pl.BlockSpec((R,E),lambda i:(i,0))],
      out_shape=[jax.ShapeDtypeStruct((T,D),BF),jax.ShapeDtypeStruct((T,E),BF)],
      compiler_params=pltpu.CompilerParams(vmem_limit_bytes=40<<20),name="qkv_proj")(tok,wT,vec)

def mlp_kernel(NR,NC,C,R,tok_ref,att_ref,cot_ref,ow_ref,up_ref,dn_ref,vec_ref,
    out_ref,gres_ref,gatt_ref,gdn_ref,gup_ref,gow_ref,vg_ref, act_s,gh_s,n2_s,gb_s):
    i=pl.program_id(0)
    @pl.when(i<NR)
    def _():
        rows=pl.ds(pl.multiple_of(i*R,R),R)
        gain=vec_ref[2:3,:]; shift=vec_ref[3:4,:]
        res=tok_ref[rows,:].astype(F32)+nn(att_ref[rows,:],ow_ref[...])
        u,rstd=ln_unit(res)
        n2=(u*gain+shift).astype(BF)
        n2_s[rows,:]=n2
        cot=cot_ref[rows,:]
        out_acc=res
        g_acc=jnp.zeros_like(res)
        for c in range(NC):
            cs=slice(c*C,(c+1)*C)
            h=nt(n2,up_ref[cs,:])
            h2=h*h
            t=jnp.tanh(h*(GC+GC*GA*h2))
            half=0.5*(1.0+t)
            act=(h*half).astype(BF)
            act_s[rows,cs]=act
            ga=nt(cot,dn_ref[cs,:])
            dg=half+(0.5*h)*(1.0-t*t)*(GC+3.0*GC*GA*h2)
            gh=(ga*dg).astype(BF)
            gh_s[rows,cs]=gh
            out_acc=out_acc+nn(act,dn_ref[cs,:])
            g_acc=g_acc+nn(gh,up_ref[cs,:])
        out_ref[...]=out_acc.astype(BF)
        vgain=jnp.sum(g_acc*u,axis=0,keepdims=True); vshift=jnp.sum(g_acc,axis=0,keepdims=True)
        @pl.when(i==0)
        def _():
            vg_ref[...]=jnp.zeros_like(vg_ref)
        vg_ref[0:1,:]+=vgain
        vg_ref[1:2,:]+=vshift
        g=g_acc*gain
        gr=cot.astype(F32)+rstd*(g-rowmean(g)-u*rowmean(g*u))
        gres_ref[...]=gr
        gb=gr.astype(BF)
        gb_s[rows,:]=gb
        gatt_ref[...]=nt(gb,ow_ref[...]).astype(BF)
    @pl.when(i>=NR)
    def _():
        j=i-NR
        cs=pl.ds(pl.multiple_of(j*C2(gdn_ref),C2(gdn_ref)),C2(gdn_ref))
        gdn_ref[...]=tn(act_s[:,cs],cot_ref[...]).astype(BF)
        gup_ref[...]=tn(gh_s[:,cs],n2_s[...]).astype(BF)
    @pl.when(i==NR)
    def _():
        gow_ref[...]=tn(att_ref[...],gb_s[...]).astype(BF)
def C2(ref): return ref.shape[0]
def mlp(tok,att,cot,ow,upT,dn,vec,R=256,C=768,WC=384):
    T,D=tok.shape; F=upT.shape[0]; NR=T//R; NW=F//WC
    c=lambda s: pl.BlockSpec(s,lambda i:(0,0),pipeline_mode=pl.Buffered(1))
    rb=lambda w: pl.BlockSpec((R,w),lambda i:(jnp.minimum(i,NR-1),0))
    wb=pl.BlockSpec((WC,D),lambda i:(jnp.maximum(i-NR,0),0))
    return pl.pallas_call(functools.partial(mlp_kernel,NR,F//C,C,R),grid=(NR+NW,),
      in_specs=[c((T,D)),c((T,D)),c((T,D)),c((D,D)),c((F,D)),c((F,D)),c(vec.shape)],
      out_specs=[rb(D),rb(D),rb(D),wb,wb,c((D,D)),c((8,D))],
      out_shape=[jax.ShapeDtypeStruct((T,D),BF),jax.ShapeDtypeStruct((T,D),F32),jax.ShapeDtypeStruct((T,D),BF),
        jax.ShapeDtypeStruct((F,D),BF),jax.ShapeDtypeStruct((F,D),BF),jax.ShapeDtypeStruct((D,D),BF),jax.ShapeDtypeStruct((8,D),F32)],
      scratch_shapes=[pltpu.VMEM((T,F),BF),pltpu.VMEM((T,F),BF),pltpu.VMEM((T,D),BF),pltpu.VMEM((T,D),BF)],
      compiler_params=pltpu.CompilerParams(vmem_limit_bytes=58<<20),name="mlp")(tok,att,cot,ow,upT,dn,vec)

def wg_kernel(gp_ref,n_ref,o_ref):
    o_ref[...]=tn(gp_ref[...],n_ref[...]).astype(BF)
def qkv_wgrad(gp,n1,WC=384):
    T,E=gp.shape; D=n1.shape[1]
    return pl.pallas_call(wg_kernel,grid=(E//WC,),in_specs=[pl.BlockSpec((T,WC),lambda i:(0,i)),pl.BlockSpec((T,D),lambda i:(0,0),pipeline_mode=pl.Buffered(1))],
      out_specs=pl.BlockSpec((WC,D),lambda i:(i,0)),out_shape=jax.ShapeDtypeStruct((E,D),BF),
      compiler_params=pltpu.CompilerParams(vmem_limit_bytes=40<<20),name="qkv_wgrad")(gp,n1)
def dg_kernel(gp_ref,w_ref,tok_ref,gres_ref,vec_ref,o_ref,vg_ref):
    i=pl.program_id(0)
    gn=nn(gp_ref[...],w_ref[...])
    u,rstd=ln_unit(tok_ref[...].astype(F32))
    @pl.when(i==0)
    def _():
        vg_ref[...]=jnp.zeros_like(vg_ref)
    vg_ref[0:1,:]+=jnp.sum(gn*u,axis=0,keepdims=True)
    vg_ref[1:2,:]+=jnp.sum(gn,axis=0,keepdims=True)
    g=gn*vec_ref[0:1,:]
    o_ref[...]=(gres_ref[...]+rstd*(g-rowmean(g)-u*rowmean(g*u))).astype(BF)
def qkv_dgrad(gp,wT,tok,gres,vec,R=256):
    T,E=gp.shape; D=tok.shape[1]
    c=lambda s: pl.BlockSpec(s,lambda i:(0,0),pipeline_mode=pl.Buffered(1))
    rb=lambda w: pl.BlockSpec((R,w),lambda i:(i,0))
    return pl.pallas_call(dg_kernel,grid=(T//R,),in_specs=[rb(E),c((E,D)),rb(D),rb(D),c(vec.shape)],out_specs=[rb(D),c((8,D))],
      out_shape=[jax.ShapeDtypeStruct((T,D),BF),jax.ShapeDtypeStruct((8,D),F32)],
      compiler_params=pltpu.CompilerParams(vmem_limit_bytes=40<<20),name="qkv_dgrad")(gp,wT,tok,gres,vec)


def gather(x):
    return lax.all_gather(x, "shard", axis=0, tiled=True)


def reduce_shard(g):
    part = lax.psum_scatter(g, "shard", scatter_dimension=0, tiled=True)
    return lax.psum(part, "rep").astype(F32)


def local(tokens, segment_ids, qkv_weight, out_weight, up_weight, down_weight,
          norm1_gain, norm1_shift, norm2_gain, norm2_shift, cotangent):
    tok = tokens[0]
    cot = cotangent[0]
    seg = segment_ids[0]
    model = tok.shape[1]
    shards = lax.axis_size("shard")
    width = qkv_weight.shape[1]
    vec_part = jnp.stack([norm1_gain, norm1_shift, norm2_gain, norm2_shift])
    vec_rows = jnp.zeros((8, model), BF).at[:4, : vec_part.shape[1]].set(vec_part)
    first = gather(jnp.concatenate([qkv_weight.T, vec_rows], axis=0)).reshape(shards, width + 8, model)
    qkv_t = first[:, :width].reshape(shards * width, model)
    vec = first[:, width:, : vec_part.shape[1]].transpose(1, 0, 2).reshape(8, model).astype(F32)
    out_full = gather(out_weight)
    up_t = gather(up_weight.T)
    down_full = gather(down_weight)
    segc, segr, nst, nblk = prep(seg)
    normed, projected = qkv_proj(tok, qkv_t, vec)
    attended, lse, bias, sig = attn_fwd(projected, segc, segr, nst, nblk, unroll=6)
    output, gres, gatt, gdn, gup, gow, vec2 = mlp(tok, attended, cot, out_full, up_t, down_full, vec)
    gproj = attn_bwd(projected, gatt, attended, lse, bias, sig, nblk, unroll=5)
    gqkv = qkv_wgrad(gproj, normed)
    tgrad, vec1 = qkv_dgrad(gproj, qkv_t, tok, gres, vec)
    down_grad = reduce_shard(gdn)
    up_grad = reduce_shard(gup).T
    out_grad = reduce_shard(gow)
    qkv_grad = reduce_shard(gqkv).T
    vec_all = lax.psum(jnp.concatenate([vec1[:2], vec2[:2]], axis=0), ("rep", "shard"))
    piece = norm1_gain.shape[0]
    mine = lax.dynamic_slice_in_dim(vec_all, lax.axis_index("shard") * piece, piece, 1)
    return (output[None], tgrad[None], qkv_grad, out_grad, up_grad, down_grad,
            mine[0], mine[1], mine[2], mine[3])


def solution(mesh):
    seq = P(("rep", "shard"), None, None)
    cols, rows, vecs = P(None, "shard"), P("shard", None), P("shard")
    return jax.shard_map(
        local,
        mesh=mesh,
        in_specs=(seq, P(("rep", "shard"), None), cols, rows, cols, rows, vecs, vecs, vecs, vecs, seq),
        out_specs=(seq, seq, cols, rows, cols, rows, vecs, vecs, vecs, vecs),
        check_vma=False,
    )
```

```python
import functools

import jax
import jax.numpy as jnp
from jax import lax
from jax.experimental import pallas as pl
from jax.experimental.pallas import tpu as pltpu
from jax.sharding import PartitionSpec as P

F32 = jnp.float32
BF = jnp.bfloat16
NEG=-1e30
def nt(a,b):
    return lax.dot_general(a,b,(((1,),(1,)),((),())),preferred_element_type=F32)
def nn(a,b):
    return lax.dot_general(a,b,(((1,),(0,)),((),())),preferred_element_type=F32)
def tn(a,b):
    return lax.dot_general(a,b,(((0,),(0,)),((),())),preferred_element_type=F32)
def split2(x):
    hi=x.astype(BF)
    lo=(x-hi.astype(F32)).astype(BF)
    return hi,lo

def attn_fwd_kernel(BQ,G,NW,HP,unroll, nblk_ref, qkv_ref, segc_ref, segr_ref, nst_ref, o_ref, lse_ref, bias_ref, sig_ref, cs_ref):
    i=pl.program_id(0)
    D=HP*128
    @pl.when(i==0)
    def _():
        cs_ref[...]=jnp.zeros_like(cs_ref)
    row0=pl.multiple_of(i*BQ,BQ)
    nb=nblk_ref[i]
    lane=lax.broadcasted_iota(jnp.int32,(BQ,128),1)
    left=lane<64
    def variant(n):
        W=n*G
        k0=pl.multiple_of(row0+BQ-W,G)
        kw=pl.ds(k0,W)
        segq=segc_ref[pl.ds(row0,BQ),:]
        segk=segr_ref[:,kw]
        same=segq==segk
        qi=lax.broadcasted_iota(jnp.int32,(BQ,W),0)+(W-BQ)
        ki=lax.broadcasted_iota(jnp.int32,(BQ,W),1)
        allowed=same&(ki<=qi)
        chosen=same&(ki<qi)&(nst_ref[:,kw]>0)
        def qpair(p):
            return qkv_ref[pl.ds(row0,BQ),pl.ds(p,128)]*jnp.asarray(0.125,BF)
        q=qpair(0)
        k=qkv_ref[kw,pl.ds(D,128)]
        s0=nt(jnp.where(left,q,jnp.zeros_like(q)),k)
        e=jnp.exp(-jnp.abs(s0))
        sp=jnp.maximum(s0,0.0)+jnp.log1p(e)
        sg=jnp.where(s0>=0,1.0,e)/(1.0+e)
        sel=jnp.where(chosen,sp,0.0)
        sig_ref[0,:,:W]=jnp.where(chosen,sg,0.0).astype(BF)
        hi,lo=split2(sel)
        ri=lax.broadcasted_iota(jnp.int32,(BQ,BQ),0); ci=lax.broadcasted_iota(jnp.int32,(BQ,BQ),1)
        L=(ri>ci).astype(BF)
        pen=nn(L,hi)+nn(L,lo)+cs_ref[:,kw]
        cs_ref[:,kw]=cs_ref[:,kw]+jnp.sum(sel,axis=0,keepdims=True)
        bias_ref[0,:,:W]=jnp.where(allowed,-pen,NEG)
        def pair(j,lse_acc):
            off=pl.multiple_of(j*128,128)
            q=qkv_ref[pl.ds(row0,BQ),pl.ds(off,128)]*jnp.asarray(0.125,BF)
            z=jnp.zeros_like(q)
            k=qkv_ref[kw,pl.ds(D+off,128)]
            v=qkv_ref[kw,pl.ds(2*D+off,128)]
            b=bias_ref[0,:,:W]
            outs=[]
            for hh in range(2):
                qm=jnp.where(left,q,z) if hh==0 else jnp.where(left,z,q)
                s=nt(qm,k)+b
                m=jnp.max(s,axis=1,keepdims=True)
                p=jnp.exp(s-m)
                l=jnp.sum(p,axis=1,keepdims=True)
                o=nn(p.astype(BF),v)*(1.0/l)
                lse_acc=jnp.where(lane==2*j+hh,m+jnp.log(l),lse_acc)
                outs.append(o)
            o_ref[:,pl.ds(off,128)]=jnp.where(left,outs[0],outs[1]).astype(BF)
            return lse_acc
        lse_ref[...]=lax.fori_loop(0,HP,pair,jnp.zeros((BQ,128),F32),unroll=unroll)
    for n in range(1,NW+1):
        pl.when(nb==n)(functools.partial(variant,n))

def attn_fwd(qkv,segc,segr,nst,nblk,BQ=128,G=128,unroll=2):
    T,D3=qkv.shape; D=D3//3; HP=D//128
    NW=min(T//G,-(-(511+BQ)//G)) if BQ%G==0 else None
    NB=T//BQ
    whole=lambda shape: pl.BlockSpec(shape,lambda i,*_:(0,0),pipeline_mode=pl.Buffered(1))
    gs=pltpu.PrefetchScalarGridSpec(num_scalar_prefetch=1,grid=(NB,),
      in_specs=[whole((T,D3)),whole((T,1)),whole((1,T)),whole((1,T))],
      out_specs=[pl.BlockSpec((BQ,D),lambda i,*_:(i,0)),pl.BlockSpec((BQ,128),lambda i,*_:(i,0)),
        pl.BlockSpec((1,BQ,NW*G),lambda i,*_:(i,0,0)),pl.BlockSpec((1,BQ,NW*G),lambda i,*_:(i,0,0))],
      scratch_shapes=[pltpu.VMEM((1,T),F32)])
    return pl.pallas_call(functools.partial(attn_fwd_kernel,BQ,G,NW,HP,unroll),grid_spec=gs,
      out_shape=[jax.ShapeDtypeStruct((T,D),BF),jax.ShapeDtypeStruct((T,128),F32),
        jax.ShapeDtypeStruct((NB,BQ,NW*G),F32),jax.ShapeDtypeStruct((NB,BQ,NW*G),BF)],
      compiler_params=pltpu.CompilerParams(vmem_limit_bytes=40<<20),name="attn_fwd")(nblk,qkv,segc,segr,nst)

def attn_bwd_kernel(BQ,G,NW,HP,unroll,NB, nblk_ref, qkv_ref, do_ref, o_ref, lse_ref, bias_ref, sig_ref, out_ref, dk_ref, dv_ref, gp_ref, ls_ref):
    step=pl.program_id(0)
    i=NB-1-step
    D=HP*128
    @pl.when(step==0)
    def _():
        dk_ref[...]=jnp.zeros_like(dk_ref)
        dv_ref[...]=jnp.zeros_like(dv_ref)
        ls_ref[...]=jnp.zeros_like(ls_ref)
    row0=pl.multiple_of(i*BQ,BQ)
    nb=nblk_ref[i]
    lane=lax.broadcasted_iota(jnp.int32,(BQ,128),1)
    left=lane<64
    def variant(n):
        W=n*G
        k0=pl.multiple_of(row0+BQ-W,G)
        kw=pl.ds(k0,W)
        gp_ref[:,:W]=jnp.zeros((BQ,W),F32)
        ones=jnp.ones((W,128),BF)
        lse=lse_ref[...]
        def work(j,first):
            off=pl.multiple_of(j*128,128)
            q=qkv_ref[pl.ds(row0,BQ),pl.ds(off,128)]*jnp.asarray(0.125,BF)
            k=qkv_ref[kw,pl.ds(D+off,128)]
            v=qkv_ref[kw,pl.ds(2*D+off,128)]
            do=do_ref[:,pl.ds(off,128)]
            z=jnp.zeros_like(q)
            b=bias_ref[0,:,:W]
            prod=do.astype(F32)*o_ref[:,pl.ds(off,128)].astype(F32)
            qs=[jnp.where(left,q,z),jnp.where(left,z,q)]
            dos=[jnp.where(left,do,z),jnp.where(left,z,do)]
            ps=[];dss=[]
            for hh in range(2):
                lh=jnp.sum(jnp.where(lane==2*j+hh,lse,0.0),axis=1,keepdims=True)
                delta=jnp.sum(jnp.where(left,prod,0.0) if hh==0 else jnp.where(left,0.0,prod),axis=1,keepdims=True)
                s=nt(qs[hh],k)
                p=jnp.exp(s+b-lh)
                dp=nt(dos[hh],v)
                ps.append(p); dss.append(p*(dp-delta))
            if not first:
                gp_ref[:,:W]=gp_ref[:,:W]+(dss[0]+dss[1])
            else:
                gp=gp_ref[:,:W]+(dss[0]+dss[1])
                hi,lo=split2(gp)
                ri=lax.broadcasted_iota(jnp.int32,(BQ,BQ),0); ci=lax.broadcasted_iota(jnp.int32,(BQ,BQ),1)
                U=(ci>ri).astype(BF)
                gsel=nn(U,hi)+nn(U,lo)+ls_ref[:,kw]
                ls_ref[:,kw]=ls_ref[:,kw]+jnp.sum(gp,axis=0,keepdims=True)
                dss[0]=dss[0]-gsel*sig_ref[0,:,:W].astype(F32)
            dsb=[x.astype(BF) for x in dss]
            pb=[x.astype(BF) for x in ps]
            dq=jnp.where(left,nn(dsb[0],k),nn(dsb[1],k))*0.125
            out_ref[pl.ds(row0,BQ),pl.ds(off,128)]=dq.astype(BF)
            dk_ref[kw,pl.ds(off,128)]+=tn(dsb[0],qs[0])+tn(dsb[1],qs[1])
            dv_ref[kw,pl.ds(off,128)]+=tn(pb[0],dos[0])+tn(pb[1],dos[1])
        def body(j,c):
            work(j,False)
            return c
        lax.fori_loop(1,HP,body,0,unroll=unroll)
        work(0,True)
    for n in range(1,NW+1):
        pl.when(nb==n)(functools.partial(variant,n))
    @pl.when(step==NB-1)
    def _():
        out_ref[:,D:2*D]=dk_ref[...].astype(BF)
        out_ref[:,2*D:]=dv_ref[...].astype(BF)

def attn_bwd(qkv,do,o,lse,bias,sig,nblk,BQ=128,G=128,unroll=1):
    T,D3=qkv.shape; D=D3//3; HP=D//128
    NW=bias.shape[2]//G
    NB=T//BQ
    whole=lambda shape: pl.BlockSpec(shape,lambda i,*_:(0,0),pipeline_mode=pl.Buffered(1))
    rb=lambda w: pl.BlockSpec((BQ,w),lambda i,*_:(NB-1-i,0))
    r3=pl.BlockSpec((1,BQ,NW*G),lambda i,*_:(NB-1-i,0,0))
    gs=pltpu.PrefetchScalarGridSpec(num_scalar_prefetch=1,grid=(NB,),
      in_specs=[whole((T,D3)),rb(D),rb(D),rb(128),r3,r3],
      out_specs=whole((T,D3)),
      scratch_shapes=[pltpu.VMEM((T,D),F32),pltpu.VMEM((T,D),F32),pltpu.VMEM((BQ,NW*G),F32),pltpu.VMEM((1,T),F32)])
    return pl.pallas_call(functools.partial(attn_bwd_kernel,BQ,G,NW,HP,unroll,NB),grid_spec=gs,
      out_shape=jax.ShapeDtypeStruct((T,D3),BF),
      compiler_params=pltpu.CompilerParams(vmem_limit_bytes=50<<20),name="attn_bwd")(nblk,qkv,do,o,lse,bias,sig)

def prep(seg,BQ=128,G=128):
    T=seg.shape[0]
    NB=T//BQ
    at=seg[::BQ]
    first=jnp.sum((seg[None,:]<at[:,None]).astype(jnp.int32),axis=1)
    ends=(jnp.arange(NB,dtype=jnp.int32)+1)*BQ
    nblk=(ends-(first//G)*G)//G
    starts=jnp.concatenate([jnp.ones((1,),bool),seg[1:]!=seg[:-1]])
    nst=jnp.logical_not(starts).astype(jnp.int32)[None,:]
    return seg[:,None],seg[None,:],nst,nblk

EPS=1e-5
GC=0.7978845608028654; GA=0.044715
def rowmean(x): return jnp.mean(x,axis=-1,keepdims=True)
def ln_unit(x):
    m=rowmean(x); c=x-m; v=rowmean(c*c); r=lax.rsqrt(v+EPS)
    return c*r, r

def qkv_kernel(tok_ref,w_ref,vec_ref,n_ref,o_ref):
    u,_=ln_unit(tok_ref[...].astype(F32))
    n=(u*vec_ref[0:1,:]+vec_ref[1:2,:]).astype(BF)
    n_ref[...]=n
    o_ref[...]=nt(n,w_ref[...]).astype(BF)
def qkv_proj(tok,wT,vec,R=256):
    T,D=tok.shape; E=wT.shape[0]
    c=lambda s: pl.BlockSpec(s,lambda i:(0,0),pipeline_mode=pl.Buffered(1))
    return pl.pallas_call(qkv_kernel,grid=(T//R,),in_specs=[pl.BlockSpec((R,D),lambda i:(i,0)),c((E,D)),c(vec.shape)],
      out_specs=[pl.BlockSpec((R,D),lambda i:(i,0)),pl.BlockSpec((R,E),lambda i:(i,0))],
      out_shape=[jax.ShapeDtypeStruct((T,D),BF),jax.ShapeDtypeStruct((T,E),BF)],
      compiler_params=pltpu.CompilerParams(vmem_limit_bytes=40<<20),name="qkv_proj")(tok,wT,vec)

def mlp_kernel(NR,NC,C,R,tok_ref,att_ref,cot_ref,ow_ref,up_ref,dn_ref,vec_ref,
    out_ref,gres_ref,gatt_ref,gdn_ref,gup_ref,gow_ref,vg_ref, act_s,gh_s,n2_s,gb_s):
    i=pl.program_id(0)
    @pl.when(i<NR)
    def _():
        rows=pl.ds(pl.multiple_of(i*R,R),R)
        gain=vec_ref[2:3,:]; shift=vec_ref[3:4,:]
        res=tok_ref[rows,:].astype(F32)+nn(att_ref[rows,:],ow_ref[...])
        u,rstd=ln_unit(res)
        n2=(u*gain+shift).astype(BF)
        n2_s[rows,:]=n2
        cot=cot_ref[rows,:]
        out_acc=res
        g_acc=jnp.zeros_like(res)
        for c in range(NC):
            cs=slice(c*C,(c+1)*C)
            h=nt(n2,up_ref[cs,:])
            h2=h*h
            t=jnp.tanh(h*(GC+GC*GA*h2))
            half=0.5*(1.0+t)
            act=(h*half).astype(BF)
            act_s[rows,cs]=act
            ga=nt(cot,dn_ref[cs,:])
            dg=half+(0.5*h)*(1.0-t*t)*(GC+3.0*GC*GA*h2)
            gh=(ga*dg).astype(BF)
            gh_s[rows,cs]=gh
            out_acc=out_acc+nn(act,dn_ref[cs,:])
            g_acc=g_acc+nn(gh,up_ref[cs,:])
        out_ref[...]=out_acc.astype(BF)
        vgain=jnp.sum(g_acc*u,axis=0,keepdims=True); vshift=jnp.sum(g_acc,axis=0,keepdims=True)
        @pl.when(i==0)
        def _():
            vg_ref[...]=jnp.zeros_like(vg_ref)
        vg_ref[0:1,:]+=vgain
        vg_ref[1:2,:]+=vshift
        g=g_acc*gain
        gr=cot.astype(F32)+rstd*(g-rowmean(g)-u*rowmean(g*u))
        gres_ref[...]=gr
        gb=gr.astype(BF)
        gb_s[rows,:]=gb
        gatt_ref[...]=nt(gb,ow_ref[...]).astype(BF)
    @pl.when(i>=NR)
    def _():
        j=i-NR
        cs=pl.ds(pl.multiple_of(j*C2(gdn_ref),C2(gdn_ref)),C2(gdn_ref))
        gdn_ref[...]=tn(act_s[:,cs],cot_ref[...]).astype(BF)
        gup_ref[...]=tn(gh_s[:,cs],n2_s[...]).astype(BF)
    @pl.when(i==NR)
    def _():
        gow_ref[...]=tn(att_ref[...],gb_s[...]).astype(BF)
def C2(ref): return ref.shape[0]
def mlp(tok,att,cot,ow,upT,dn,vec,R=256,C=768,WC=384):
    T,D=tok.shape; F=upT.shape[0]; NR=T//R; NW=F//WC
    c=lambda s: pl.BlockSpec(s,lambda i:(0,0),pipeline_mode=pl.Buffered(1))
    rb=lambda w: pl.BlockSpec((R,w),lambda i:(jnp.minimum(i,NR-1),0))
    wb=pl.BlockSpec((WC,D),lambda i:(jnp.maximum(i-NR,0),0))
    return pl.pallas_call(functools.partial(mlp_kernel,NR,F//C,C,R),grid=(NR+NW,),
      in_specs=[c((T,D)),c((T,D)),c((T,D)),c((D,D)),c((F,D)),c((F,D)),c(vec.shape)],
      out_specs=[rb(D),rb(D),rb(D),wb,wb,c((D,D)),c((8,D))],
      out_shape=[jax.ShapeDtypeStruct((T,D),BF),jax.ShapeDtypeStruct((T,D),F32),jax.ShapeDtypeStruct((T,D),BF),
        jax.ShapeDtypeStruct((F,D),BF),jax.ShapeDtypeStruct((F,D),BF),jax.ShapeDtypeStruct((D,D),BF),jax.ShapeDtypeStruct((8,D),F32)],
      scratch_shapes=[pltpu.VMEM((T,F),BF),pltpu.VMEM((T,F),BF),pltpu.VMEM((T,D),BF),pltpu.VMEM((T,D),BF)],
      compiler_params=pltpu.CompilerParams(vmem_limit_bytes=58<<20),name="mlp")(tok,att,cot,ow,upT,dn,vec)

def wg_kernel(gp_ref,n_ref,o_ref):
    o_ref[...]=tn(gp_ref[...],n_ref[...]).astype(BF)
def qkv_wgrad(gp,n1,WC=384):
    T,E=gp.shape; D=n1.shape[1]
    return pl.pallas_call(wg_kernel,grid=(E//WC,),in_specs=[pl.BlockSpec((T,WC),lambda i:(0,i)),pl.BlockSpec((T,D),lambda i:(0,0),pipeline_mode=pl.Buffered(1))],
      out_specs=pl.BlockSpec((WC,D),lambda i:(i,0)),out_shape=jax.ShapeDtypeStruct((E,D),BF),
      compiler_params=pltpu.CompilerParams(vmem_limit_bytes=40<<20),name="qkv_wgrad")(gp,n1)
def dg_kernel(gp_ref,w_ref,tok_ref,gres_ref,vec_ref,o_ref,vg_ref):
    i=pl.program_id(0)
    gn=nn(gp_ref[...],w_ref[...])
    u,rstd=ln_unit(tok_ref[...].astype(F32))
    @pl.when(i==0)
    def _():
        vg_ref[...]=jnp.zeros_like(vg_ref)
    vg_ref[0:1,:]+=jnp.sum(gn*u,axis=0,keepdims=True)
    vg_ref[1:2,:]+=jnp.sum(gn,axis=0,keepdims=True)
    g=gn*vec_ref[0:1,:]
    o_ref[...]=(gres_ref[...]+rstd*(g-rowmean(g)-u*rowmean(g*u))).astype(BF)
def qkv_dgrad(gp,wT,tok,gres,vec,R=256):
    T,E=gp.shape; D=tok.shape[1]
    c=lambda s: pl.BlockSpec(s,lambda i:(0,0),pipeline_mode=pl.Buffered(1))
    rb=lambda w: pl.BlockSpec((R,w),lambda i:(i,0))
    return pl.pallas_call(dg_kernel,grid=(T//R,),in_specs=[rb(E),c((E,D)),rb(D),rb(D),c(vec.shape)],out_specs=[rb(D),c((8,D))],
      out_shape=[jax.ShapeDtypeStruct((T,D),BF),jax.ShapeDtypeStruct((8,D),F32)],
      compiler_params=pltpu.CompilerParams(vmem_limit_bytes=40<<20),name="qkv_dgrad")(gp,wT,tok,gres,vec)

MESH=pl.DeviceIdType.MESH

def place():
    r=lax.axis_index("rep"); s=lax.axis_index("shard")
    y=r//2; x=r%2; z=s//2; c=s%2
    return dict(r=r,s=s,y=y,x=x,z=z,c=c,rx=y*2+(1-x),ry=(1-y)*2+x,rd=(1-y)*2+(1-x),mate=z*2+(1-c))
def zpeer(p,dz):
    return (p["z"]+dz)%4
def greet(p):
    bar=pltpu.get_barrier_semaphore()
    for dev in ((p["r"],p["mate"]),(p["rx"],p["s"]),(p["ry"],p["s"]))+tuple((p["r"],zpeer(p,dz)*2+p["c"]) for dz in (1,2,3)):
        pl.semaphore_signal(bar,inc=1,device_id=dev,device_id_type=MESH)
    pl.semaphore_wait(bar,6)
def rcopy(src,dst,ss,rs,dev):
    return pltpu.make_async_remote_copy(src_ref=src,dst_ref=dst,send_sem=ss,recv_sem=rs,device_id=dev,device_id_type=MESH)

def gather_kernel(q_ref,o_ref,u_ref,d_ref,v_ref,qf,of,uf,df,vf,vz,vp,vm,lsem,c0s,c0r,ss,rs,vs,vr):
    p=place()
    greet(p)
    r,s,c,z=p["r"],p["s"],p["c"],p["z"]
    mate=(r,p["mate"]); xm=(p["rx"],s); ym=(p["ry"],s)
    sets=((q_ref,qf),(o_ref,of),(u_ref,uf),(d_ref,df))
    done=[]
    def go(cp):
        cp.start(); done.append(cp); return cp
    locs=[]
    for w,(a,f) in enumerate(sets):
        cp=pltpu.make_async_copy(a,f.at[s],lsem.at[w]); cp.start(); locs.append(cp)
    H=q_ref.shape[1]//2
    vcs=[go(rcopy(v_ref,vz.at[dz-1],vs.at[dz-1],vr.at[dz-1],(r,zpeer(p,dz)*2+c))) for dz in (1,2,3)]
    def zsend(w):
        a,f=sets[w]; Q=a.shape[0]//4
        rows=pl.ds(pl.multiple_of(r*Q,8),Q)
        return [go(rcopy(a.at[rows],f.at[s,rows],ss.at[w,0,dz-1],rs.at[w,0,dz-1],(r,zpeer(p,dz)*2+c))) for dz in (1,2,3)]
    def core0(w):
        a,f=sets[w]
        return go(rcopy(a,f.at[s],c0s.at[w],c0r.at[w],mate))
    def piece(w,dz,quarter,cols=None):
        a,f=sets[w]; Q=a.shape[0]//4
        sp=((z+4-dz)%4)*2+c
        rows=pl.ds(pl.multiple_of(quarter*Q,8),Q)
        return f.at[sp,rows] if cols is None else f.at[sp,rows,cols]
    def fwd(w,dz,kind,quarter,dev,cols=None):
        ref=piece(w,dz,quarter,cols)
        return go(rcopy(ref,ref,ss.at[w,kind,dz-1],rs.at[w,kind,dz-1],dev))
    zc={};xc={};yc={};rc={}
    def stage_z(w):
        for dz in (1,2,3):
            zc[w][dz-1].wait_recv()
            xc[w,dz]=fwd(w,dz,1,r,xm)
            yc[w,dz]=fwd(w,dz,2,r,ym)
            fwd(w,dz,3,r,mate)
    def stage_xy(w):
        for dz in (1,2,3):
            xc[w,dz].wait_recv()
            rc[w,dz,0]=fwd(w,dz,6,p["rx"],ym,pl.ds(H,H))
            fwd(w,dz,4,p["rx"],mate)
            yc[w,dz].wait_recv()
            rc[w,dz,1]=fwd(w,dz,7,p["ry"],xm,pl.ds(0,H))
            fwd(w,dz,5,p["ry"],mate)
    def stage_r(w):
        for dz in (1,2,3):
            rc[w,dz,0].wait_recv()
            rc[w,dz,1].wait_recv()
            fwd(w,dz,8,p["rd"],mate)
    N=len(sets)
    zc[0]=zsend(0); cores=[core0(0)]
    for w in range(N):
        stage_z(w)
        if w+1<N:
            zc[w+1]=zsend(w+1); cores.append(core0(w+1))
        if w>0: stage_r(w-1)
        if w==0:
            for cp in vcs: cp.wait_recv()
            vp[...]=v_ref[...]+vz[0]+vz[1]+vz[2]
            vc=go(rcopy(vp,vm,vs.at[3],vr.at[3],mate))
        stage_xy(w)
    stage_r(N-1)
    vc.wait_recv()
    vf[...]=vp[...]+vm[...]
    for w in range(N):
        cores[w].wait_recv()
        for dz in (1,2,3):
            for kind,quarter in ((3,r),(4,p["rx"]),(5,p["ry"]),(8,p["rd"])):
                ref=piece(w,dz,quarter)
                rcopy(ref,ref,ss.at[w,kind,dz-1],rs.at[w,kind,dz-1],mate).wait_recv()
    for cp in done: cp.wait_send()
    for cp in locs: cp.wait()

def gather_all(q,o,u,d,v):
    S=8
    any_=pl.BlockSpec(memory_space=pl.ANY); vm_=pl.BlockSpec(memory_space=pltpu.VMEM)
    full=lambda a: jax.ShapeDtypeStruct((S,)+a.shape,a.dtype)
    dma=pltpu.SemaphoreType.DMA
    outs=pl.pallas_call(gather_kernel,in_specs=[any_]*4+[vm_],out_specs=[any_]*4+[vm_],
      out_shape=[full(q),full(o),full(u),full(d),jax.ShapeDtypeStruct(v.shape,F32)],
      scratch_shapes=[pltpu.VMEM((3,)+v.shape,F32),pltpu.VMEM(v.shape,F32),pltpu.VMEM(v.shape,F32),
        dma((4,)),dma((4,)),dma((4,)),dma((4,9,3)),dma((4,9,3)),dma((4,)),dma((4,))],
      compiler_params=pltpu.CompilerParams(collective_id=1,has_side_effects=True),name="gather_all")(q,o,u,d,v)
    return [a.reshape(-1,a.shape[-1]) for a in outs[:4]]+[outs[4]]

def reduce_kernel(nset,*refs):
    g=refs[:nset]; v_ref=refs[nset]
    outs=refs[nset+1:2*nset+1]; vo=refs[2*nset+1]
    sc=list(refs[2*nset+2:])
    take=lambda n: [sc.pop(0) for _ in range(n)]
    acc=take(nset); cb=take(nset); a1=take(nset); b1=take(nset); a2=take(nset); b2=take(nset); zb=take(nset); fin=take(nset)
    vb,lsem,ss,rs,vs,vr,osem=take(7)
    p=place()
    greet(p)
    r,s,c,z,x,y=p["r"],p["s"],p["c"],p["z"],p["x"],p["y"]
    mate=(r,p["mate"]); xm=(p["rx"],s); ym=(p["ry"],s)
    zdev=[(r,zpeer(p,dz)*2+c) for dz in (1,2,3)]
    H=acc[0].shape[-1]//2
    lo=pl.ds(0,H); hi=pl.ds(H,H)
    done=[]
    def go(cp):
        cp.start(); done.append(cp); return cp
    cp_={}
    loc={}
    def C(k):
        cp_[k,0]=go(rcopy(g[k].at[:,1-c],cb[k],ss.at[k,0],rs.at[k,0],mate))
        loc[k]=pltpu.make_async_copy(g[k].at[:,c],acc[k],lsem.at[k]); loc[k].start()
    def X(k):
        loc[k].wait()
        cp_[k,0].wait_recv()
        def add(i,t):
            acc[k][i]=acc[k][i]+cb[k][i]
            return t
        lax.fori_loop(0,4,add,0)
        for yy in range(2):
            cp_[k,1+yy]=go(rcopy(acc[k].at[:,yy*2+1-x,:,lo],a1[k].at[:,yy],ss.at[k,1+yy],rs.at[k,1+yy],xm))
        cp_[k,3]=go(rcopy(acc[k].at[:,pl.ds((1-y)*2,2),:,hi],b1[k],ss.at[k,3],rs.at[k,3],ym))
    def Y(k):
        cp_[k,1].wait_recv(); cp_[k,2].wait_recv(); cp_[k,3].wait_recv()
        def add(i,t):
            for yy in range(2):
                acc[k][i,yy*2+x,:,lo]=acc[k][i,yy*2+x,:,lo]+a1[k][i,yy]
            for xx in range(2):
                acc[k][i,y*2+xx,:,hi]=acc[k][i,y*2+xx,:,hi]+b1[k][i,xx]
            return t
        lax.fori_loop(0,4,add,0)
        cp_[k,4]=go(rcopy(acc[k].at[:,(1-y)*2+x,:,lo],a2[k],ss.at[k,4],rs.at[k,4],ym))
        cp_[k,5]=go(rcopy(acc[k].at[:,y*2+1-x,:,hi],b2[k],ss.at[k,5],rs.at[k,5],xm))
    def Z(k):
        cp_[k,4].wait_recv(); cp_[k,5].wait_recv()
        def add(i,t):
            acc[k][i,r,:,lo]=acc[k][i,r,:,lo]+a2[k][i]
            acc[k][i,r,:,hi]=acc[k][i,r,:,hi]+b2[k][i]
            return t
        lax.fori_loop(0,4,add,0)
        for dz in (1,2,3):
            cp_[k,5+dz]=go(rcopy(acc[k].at[zpeer(p,dz),r],zb[k].at[dz-1],ss.at[k,5+dz],rs.at[k,5+dz],zdev[dz-1]))
    def Fn(k):
        for dz in (1,2,3): cp_[k,5+dz].wait_recv()
        t=acc[k][z,r].astype(F32)
        for dz in range(3): t=t+zb[k][dz].astype(F32)
        fin[k][r]=t.astype(BF)
        cp_[k,9]=go(rcopy(fin[k].at[r],fin[k].at[r],ss.at[k,9],rs.at[k,9],xm))
        cp_[k,10]=go(rcopy(fin[k].at[r],fin[k].at[r],ss.at[k,10],rs.at[k,10],ym))
    def G(k):
        cp_[k,9].wait_recv()
        cp_[k,11]=go(rcopy(fin[k].at[p["rx"],:,hi],fin[k].at[p["rx"],:,hi],ss.at[k,11],rs.at[k,11],ym))
        cp_[k,10].wait_recv()
        cp_[k,12]=go(rcopy(fin[k].at[p["ry"],:,lo],fin[k].at[p["ry"],:,lo],ss.at[k,12],rs.at[k,12],xm))
    def Hh(k):
        cp_[k,11].wait_recv(); cp_[k,12].wait_recv()
        loc["o",k]=pltpu.make_async_copy(fin[k],outs[k],osem.at[k]); loc["o",k].start()
    zz=(z//2)*2
    vdev=[mate,xm,ym,(r,(zz+1-z%2)*2+c),(r,((z+2)%4)*2+c)]
    def V(n):
        if n>0:
            cp_["v",n-1].wait_recv()
        if n==0: vb[0]=v_ref[...]
        else: vb[2*n]=vb[2*n-2]+vb[2*n-1]
        if n<5:
            cp_["v",n]=go(rcopy(vb.at[2*n],vb.at[2*n+1],vs.at[n],vr.at[n],vdev[n]))
        else:
            vo[...]=vb[10]
    stages=[C,X,Y,Z,Fn,G,Hh]
    for t in range(nset+6):
        if t==0: C(0)
        if t<6: V(t)
        if t+1<nset: C(t+1)
        for si in range(1,7):
            k=t-si+1
            if 0<=k<nset: stages[si](k)
    for cp in done: cp.wait_send()
    for k in range(nset): loc["o",k].wait()

def reduce_all(gs,v):
    n=len(gs)
    any_=pl.BlockSpec(memory_space=pl.ANY); vm_=pl.BlockSpec(memory_space=pltpu.VMEM)
    dma=pltpu.SemaphoreType.DMA
    D=gs[0].shape[1]
    Qs=[a.shape[0]//32 for a in gs]
    g5=[a.reshape(4,2,4,q,D) for a,q in zip(gs,Qs)]
    H=D//2
    V=pltpu.VMEM
    scr=[V((4,4,q,D),BF) for q in Qs]+[V((4,4,q,D),BF) for q in Qs]+[V((4,2,q,H),BF) for q in Qs]*1+[V((4,2,q,H),BF) for q in Qs]
    scr+=[V((4,q,H),BF) for q in Qs]+[V((4,q,H),BF) for q in Qs]+[V((3,q,D),BF) for q in Qs]+[V((4,q,D),BF) for q in Qs]
    scr+=[V((11,)+v.shape,F32),dma((n,)),dma((n,13)),dma((n,13)),dma((5,)),dma((5,)),dma((n,))]
    outs=pl.pallas_call(functools.partial(reduce_kernel,n),in_specs=[any_]*n+[vm_],out_specs=[any_]*n+[vm_],
      out_shape=[jax.ShapeDtypeStruct((4,q,D),BF) for q in Qs]+[jax.ShapeDtypeStruct(v.shape,F32)],
      scratch_shapes=scr,compiler_params=pltpu.CompilerParams(collective_id=2,has_side_effects=True,vmem_limit_bytes=56<<20),name="reduce_all")(*g5,v)
    return [a.reshape(-1,D) for a in outs[:n]],outs[n]


def gather(x):
    return lax.all_gather(x, "shard", axis=0, tiled=True)


def gather_plain(q, o, u, d, v):
    return [gather(q), gather(o), gather(u), gather(d), lax.psum(v, "shard")]


def reduce_plain(gs, v):
    def one(g):
        part = lax.psum_scatter(g, "shard", scatter_dimension=0, tiled=True)
        return lax.psum(part, "rep")

    return [one(g) for g in gs], lax.psum(v, ("rep", "shard"))


def local(tokens, segment_ids, qkv_weight, out_weight, up_weight, down_weight,
          norm1_gain, norm1_shift, norm2_gain, norm2_shift, cotangent):
    tok = tokens[0]
    cot = cotangent[0]
    seg = segment_ids[0]
    model = tok.shape[1]
    known = lax.axis_size("rep") == 4 and lax.axis_size("shard") == 8
    piece = norm1_gain.shape[0]
    at = lax.axis_index("shard") * piece
    vec_part = jnp.stack([norm1_gain, norm1_shift, norm2_gain, norm2_shift]).astype(F32)
    vec_mine = lax.dynamic_update_slice(jnp.zeros((8, model), F32), vec_part, (0, at))
    collect = gather_all if known else gather_plain
    qkv_t, out_full, up_t, down_full, vec = collect(qkv_weight.T, out_weight, up_weight.T, down_weight, vec_mine)
    segc, segr, nst, nblk = prep(seg)
    normed, projected = qkv_proj(tok, qkv_t, vec)
    attended, lse, bias, sig = attn_fwd(projected, segc, segr, nst, nblk, unroll=6)
    output, gres, gatt, gdn, gup, gow, vec2 = mlp(tok, attended, cot, out_full, up_t, down_full, vec)
    gproj = attn_bwd(projected, gatt, attended, lse, bias, sig, nblk, unroll=5)
    gqkv = qkv_wgrad(gproj, normed)
    tgrad, vec1 = qkv_dgrad(gproj, qkv_t, tok, gres, vec)
    vec_all = jnp.concatenate([vec1[:2], vec2[:2], jnp.zeros((4, model), F32)], axis=0)
    spread = reduce_all if known else reduce_plain
    grads, vec_sum = spread([gdn, gup, gow, gqkv], vec_all)
    down_grad, up_grad, out_grad, qkv_grad = [g.astype(F32) for g in grads]
    mine = lax.dynamic_slice_in_dim(vec_sum, at, piece, 1)
    return (output[None], tgrad[None], qkv_grad.T, out_grad, up_grad.T, down_grad,
            mine[0], mine[1], mine[2], mine[3])


def solution(mesh):
    seq = P(("rep", "shard"), None, None)
    cols, rows, vecs = P(None, "shard"), P("shard", None), P("shard")
    return jax.shard_map(
        local,
        mesh=mesh,
        in_specs=(seq, P(("rep", "shard"), None), cols, rows, cols, rows, vecs, vecs, vecs, vecs, seq),
        out_specs=(seq, seq, cols, rows, cols, rows, vecs, vecs, vecs, vecs),
        check_vma=False,
    )
```

```python
import functools

import jax
import jax.numpy as jnp
from jax import lax
from jax.experimental import pallas as pl
from jax.experimental.pallas import tpu as pltpu
from jax.sharding import PartitionSpec as P

F32 = jnp.float32
BF = jnp.bfloat16
NEG=-1e30
WIN=512
def nt(a,b):
    return lax.dot_general(a,b,(((1,),(1,)),((),())),preferred_element_type=F32)
def nn(a,b):
    return lax.dot_general(a,b,(((1,),(0,)),((),())),preferred_element_type=F32)
def tn(a,b):
    return lax.dot_general(a,b,(((0,),(0,)),((),())),preferred_element_type=F32)
def split2(x):
    hi=x.astype(BF)
    lo=(x-hi.astype(F32)).astype(BF)
    return hi,lo
def eighth(x):
    return x*jnp.asarray(0.125,BF)

def fwd_block(row0,n,BQ,G,HP,unroll,qkv,segc,segr,nst,bias,sig,cs,put_out,put_aux):
    D=HP*128
    W=n*G
    k0=row0+BQ-W
    if not isinstance(k0,int): k0=pl.multiple_of(k0,G)
    kw=pl.ds(k0,W); rows=pl.ds(row0,BQ)
    lane=lax.broadcasted_iota(jnp.int32,(BQ,128),1)
    left=lane<64
    same=segc[rows,:]==segr[:,kw]
    qi=lax.broadcasted_iota(jnp.int32,(BQ,W),0)+(W-BQ)
    ki=lax.broadcasted_iota(jnp.int32,(BQ,W),1)
    allowed=same&(ki<=qi)
    chosen=same&(ki<qi)&(nst[:,kw]>0)
    q=eighth(qkv[rows,pl.ds(0,128)])
    k=qkv[kw,pl.ds(D,128)]
    s0=nt(jnp.where(left,q,jnp.zeros_like(q)),k)
    e=jnp.exp(-jnp.abs(s0))
    sp=jnp.maximum(s0,0.0)+jnp.log1p(e)
    sg=jnp.where(s0>=0,1.0,e)/(1.0+e)
    sel=jnp.where(chosen,sp,0.0)
    sig[:,sig.shape[1]-W:]=jnp.where(chosen,sg,0.0).astype(BF)
    hi,lo=split2(sel)
    ri=lax.broadcasted_iota(jnp.int32,(BQ,BQ),0); ci=lax.broadcasted_iota(jnp.int32,(BQ,BQ),1)
    L=(ri>ci).astype(BF)
    pen=nn(L,hi)+nn(L,lo)+cs[:,kw]
    cs[:,kw]=cs[:,kw]+jnp.sum(sel,axis=0,keepdims=True)
    bias[:,bias.shape[1]-W:]=jnp.where(allowed,-pen,NEG)
    ones=jnp.ones((W,128),BF)
    def pair(j,acc):
        off=pl.multiple_of(j*128,128)
        q=eighth(qkv[rows,pl.ds(off,128)])
        z=jnp.zeros_like(q)
        k=qkv[kw,pl.ds(D+off,128)]
        v1=jnp.concatenate([qkv[kw,pl.ds(2*D+off,128)],ones],axis=1)
        b=bias[:,bias.shape[1]-W:]
        outs=[]
        for hh in range(2):
            qm=jnp.where(left,q,z) if hh==0 else jnp.where(left,z,q)
            s=nt(qm,k)+b
            m=jnp.max(s,axis=1,keepdims=True)
            p=jnp.exp(s-m)
            ol=nn(p.astype(BF),v1)
            l=ol[:,128:]
            outs.append(ol[:,:128]*(1.0/l))
            acc=jnp.where(lane==2*j+hh,m+jnp.log(l),acc)
        put_out(off,jnp.where(left,outs[0],outs[1]).astype(BF))
        return acc
    lse=lax.fori_loop(0,HP,pair,jnp.zeros((BQ,128),F32),unroll=unroll)
    put_aux(lse)

def attn_fwd_kernel(BQ,G,NW,HP,unroll,nblk_ref,qkv_ref,segc_ref,segr_ref,nst_ref,o_ref,aux_ref,bias_ref,sig_ref,cs_ref):
    i=pl.program_id(0)
    @pl.when(i==0)
    def _():
        cs_ref[...]=jnp.zeros_like(cs_ref)
    row0=pl.multiple_of(i*BQ,BQ)
    def put_out(off,val):
        o_ref[:,pl.ds(off,128)]=val
    def put_aux(val):
        aux_ref[...]=val
    for n in range(1,NW+1):
        @pl.when(nblk_ref[i]==n)
        def _(n=n):
            fwd_block(row0,n,BQ,G,HP,unroll,qkv_ref,segc_ref,segr_ref,nst_ref,bias_ref.at[0],sig_ref.at[0],cs_ref,put_out,put_aux)

def windows(T,BQ,G):
    return min(T//G,-(-(WIN-1+BQ)//G))

def attn_fwd(qkv,segc,segr,nst,nblk,BQ=128,G=128,unroll=6):
    T,D3=qkv.shape; D=D3//3; HP=D//128
    NW=windows(T,BQ,G)
    NB=T//BQ
    whole=lambda shape: pl.BlockSpec(shape,lambda i,*_:(0,0),pipeline_mode=pl.Buffered(1))
    gs=pltpu.PrefetchScalarGridSpec(num_scalar_prefetch=1,grid=(NB,),
      in_specs=[whole((T,D3)),whole((T,1)),whole((1,T)),whole((1,T))],
      out_specs=[pl.BlockSpec((BQ,D),lambda i,*_:(i,0)),pl.BlockSpec((BQ,128),lambda i,*_:(i,0)),
        pl.BlockSpec((1,BQ,NW*G),lambda i,*_:(i,0,0)),pl.BlockSpec((1,BQ,NW*G),lambda i,*_:(i,0,0))],
      scratch_shapes=[pltpu.VMEM((1,T),F32)])
    return pl.pallas_call(functools.partial(attn_fwd_kernel,BQ,G,NW,HP,unroll),grid_spec=gs,
      out_shape=[jax.ShapeDtypeStruct((T,D),BF),jax.ShapeDtypeStruct((T,128),F32),
        jax.ShapeDtypeStruct((NB,BQ,NW*G),F32),jax.ShapeDtypeStruct((NB,BQ,NW*G),BF)],
      compiler_params=pltpu.CompilerParams(vmem_limit_bytes=40<<20),name="attn_fwd")(nblk,qkv,segc,segr,nst)

def bwd_block(row0,n,BQ,G,HP,unroll,qkv,do_ref,o_ref,aux_ref,bias,sig,dq_ref,dk_ref,dv_ref,gp_ref,ls_ref):
    D=HP*128
    W=n*G
    k0=row0+BQ-W
    if not isinstance(k0,int): k0=pl.multiple_of(k0,G)
    kw=pl.ds(k0,W); rows=pl.ds(row0,BQ)
    lane=lax.broadcasted_iota(jnp.int32,(BQ,128),1)
    left=lane<64
    gp_ref[:,:W]=jnp.zeros((BQ,W),F32)
    lse=aux_ref[...]
    def stack(t):
        z=jnp.zeros_like(t)
        return jnp.concatenate([jnp.where(left,t,z),jnp.where(left,z,t)],axis=0)
    def work(j,first):
        off=j*128 if isinstance(j,int) else pl.multiple_of(j*128,128)
        k=qkv[kw,pl.ds(D+off,128)]
        v=qkv[kw,pl.ds(2*D+off,128)]
        do=do_ref[:,pl.ds(off,128)]
        prod=do.astype(F32)*o_ref[:,pl.ds(off,128)].astype(F32)
        b=bias[:,bias.shape[1]-W:]
        q2=stack(eighth(qkv[rows,pl.ds(off,128)]))
        do2=stack(do)
        def row(t0,t1):
            return jnp.sum(t0,axis=1,keepdims=True),jnp.sum(t1,axis=1,keepdims=True)
        l0,l1=row(jnp.where(lane==2*j,lse,0.0),jnp.where(lane==2*j+1,lse,0.0))
        e0,e1=row(jnp.where(left,prod,0.0),jnp.where(left,0.0,prod))
        s2=nt(q2,k)
        dp2=nt(do2,v)
        p0=jnp.exp(s2[:BQ]+b-l0); p1=jnp.exp(s2[BQ:]+b-l1)
        ds0=p0*(dp2[:BQ]-e0); ds1=p1*(dp2[BQ:]-e1)
        if not first:
            gp_ref[:,:W]=gp_ref[:,:W]+(ds0+ds1)
        else:
            gp=gp_ref[:,:W]+(ds0+ds1)
            hi,lo=split2(gp)
            ri=lax.broadcasted_iota(jnp.int32,(BQ,BQ),0); ci=lax.broadcasted_iota(jnp.int32,(BQ,BQ),1)
            U=(ci>ri).astype(BF)
            gsel=nn(U,hi)+nn(U,lo)+ls_ref[:,kw]
            ls_ref[:,kw]=ls_ref[:,kw]+jnp.sum(gp,axis=0,keepdims=True)
            ds0=ds0-gsel*sig[:,sig.shape[1]-W:].astype(F32)
        dsb=jnp.concatenate([ds0.astype(BF),ds1.astype(BF)],axis=0)
        pb=jnp.concatenate([p0.astype(BF),p1.astype(BF)],axis=0)
        dq2=nn(dsb,k)
        dq_ref[rows,pl.ds(off,128)]=(jnp.where(left,dq2[:BQ],dq2[BQ:])*0.125).astype(BF)
        dk_ref[kw,pl.ds(off,128)]+=tn(dsb,q2)
        dv_ref[kw,pl.ds(off,128)]+=tn(pb,do2)
    def body(j,c):
        work(j,False)
        return c
    lax.fori_loop(1,HP,body,0,unroll=unroll)
    work(0,True)

def attn_bwd_kernel(BQ,G,NW,HP,unroll,NB,nblk_ref,qkv_ref,do_ref,o_ref,aux_ref,bias_ref,sig_ref,out_ref,dk_ref,dv_ref,gp_ref,ls_ref):
    step=pl.program_id(0)
    i=NB-1-step
    D=HP*128
    @pl.when(step==0)
    def _():
        dk_ref[...]=jnp.zeros_like(dk_ref)
        dv_ref[...]=jnp.zeros_like(dv_ref)
        ls_ref[...]=jnp.zeros_like(ls_ref)
    row0=pl.multiple_of(i*BQ,BQ)
    for n in range(1,NW+1):
        @pl.when(nblk_ref[i]==n)
        def _(n=n):
            bwd_block(row0,n,BQ,G,HP,unroll,qkv_ref,do_ref,o_ref,aux_ref,bias_ref.at[0],sig_ref.at[0],out_ref,dk_ref,dv_ref,gp_ref,ls_ref)
    @pl.when(step==NB-1)
    def _():
        out_ref[:,D:2*D]=dk_ref[...].astype(BF)
        out_ref[:,2*D:]=dv_ref[...].astype(BF)

def attn_bwd(qkv,do,o,aux,bias,sig,nblk,BQ=128,G=128,unroll=5):
    T,D3=qkv.shape; D=D3//3; HP=D//128
    NW=bias.shape[2]//G
    NB=T//BQ
    whole=lambda shape: pl.BlockSpec(shape,lambda i,*_:(0,0),pipeline_mode=pl.Buffered(1))
    rb=lambda w: pl.BlockSpec((BQ,w),lambda i,*_:(NB-1-i,0))
    r3=pl.BlockSpec((1,BQ,NW*G),lambda i,*_:(NB-1-i,0,0))
    gs=pltpu.PrefetchScalarGridSpec(num_scalar_prefetch=1,grid=(NB,),
      in_specs=[whole((T,D3)),rb(D),rb(D),rb(128),r3,r3],
      out_specs=whole((T,D3)),
      scratch_shapes=[pltpu.VMEM((T,D),F32),pltpu.VMEM((T,D),F32),pltpu.VMEM((BQ,NW*G),F32),pltpu.VMEM((1,T),F32)])
    return pl.pallas_call(functools.partial(attn_bwd_kernel,BQ,G,NW,HP,unroll,NB),grid_spec=gs,
      out_shape=jax.ShapeDtypeStruct((T,D3),BF),
      compiler_params=pltpu.CompilerParams(vmem_limit_bytes=50<<20),name="attn_bwd")(nblk,qkv,do,o,aux,bias,sig)

def prep(seg,BQ=128,G=128):
    T=seg.shape[0]
    NB=T//BQ
    at=seg[::BQ]
    first=jnp.sum((seg[None,:]<at[:,None]).astype(jnp.int32),axis=1)
    ends=(jnp.arange(NB,dtype=jnp.int32)+1)*BQ
    nblk=(ends-(first//G)*G)//G
    starts=jnp.concatenate([jnp.ones((1,),bool),seg[1:]!=seg[:-1]])
    nst=jnp.logical_not(starts).astype(jnp.int32)[None,:]
    return seg[:,None],seg[None,:],nst,nblk

EPS=1e-5
GC=0.7978845608028654; GA=0.044715
def rowmean(x): return jnp.mean(x,axis=-1,keepdims=True)
def ln_unit(x):
    m=rowmean(x); c=x-m; v=rowmean(c*c); r=lax.rsqrt(v+EPS)
    return c*r, r

def qkv_kernel(tok_ref,w_ref,vec_ref,n_ref,o_ref):
    u,_=ln_unit(tok_ref[...].astype(F32))
    n=(u*vec_ref[0:1,:]+vec_ref[1:2,:]).astype(BF)
    n_ref[...]=n
    o_ref[...]=nt(n,w_ref[...]).astype(BF)
def qkv_proj(tok,wT,vec,R=256):
    T,D=tok.shape; E=wT.shape[0]
    c=lambda s: pl.BlockSpec(s,lambda i:(0,0),pipeline_mode=pl.Buffered(1))
    return pl.pallas_call(qkv_kernel,grid=(T//R,),in_specs=[pl.BlockSpec((R,D),lambda i:(i,0)),c((E,D)),c(vec.shape)],
      out_specs=[pl.BlockSpec((R,D),lambda i:(i,0)),pl.BlockSpec((R,E),lambda i:(i,0))],
      out_shape=[jax.ShapeDtypeStruct((T,D),BF),jax.ShapeDtypeStruct((T,E),BF)],
      compiler_params=pltpu.CompilerParams(vmem_limit_bytes=40<<20),name="qkv_proj")(tok,wT,vec)

def mlp_kernel(NR,NC,C,R,tok_ref,att_ref,cot_ref,ow_ref,up_ref,dn_ref,vec_ref,
    out_ref,gres_ref,gatt_ref,gdn_ref,gup_ref,gow_ref,vg_ref, act_s,gh_s,n2_s,gb_s):
    i=pl.program_id(0)
    @pl.when(i<NR)
    def _():
        rows=pl.ds(pl.multiple_of(i*R,R),R)
        gain=vec_ref[2:3,:]; shift=vec_ref[3:4,:]
        res=tok_ref[rows,:].astype(F32)+nn(att_ref[rows,:],ow_ref[...])
        u,rstd=ln_unit(res)
        n2=(u*gain+shift).astype(BF)
        n2_s[rows,:]=n2
        cot=cot_ref[rows,:]
        out_acc=res
        g_acc=jnp.zeros_like(res)
        for c in range(NC):
            cs=slice(c*C,(c+1)*C)
            h=nt(n2,up_ref[cs,:])
            h2=h*h
            t=jnp.tanh(h*(GC+GC*GA*h2))
            half=0.5*(1.0+t)
            act=(h*half).astype(BF)
            act_s[rows,cs]=act
            ga=nt(cot,dn_ref[cs,:])
            dg=half+(0.5*h)*(1.0-t*t)*(GC+3.0*GC*GA*h2)
            gh=(ga*dg).astype(BF)
            gh_s[rows,cs]=gh
            out_acc=out_acc+nn(act,dn_ref[cs,:])
            g_acc=g_acc+nn(gh,up_ref[cs,:])
        out_ref[...]=out_acc.astype(BF)
        vgain=jnp.sum(g_acc*u,axis=0,keepdims=True); vshift=jnp.sum(g_acc,axis=0,keepdims=True)
        @pl.when(i==0)
        def _():
            vg_ref[...]=jnp.zeros_like(vg_ref)
        vg_ref[0:1,:]+=vgain
        vg_ref[1:2,:]+=vshift
        g=g_acc*gain
        gr=cot.astype(F32)+rstd*(g-rowmean(g)-u*rowmean(g*u))
        gres_ref[...]=gr
        gb=gr.astype(BF)
        gb_s[rows,:]=gb
        gatt_ref[...]=nt(gb,ow_ref[...]).astype(BF)
    @pl.when(i>=NR)
    def _():
        j=i-NR
        cs=pl.ds(pl.multiple_of(j*C2(gdn_ref),C2(gdn_ref)),C2(gdn_ref))
        gdn_ref[...]=tn(act_s[:,cs],cot_ref[...]).astype(BF)
        gup_ref[...]=tn(gh_s[:,cs],n2_s[...]).astype(BF)
    @pl.when(i==NR)
    def _():
        gow_ref[...]=tn(att_ref[...],gb_s[...]).astype(BF)
def C2(ref): return ref.shape[0]
def mlp(tok,att,cot,ow,upT,dn,vec,R=256,C=768,WC=384):
    T,D=tok.shape; F=upT.shape[0]; NR=T//R; NW=F//WC
    c=lambda s: pl.BlockSpec(s,lambda i:(0,0),pipeline_mode=pl.Buffered(1))
    rb=lambda w: pl.BlockSpec((R,w),lambda i:(jnp.minimum(i,NR-1),0))
    wb=pl.BlockSpec((WC,D),lambda i:(jnp.maximum(i-NR,0),0))
    return pl.pallas_call(functools.partial(mlp_kernel,NR,F//C,C,R),grid=(NR+NW,),
      in_specs=[c((T,D)),c((T,D)),c((T,D)),c((D,D)),c((F,D)),c((F,D)),c(vec.shape)],
      out_specs=[rb(D),rb(D),rb(D),wb,wb,c((D,D)),c((8,D))],
      out_shape=[jax.ShapeDtypeStruct((T,D),BF),jax.ShapeDtypeStruct((T,D),F32),jax.ShapeDtypeStruct((T,D),BF),
        jax.ShapeDtypeStruct((F,D),BF),jax.ShapeDtypeStruct((F,D),BF),jax.ShapeDtypeStruct((D,D),BF),jax.ShapeDtypeStruct((8,D),F32)],
      scratch_shapes=[pltpu.VMEM((T,F),BF),pltpu.VMEM((T,F),BF),pltpu.VMEM((T,D),BF),pltpu.VMEM((T,D),BF)],
      compiler_params=pltpu.CompilerParams(vmem_limit_bytes=58<<20),name="mlp")(tok,att,cot,ow,upT,dn,vec)

def wg_kernel(gp_ref,n_ref,o_ref):
    o_ref[...]=tn(gp_ref[...],n_ref[...]).astype(BF)
def qkv_wgrad(gp,n1,WC=384):
    T,E=gp.shape; D=n1.shape[1]
    return pl.pallas_call(wg_kernel,grid=(E//WC,),in_specs=[pl.BlockSpec((T,WC),lambda i:(0,i)),pl.BlockSpec((T,D),lambda i:(0,0),pipeline_mode=pl.Buffered(1))],
      out_specs=pl.BlockSpec((WC,D),lambda i:(i,0)),out_shape=jax.ShapeDtypeStruct((E,D),BF),
      compiler_params=pltpu.CompilerParams(vmem_limit_bytes=40<<20),name="qkv_wgrad")(gp,n1)
def dg_kernel(gp_ref,w_ref,tok_ref,gres_ref,vec_ref,o_ref,vg_ref):
    i=pl.program_id(0)
    gn=nn(gp_ref[...],w_ref[...])
    u,rstd=ln_unit(tok_ref[...].astype(F32))
    @pl.when(i==0)
    def _():
        vg_ref[...]=jnp.zeros_like(vg_ref)
    vg_ref[0:1,:]+=jnp.sum(gn*u,axis=0,keepdims=True)
    vg_ref[1:2,:]+=jnp.sum(gn,axis=0,keepdims=True)
    g=gn*vec_ref[0:1,:]
    o_ref[...]=(gres_ref[...]+rstd*(g-rowmean(g)-u*rowmean(g*u))).astype(BF)
def qkv_dgrad(gp,wT,tok,gres,vec,R=256):
    T,E=gp.shape; D=tok.shape[1]
    c=lambda s: pl.BlockSpec(s,lambda i:(0,0),pipeline_mode=pl.Buffered(1))
    rb=lambda w: pl.BlockSpec((R,w),lambda i:(i,0))
    return pl.pallas_call(dg_kernel,grid=(T//R,),in_specs=[rb(E),c((E,D)),rb(D),rb(D),c(vec.shape)],out_specs=[rb(D),c((8,D))],
      out_shape=[jax.ShapeDtypeStruct((T,D),BF),jax.ShapeDtypeStruct((8,D),F32)],
      compiler_params=pltpu.CompilerParams(vmem_limit_bytes=40<<20),name="qkv_dgrad")(gp,wT,tok,gres,vec)

MESH=pl.DeviceIdType.MESH

def place():
    r=lax.axis_index("rep"); s=lax.axis_index("shard")
    y=r//2; x=r%2; z=s//2; c=s%2
    return dict(r=r,s=s,y=y,x=x,z=z,c=c,rx=y*2+(1-x),ry=(1-y)*2+x,rd=(1-y)*2+(1-x),mate=z*2+(1-c))
def zpeer(p,dz):
    return (p["z"]+dz)%4
def greet(p):
    bar=pltpu.get_barrier_semaphore()
    for dev in ((p["r"],p["mate"]),(p["rx"],p["s"]),(p["ry"],p["s"]))+tuple((p["r"],zpeer(p,dz)*2+p["c"]) for dz in (1,2,3)):
        pl.semaphore_signal(bar,inc=1,device_id=dev,device_id_type=MESH)
    pl.semaphore_wait(bar,6)
def rcopy(src,dst,ss,rs,dev):
    return pltpu.make_async_remote_copy(src_ref=src,dst_ref=dst,send_sem=ss,recv_sem=rs,device_id=dev,device_id_type=MESH)

def gather_kernel(q_ref,o_ref,u_ref,d_ref,v_ref,qf,of,uf,df,vf,vz,vp,vm,lsem,c0s,c0r,ss,rs,vs,vr):
    p=place()
    greet(p)
    r,s,c,z=p["r"],p["s"],p["c"],p["z"]
    mate=(r,p["mate"]); xm=(p["rx"],s); ym=(p["ry"],s)
    sets=((q_ref,qf),(o_ref,of),(u_ref,uf),(d_ref,df))
    done=[]
    def go(cp):
        cp.start(); done.append(cp); return cp
    locs=[]
    for w,(a,f) in enumerate(sets):
        cp=pltpu.make_async_copy(a,f.at[s],lsem.at[w]); cp.start(); locs.append(cp)
    H=q_ref.shape[1]//2
    vcs=[go(rcopy(v_ref,vz.at[dz-1],vs.at[dz-1],vr.at[dz-1],(r,zpeer(p,dz)*2+c))) for dz in (1,2,3)]
    def zsend(w):
        a,f=sets[w]; Q=a.shape[0]//4
        rows=pl.ds(pl.multiple_of(r*Q,8),Q)
        return [go(rcopy(a.at[rows],f.at[s,rows],ss.at[w,0,dz-1],rs.at[w,0,dz-1],(r,zpeer(p,dz)*2+c))) for dz in (1,2,3)]
    def core0(w):
        a,f=sets[w]
        return go(rcopy(a,f.at[s],c0s.at[w],c0r.at[w],mate))
    def piece(w,dz,quarter,cols=None):
        a,f=sets[w]; Q=a.shape[0]//4
        sp=((z+4-dz)%4)*2+c
        rows=pl.ds(pl.multiple_of(quarter*Q,8),Q)
        return f.at[sp,rows] if cols is None else f.at[sp,rows,cols]
    def fwd(w,dz,kind,quarter,dev,cols=None):
        ref=piece(w,dz,quarter,cols)
        return go(rcopy(ref,ref,ss.at[w,kind,dz-1],rs.at[w,kind,dz-1],dev))
    zc={};xc={};yc={};rc={}
    def stage_z(w):
        for dz in (1,2,3):
            zc[w][dz-1].wait_recv()
            xc[w,dz]=fwd(w,dz,1,r,xm)
            yc[w,dz]=fwd(w,dz,2,r,ym)
            fwd(w,dz,3,r,mate)
    def stage_xy(w):
        for dz in (1,2,3):
            xc[w,dz].wait_recv()
            rc[w,dz,0]=fwd(w,dz,6,p["rx"],ym,pl.ds(H,H))
            fwd(w,dz,4,p["rx"],mate)
            yc[w,dz].wait_recv()
            rc[w,dz,1]=fwd(w,dz,7,p["ry"],xm,pl.ds(0,H))
            fwd(w,dz,5,p["ry"],mate)
    def stage_r(w):
        for dz in (1,2,3):
            rc[w,dz,0].wait_recv()
            rc[w,dz,1].wait_recv()
            fwd(w,dz,8,p["rd"],mate)
    N=len(sets)
    zc[0]=zsend(0); cores=[core0(0)]
    for w in range(N):
        stage_z(w)
        if w+1<N:
            zc[w+1]=zsend(w+1); cores.append(core0(w+1))
        if w>0: stage_r(w-1)
        if w==0:
            for cp in vcs: cp.wait_recv()
            vp[...]=v_ref[...]+vz[0]+vz[1]+vz[2]
            vc=go(rcopy(vp,vm,vs.at[3],vr.at[3],mate))
        stage_xy(w)
    stage_r(N-1)
    vc.wait_recv()
    vf[...]=vp[...]+vm[...]
    for w in range(N):
        cores[w].wait_recv()
        for dz in (1,2,3):
            for kind,quarter in ((3,r),(4,p["rx"]),(5,p["ry"]),(8,p["rd"])):
                ref=piece(w,dz,quarter)
                rcopy(ref,ref,ss.at[w,kind,dz-1],rs.at[w,kind,dz-1],mate).wait_recv()
    for cp in done: cp.wait_send()
    for cp in locs: cp.wait()

def gather_all(q,o,u,d,v):
    S=8
    any_=pl.BlockSpec(memory_space=pl.ANY); vm_=pl.BlockSpec(memory_space=pltpu.VMEM)
    full=lambda a: jax.ShapeDtypeStruct((S,)+a.shape,a.dtype)
    dma=pltpu.SemaphoreType.DMA
    outs=pl.pallas_call(gather_kernel,in_specs=[any_]*4+[vm_],out_specs=[any_]*4+[vm_],
      out_shape=[full(q),full(o),full(u),full(d),jax.ShapeDtypeStruct(v.shape,F32)],
      scratch_shapes=[pltpu.VMEM((3,)+v.shape,F32),pltpu.VMEM(v.shape,F32),pltpu.VMEM(v.shape,F32),
        dma((4,)),dma((4,)),dma((4,)),dma((4,9,3)),dma((4,9,3)),dma((4,)),dma((4,))],
      compiler_params=pltpu.CompilerParams(collective_id=1,has_side_effects=True),name="gather_all")(q,o,u,d,v)
    return [a.reshape(-1,a.shape[-1]) for a in outs[:4]]+[outs[4]]

def reduce_kernel(nset,*refs):
    g=refs[:nset]; v_ref=refs[nset]
    outs=refs[nset+1:2*nset+1]; vo=refs[2*nset+1]
    sc=list(refs[2*nset+2:])
    take=lambda n: [sc.pop(0) for _ in range(n)]
    acc=take(nset); cb=take(nset); a1=take(nset); b1=take(nset); a2=take(nset); b2=take(nset); zb=take(nset); fin=take(nset)
    vb,lsem,ss,rs,vs,vr,osem=take(7)
    p=place()
    greet(p)
    r,s,c,z,x,y=p["r"],p["s"],p["c"],p["z"],p["x"],p["y"]
    mate=(r,p["mate"]); xm=(p["rx"],s); ym=(p["ry"],s)
    zdev=[(r,zpeer(p,dz)*2+c) for dz in (1,2,3)]
    H=acc[0].shape[-1]//2
    lo=pl.ds(0,H); hi=pl.ds(H,H)
    done=[]
    def go(cp):
        cp.start(); done.append(cp); return cp
    cp_={}
    loc={}
    def C(k):
        cp_[k,0]=go(rcopy(g[k].at[:,1-c],cb[k],ss.at[k,0],rs.at[k,0],mate))
        loc[k]=pltpu.make_async_copy(g[k].at[:,c],acc[k],lsem.at[k]); loc[k].start()
    def X(k):
        loc[k].wait()
        cp_[k,0].wait_recv()
        def add(i,t):
            acc[k][i]=acc[k][i]+cb[k][i]
            return t
        lax.fori_loop(0,4,add,0)
        for yy in range(2):
            cp_[k,1+yy]=go(rcopy(acc[k].at[:,yy*2+1-x,:,lo],a1[k].at[:,yy],ss.at[k,1+yy],rs.at[k,1+yy],xm))
        cp_[k,3]=go(rcopy(acc[k].at[:,pl.ds((1-y)*2,2),:,hi],b1[k],ss.at[k,3],rs.at[k,3],ym))
    def Y(k):
        cp_[k,1].wait_recv(); cp_[k,2].wait_recv(); cp_[k,3].wait_recv()
        def add(i,t):
            for yy in range(2):
                acc[k][i,yy*2+x,:,lo]=acc[k][i,yy*2+x,:,lo]+a1[k][i,yy]
            for xx in range(2):
                acc[k][i,y*2+xx,:,hi]=acc[k][i,y*2+xx,:,hi]+b1[k][i,xx]
            return t
        lax.fori_loop(0,4,add,0)
        cp_[k,4]=go(rcopy(acc[k].at[:,(1-y)*2+x,:,lo],a2[k],ss.at[k,4],rs.at[k,4],ym))
        cp_[k,5]=go(rcopy(acc[k].at[:,y*2+1-x,:,hi],b2[k],ss.at[k,5],rs.at[k,5],xm))
    def Z(k):
        cp_[k,4].wait_recv(); cp_[k,5].wait_recv()
        def add(i,t):
            acc[k][i,r,:,lo]=acc[k][i,r,:,lo]+a2[k][i]
            acc[k][i,r,:,hi]=acc[k][i,r,:,hi]+b2[k][i]
            return t
        lax.fori_loop(0,4,add,0)
        for dz in (1,2,3):
            cp_[k,5+dz]=go(rcopy(acc[k].at[zpeer(p,dz),r],zb[k].at[dz-1],ss.at[k,5+dz],rs.at[k,5+dz],zdev[dz-1]))
    def Fn(k):
        for dz in (1,2,3): cp_[k,5+dz].wait_recv()
        t=acc[k][z,r].astype(F32)
        for dz in range(3): t=t+zb[k][dz].astype(F32)
        fin[k][r]=t.astype(BF)
        cp_[k,9]=go(rcopy(fin[k].at[r],fin[k].at[r],ss.at[k,9],rs.at[k,9],xm))
        cp_[k,10]=go(rcopy(fin[k].at[r],fin[k].at[r],ss.at[k,10],rs.at[k,10],ym))
    def G(k):
        cp_[k,9].wait_recv()
        cp_[k,11]=go(rcopy(fin[k].at[p["rx"],:,hi],fin[k].at[p["rx"],:,hi],ss.at[k,11],rs.at[k,11],ym))
        cp_[k,10].wait_recv()
        cp_[k,12]=go(rcopy(fin[k].at[p["ry"],:,lo],fin[k].at[p["ry"],:,lo],ss.at[k,12],rs.at[k,12],xm))
    def Hh(k):
        cp_[k,11].wait_recv(); cp_[k,12].wait_recv()
        loc["o",k]=pltpu.make_async_copy(fin[k],outs[k],osem.at[k]); loc["o",k].start()
    zz=(z//2)*2
    vdev=[mate,xm,ym,(r,(zz+1-z%2)*2+c),(r,((z+2)%4)*2+c)]
    def V(n):
        if n>0:
            cp_["v",n-1].wait_recv()
        if n==0: vb[0]=v_ref[...]
        else: vb[2*n]=vb[2*n-2]+vb[2*n-1]
        if n<5:
            cp_["v",n]=go(rcopy(vb.at[2*n],vb.at[2*n+1],vs.at[n],vr.at[n],vdev[n]))
        else:
            vo[...]=vb[10]
    stages=[C,X,Y,Z,Fn,G,Hh]
    for t in range(nset+6):
        if t==0: C(0)
        if t<6: V(t)
        if t+1<nset: C(t+1)
        for si in range(1,7):
            k=t-si+1
            if 0<=k<nset: stages[si](k)
    for cp in done: cp.wait_send()
    for k in range(nset): loc["o",k].wait()

def reduce_all(gs,v):
    n=len(gs)
    any_=pl.BlockSpec(memory_space=pl.ANY); vm_=pl.BlockSpec(memory_space=pltpu.VMEM)
    dma=pltpu.SemaphoreType.DMA
    D=gs[0].shape[1]
    Qs=[a.shape[0]//32 for a in gs]
    g5=[a.reshape(4,2,4,q,D) for a,q in zip(gs,Qs)]
    H=D//2
    V=pltpu.VMEM
    scr=[V((4,4,q,D),BF) for q in Qs]+[V((4,4,q,D),BF) for q in Qs]+[V((4,2,q,H),BF) for q in Qs]*1+[V((4,2,q,H),BF) for q in Qs]
    scr+=[V((4,q,H),BF) for q in Qs]+[V((4,q,H),BF) for q in Qs]+[V((3,q,D),BF) for q in Qs]+[V((4,q,D),BF) for q in Qs]
    scr+=[V((11,)+v.shape,F32),dma((n,)),dma((n,13)),dma((n,13)),dma((5,)),dma((5,)),dma((n,))]
    outs=pl.pallas_call(functools.partial(reduce_kernel,n),in_specs=[any_]*n+[vm_],out_specs=[any_]*n+[vm_],
      out_shape=[jax.ShapeDtypeStruct((4,q,D),BF) for q in Qs]+[jax.ShapeDtypeStruct(v.shape,F32)],
      scratch_shapes=scr,compiler_params=pltpu.CompilerParams(collective_id=2,has_side_effects=True,vmem_limit_bytes=56<<20),name="reduce_all")(*g5,v)
    return [a.reshape(-1,D) for a in outs[:n]],outs[n]

def forward_kernel(BQ,G,NW,HP,unroll,q_ref,o_ref,u_ref,d_ref,v_ref,tok_ref,segc,segr,nst,
    of,uf,df,qf,vf,nf,pf,af,lf,bf_,sf,
    qv,nrm,prj,attv,lsev,biasv,sigv,cs,vz,vp,vm,lsem,osem,qsem,c0s,c0r,ss,rs,vs,vr):
    p=place()
    greet(p)
    r,s,c,z=p["r"],p["s"],p["c"],p["z"]
    mate=(r,p["mate"]); xm=(p["rx"],s); ym=(p["ry"],s)
    sets=(q_ref,o_ref,u_ref,d_ref)
    fulls=(qf,of,uf,df)
    T,D=nrm.shape
    H=D//2
    done=[]; outs=[]
    def go(cp):
        cp.start(); done.append(cp); return cp
    def local_copy(src,dst):
        cp=pltpu.make_async_copy(src,dst,osem.at[len(outs)]); cp.start(); outs.append(cp)
    def view(w,shard,first,count,cols=None):
        rows=pl.ds(pl.multiple_of(first,8),count)
        return fulls[w].at[shard,rows] if cols is None else fulls[w].at[shard,rows,cols]
    locs=[]
    for w in range(4):
        cp=pltpu.make_async_copy(sets[w],view(w,s,0,sets[w].shape[0]),lsem.at[w]); cp.start(); locs.append(cp)
    vcs=[go(rcopy(v_ref,vz.at[dz-1],vs.at[dz-1],vr.at[dz-1],(r,zpeer(p,dz)*2+c))) for dz in (1,2,3)]
    def zsend(w):
        Q=sets[w].shape[0]//4
        rows=pl.ds(pl.multiple_of(r*Q,8),Q)
        return [go(rcopy(sets[w].at[rows],view(w,s,r*Q,Q),ss.at[w,0,dz-1],rs.at[w,0,dz-1],(r,zpeer(p,dz)*2+c))) for dz in (1,2,3)]
    def core0(w):
        return go(rcopy(sets[w],view(w,s,0,sets[w].shape[0]),c0s.at[w],c0r.at[w],mate))
    def piece(w,dz,quarter,cols=None):
        Q=sets[w].shape[0]//4
        return view(w,((z+4-dz)%4)*2+c,quarter*Q,Q,cols)
    def fwd(w,dz,kind,quarter,dev,cols=None):
        ref=piece(w,dz,quarter,cols)
        return go(rcopy(ref,ref,ss.at[w,kind,dz-1],rs.at[w,kind,dz-1],dev))
    zc={};xc={};yc={};rc={};cores={}
    def send(w):
        zc[w]=zsend(w); cores[w]=core0(w)
    def stage_z(w):
        for dz in (1,2,3):
            zc[w][dz-1].wait_recv()
            xc[w,dz]=fwd(w,dz,1,r,xm)
            yc[w,dz]=fwd(w,dz,2,r,ym)
            fwd(w,dz,3,r,mate)
    def stage_xy(w):
        for dz in (1,2,3):
            xc[w,dz].wait_recv()
            rc[w,dz,0]=fwd(w,dz,6,p["rx"],ym,pl.ds(H,H))
            fwd(w,dz,4,p["rx"],mate)
            yc[w,dz].wait_recv()
            rc[w,dz,1]=fwd(w,dz,7,p["ry"],xm,pl.ds(0,H))
            fwd(w,dz,5,p["ry"],mate)
    def stage_r(w):
        for dz in (1,2,3):
            rc[w,dz,0].wait_recv()
            rc[w,dz,1].wait_recv()
            fwd(w,dz,8,p["rd"],mate)
    def from_mate(w):
        cores[w].wait_recv()
        for dz in (1,2,3):
            for kind,quarter in ((3,r),(4,p["rx"]),(5,p["ry"]),(8,p["rd"])):
                ref=piece(w,dz,quarter)
                rcopy(ref,ref,ss.at[w,kind,dz-1],rs.at[w,kind,dz-1],mate).wait_recv()
    send(0)
    for cp in vcs: cp.wait_recv()
    vp[...]=v_ref[...]+vz[0]+vz[1]+vz[2]
    vc=go(rcopy(vp,vm,vs.at[3],vr.at[3],mate))
    vc.wait_recv()
    vf[...]=vp[...]+vm[...]
    R=256
    gain=vf[0:1,:]; shift=vf[1:2,:]
    def norm(i,t):
        rows=pl.ds(pl.multiple_of(i*R,R),R)
        u,_=ln_unit(tok_ref[rows,:].astype(F32))
        nrm[rows,:]=(u*gain+shift).astype(BF)
        return t
    stage_z(0); send(1)
    lax.fori_loop(0,T//R,norm,0)
    local_copy(nrm,nf)
    cs[...]=jnp.zeros_like(cs)
    stage_xy(0); stage_z(1); send(2)
    stage_r(0)
    from_mate(0)
    locs[0].wait()
    S=qf.shape[0]; B=qf.shape[1]
    loads=[pltpu.make_async_copy(qf.at[t],qv.at[pl.ds(t*B,B)],qsem.at[t]) for t in range(S)]
    for cp in loads: cp.start()
    for cp in loads: cp.wait()
    def project(i,t):
        rows=pl.ds(pl.multiple_of(i*R,R),R)
        prj[rows,:]=nt(nrm[rows,:],qv[...]).astype(BF)
        return t
    half=T//R//2
    lax.fori_loop(0,half,project,0)
    stage_xy(1)
    lax.fori_loop(half,T//R,project,0)
    local_copy(prj,pf)
    stage_z(2); send(3); stage_r(1)
    def block(i,n):
        row0=i*BQ if isinstance(i,int) else pl.multiple_of(i*BQ,BQ)
        rows=pl.ds(row0,BQ)
        def put_out(off,val):
            attv[rows,pl.ds(off,128)]=val
        def put_aux(val):
            lsev[rows,:]=val
        fwd_block(row0,n,BQ,G,HP,unroll,prj,segc,segr,nst,biasv.at[i],sigv.at[i],cs,put_out,put_aux)
    def run(i,t):
        block(i,NW)
        return t
    NB=T//BQ
    first=min(NW-1,NB)
    events=[lambda: stage_xy(2), lambda: None, lambda: (stage_z(3),stage_r(2)), lambda: None]
    for i in range(first):
        block(i,i+1)
        events[i]()
    mid=(first+NB)//2
    lax.fori_loop(first,mid,run,0)
    stage_xy(3)
    lax.fori_loop(mid,NB,run,0)
    local_copy(attv,af); local_copy(lsev,lf); local_copy(biasv,bf_); local_copy(sigv,sf)
    stage_r(3)
    for w in (1,2,3): from_mate(w)
    for cp in done: cp.wait_send()
    for cp in locs[1:]: cp.wait()
    for cp in outs: cp.wait()

def forward_all(q,o,u,d,v,tok,segc,segr,nst,BQ=128,G=128,unroll=6):
    S=8
    T,D=tok.shape; NW=windows(T,BQ,G); NB=T//BQ
    any_=pl.BlockSpec(memory_space=pl.ANY); vm_=pl.BlockSpec(memory_space=pltpu.VMEM)
    full=lambda a: jax.ShapeDtypeStruct((S,)+a.shape,a.dtype)
    sd=jax.ShapeDtypeStruct
    dma=pltpu.SemaphoreType.DMA
    V=pltpu.VMEM
    E=S*q.shape[0]
    outs=pl.pallas_call(functools.partial(forward_kernel,BQ,G,NW,D//128,unroll),in_specs=[any_]*4+[vm_]*5,out_specs=[any_]*4+[vm_]+[any_]*6,
      out_shape=[full(o),full(u),full(d),full(q),sd(v.shape,F32),sd((T,D),BF),sd((T,E),BF),sd((T,D),BF),sd((T,128),F32),sd((NB,BQ,NW*G),F32),sd((NB,BQ,NW*G),BF)],
      scratch_shapes=[V((E,D),BF),V((T,D),BF),V((T,E),BF),V((T,D),BF),V((T,128),F32),V((NB,BQ,NW*G),F32),V((NB,BQ,NW*G),BF),V((1,T),F32),
        V((3,)+v.shape,F32),V(v.shape,F32),V(v.shape,F32),
        dma((4,)),dma((8,)),dma((8,)),dma((4,)),dma((4,)),dma((4,9,3)),dma((4,9,3)),dma((4,)),dma((4,))],
      compiler_params=pltpu.CompilerParams(collective_id=1,has_side_effects=True,vmem_limit_bytes=56<<20),name="forward_all")(q,o,u,d,v,tok,segc,segr,nst)
    return [a.reshape(-1,D) for a in outs[:4]]+list(outs[4:])


def gather(x):
    return lax.all_gather(x, "shard", axis=0, tiled=True)


def forward_plain(q, o, u, d, v, tok, segc, segr, nst, nblk):
    q, o, u, d = gather(q), gather(o), gather(u), gather(d)
    vec = lax.psum(v, "shard")
    normed, projected = qkv_proj(tok, q, vec)
    return [o, u, d, q, vec, normed, projected] + list(attn_fwd(projected, segc, segr, nst, nblk))


def reduce_plain(gs, v):
    def one(g):
        part = lax.psum_scatter(g, "shard", scatter_dimension=0, tiled=True)
        return lax.psum(part, "rep")

    return [one(g) for g in gs], lax.psum(v, ("rep", "shard"))


def local(tokens, segment_ids, qkv_weight, out_weight, up_weight, down_weight,
          norm1_gain, norm1_shift, norm2_gain, norm2_shift, cotangent):
    tok = tokens[0]
    cot = cotangent[0]
    seg = segment_ids[0]
    model = tok.shape[1]
    known = lax.axis_size("rep") == 4 and lax.axis_size("shard") == 8
    piece = norm1_gain.shape[0]
    at = lax.axis_index("shard") * piece
    vec_part = jnp.stack([norm1_gain, norm1_shift, norm2_gain, norm2_shift]).astype(F32)
    vec_mine = lax.dynamic_update_slice(jnp.zeros((8, model), F32), vec_part, (0, at))
    segc, segr, nst, nblk = prep(seg)
    parts = (qkv_weight.T, out_weight, up_weight.T, down_weight, vec_mine, tok, segc, segr, nst)
    held = forward_all(*parts) if known else forward_plain(*parts, nblk)
    out_full, up_t, down_full, qkv_t, vec, normed, projected, attended, lse, bias, sig = held
    output, gres, gatt, gdn, gup, gow, vec2 = mlp(tok, attended, cot, out_full, up_t, down_full, vec)
    gproj = attn_bwd(projected, gatt, attended, lse, bias, sig, nblk)
    gqkv = qkv_wgrad(gproj, normed)
    tgrad, vec1 = qkv_dgrad(gproj, qkv_t, tok, gres, vec)
    vec_all = jnp.concatenate([vec1[:2], vec2[:2], jnp.zeros((4, model), F32)], axis=0)
    spread = reduce_all if known else reduce_plain
    grads, vec_sum = spread([gdn, gup, gow, gqkv], vec_all)
    down_grad, up_grad, out_grad, qkv_grad = [g.astype(F32) for g in grads]
    mine = lax.dynamic_slice_in_dim(vec_sum, at, piece, 1)
    return (output[None], tgrad[None], qkv_grad.T, out_grad, up_grad.T, down_grad,
            mine[0], mine[1], mine[2], mine[3])


def solution(mesh):
    seq = P(("rep", "shard"), None, None)
    cols, rows, vecs = P(None, "shard"), P("shard", None), P("shard")
    return jax.shard_map(
        local,
        mesh=mesh,
        in_specs=(seq, P(("rep", "shard"), None), cols, rows, cols, rows, vecs, vecs, vecs, vecs, seq),
        out_specs=(seq, seq, cols, rows, cols, rows, vecs, vecs, vecs, vecs),
        check_vma=False,
    )
```

```python
import functools

import jax
import jax.numpy as jnp
from jax import lax
from jax.experimental import pallas as pl
from jax.experimental.pallas import tpu as pltpu
from jax.sharding import PartitionSpec as P

F32 = jnp.float32
BF = jnp.bfloat16
NEG=-1e30
WIN=512
def nt(a,b):
    return lax.dot_general(a,b,(((1,),(1,)),((),())),preferred_element_type=F32)
def nn(a,b):
    return lax.dot_general(a,b,(((1,),(0,)),((),())),preferred_element_type=F32)
def tn(a,b):
    return lax.dot_general(a,b,(((0,),(0,)),((),())),preferred_element_type=F32)
def split2(x):
    hi=x.astype(BF)
    lo=(x-hi.astype(F32)).astype(BF)
    return hi,lo
def eighth(x):
    return x*jnp.asarray(0.125,BF)

def fwd_block(row0,n,BQ,G,HP,unroll,qkv,segc,segr,nst,bias,sig,cs,put_out,put_aux):
    D=HP*128
    W=n*G
    k0=row0+BQ-W
    if not isinstance(k0,int): k0=pl.multiple_of(k0,G)
    kw=pl.ds(k0,W); rows=pl.ds(row0,BQ)
    lane=lax.broadcasted_iota(jnp.int32,(BQ,128),1)
    left=lane<64
    same=segc[rows,:]==segr[:,kw]
    qi=lax.broadcasted_iota(jnp.int32,(BQ,W),0)+(W-BQ)
    ki=lax.broadcasted_iota(jnp.int32,(BQ,W),1)
    allowed=same&(ki<=qi)
    chosen=same&(ki<qi)&(nst[:,kw]>0)
    q=eighth(qkv[rows,pl.ds(0,128)])
    k=qkv[kw,pl.ds(D,128)]
    s0=nt(jnp.where(left,q,jnp.zeros_like(q)),k)
    e=jnp.exp(-jnp.abs(s0))
    sp=jnp.maximum(s0,0.0)+jnp.log1p(e)
    sg=jnp.where(s0>=0,1.0,e)/(1.0+e)
    sel=jnp.where(chosen,sp,0.0)
    sig[:,sig.shape[1]-W:]=jnp.where(chosen,sg,0.0).astype(BF)
    hi,lo=split2(sel)
    ri=lax.broadcasted_iota(jnp.int32,(BQ,BQ),0); ci=lax.broadcasted_iota(jnp.int32,(BQ,BQ),1)
    L=(ri>ci).astype(BF)
    pen=nn(L,hi)+nn(L,lo)+cs[:,kw]
    cs[:,kw]=cs[:,kw]+jnp.sum(sel,axis=0,keepdims=True)
    bias[:,bias.shape[1]-W:]=jnp.where(allowed,-pen,NEG)
    ones=jnp.ones((W,128),BF)
    def pair(j,acc):
        off=pl.multiple_of(j*128,128)
        q=eighth(qkv[rows,pl.ds(off,128)])
        z=jnp.zeros_like(q)
        k=qkv[kw,pl.ds(D+off,128)]
        v1=jnp.concatenate([qkv[kw,pl.ds(2*D+off,128)],ones],axis=1)
        b=bias[:,bias.shape[1]-W:]
        outs=[]
        for hh in range(2):
            qm=jnp.where(left,q,z) if hh==0 else jnp.where(left,z,q)
            s=nt(qm,k)+b
            m=jnp.max(s,axis=1,keepdims=True)
            p=jnp.exp(s-m)
            ol=nn(p.astype(BF),v1)
            l=ol[:,128:]
            outs.append(ol[:,:128]*(1.0/l))
            acc=jnp.where(lane==2*j+hh,m+jnp.log(l),acc)
        put_out(off,jnp.where(left,outs[0],outs[1]).astype(BF))
        return acc
    lse=lax.fori_loop(0,HP,pair,jnp.zeros((BQ,128),F32),unroll=unroll)
    put_aux(lse)

def attn_fwd_kernel(BQ,G,NW,HP,unroll,nblk_ref,qkv_ref,segc_ref,segr_ref,nst_ref,o_ref,aux_ref,bias_ref,sig_ref,cs_ref):
    i=pl.program_id(0)
    @pl.when(i==0)
    def _():
        cs_ref[...]=jnp.zeros_like(cs_ref)
    row0=pl.multiple_of(i*BQ,BQ)
    def put_out(off,val):
        o_ref[:,pl.ds(off,128)]=val
    def put_aux(val):
        aux_ref[...]=val
    for n in range(1,NW+1):
        @pl.when(nblk_ref[i]==n)
        def _(n=n):
            fwd_block(row0,n,BQ,G,HP,unroll,qkv_ref,segc_ref,segr_ref,nst_ref,bias_ref.at[0],sig_ref.at[0],cs_ref,put_out,put_aux)

def windows(T,BQ,G):
    return min(T//G,-(-(WIN-1+BQ)//G))

def attn_fwd(qkv,segc,segr,nst,nblk,BQ=128,G=128,unroll=6):
    T,D3=qkv.shape; D=D3//3; HP=D//128
    NW=windows(T,BQ,G)
    NB=T//BQ
    whole=lambda shape: pl.BlockSpec(shape,lambda i,*_:(0,0),pipeline_mode=pl.Buffered(1))
    gs=pltpu.PrefetchScalarGridSpec(num_scalar_prefetch=1,grid=(NB,),
      in_specs=[whole((T,D3)),whole((T,1)),whole((1,T)),whole((1,T))],
      out_specs=[pl.BlockSpec((BQ,D),lambda i,*_:(i,0)),pl.BlockSpec((BQ,128),lambda i,*_:(i,0)),
        pl.BlockSpec((1,BQ,NW*G),lambda i,*_:(i,0,0)),pl.BlockSpec((1,BQ,NW*G),lambda i,*_:(i,0,0))],
      scratch_shapes=[pltpu.VMEM((1,T),F32)])
    return pl.pallas_call(functools.partial(attn_fwd_kernel,BQ,G,NW,HP,unroll),grid_spec=gs,
      out_shape=[jax.ShapeDtypeStruct((T,D),BF),jax.ShapeDtypeStruct((T,128),F32),
        jax.ShapeDtypeStruct((NB,BQ,NW*G),F32),jax.ShapeDtypeStruct((NB,BQ,NW*G),BF)],
      compiler_params=pltpu.CompilerParams(vmem_limit_bytes=40<<20),name="attn_fwd")(nblk,qkv,segc,segr,nst)

def bwd_block(row0,n,BQ,G,HP,unroll,qkv,do_ref,o_ref,aux_ref,bias,sig,dq_ref,dk_ref,dv_ref,gp_ref,ls_ref):
    D=HP*128
    W=n*G
    k0=row0+BQ-W
    if not isinstance(k0,int): k0=pl.multiple_of(k0,G)
    kw=pl.ds(k0,W); rows=pl.ds(row0,BQ)
    lane=lax.broadcasted_iota(jnp.int32,(BQ,128),1)
    left=lane<64
    gp_ref[:,:W]=jnp.zeros((BQ,W),F32)
    lse=aux_ref[...]
    def stack(t):
        z=jnp.zeros_like(t)
        return jnp.concatenate([jnp.where(left,t,z),jnp.where(left,z,t)],axis=0)
    def work(j,first):
        off=j*128 if isinstance(j,int) else pl.multiple_of(j*128,128)
        k=qkv[kw,pl.ds(D+off,128)]
        v=qkv[kw,pl.ds(2*D+off,128)]
        do=do_ref[:,pl.ds(off,128)]
        prod=do.astype(F32)*o_ref[:,pl.ds(off,128)].astype(F32)
        b=bias[:,bias.shape[1]-W:]
        q2=stack(eighth(qkv[rows,pl.ds(off,128)]))
        do2=stack(do)
        def row(t0,t1):
            return jnp.sum(t0,axis=1,keepdims=True),jnp.sum(t1,axis=1,keepdims=True)
        l0,l1=row(jnp.where(lane==2*j,lse,0.0),jnp.where(lane==2*j+1,lse,0.0))
        e0,e1=row(jnp.where(left,prod,0.0),jnp.where(left,0.0,prod))
        s2=nt(q2,k)
        dp2=nt(do2,v)
        p0=jnp.exp(s2[:BQ]+b-l0); p1=jnp.exp(s2[BQ:]+b-l1)
        ds0=p0*(dp2[:BQ]-e0); ds1=p1*(dp2[BQ:]-e1)
        if not first:
            gp_ref[:,:W]=gp_ref[:,:W]+(ds0+ds1)
        else:
            gp=gp_ref[:,:W]+(ds0+ds1)
            hi,lo=split2(gp)
            ri=lax.broadcasted_iota(jnp.int32,(BQ,BQ),0); ci=lax.broadcasted_iota(jnp.int32,(BQ,BQ),1)
            U=(ci>ri).astype(BF)
            gsel=nn(U,hi)+nn(U,lo)+ls_ref[:,kw]
            ls_ref[:,kw]=ls_ref[:,kw]+jnp.sum(gp,axis=0,keepdims=True)
            ds0=ds0-gsel*sig[:,sig.shape[1]-W:].astype(F32)
        dsb=jnp.concatenate([ds0.astype(BF),ds1.astype(BF)],axis=0)
        pb=jnp.concatenate([p0.astype(BF),p1.astype(BF)],axis=0)
        dq2=nn(dsb,k)
        dq_ref[rows,pl.ds(off,128)]=(jnp.where(left,dq2[:BQ],dq2[BQ:])*0.125).astype(BF)
        dk_ref[kw,pl.ds(off,128)]+=tn(dsb,q2)
        dv_ref[kw,pl.ds(off,128)]+=tn(pb,do2)
    def body(j,c):
        work(j,False)
        return c
    lax.fori_loop(1,HP,body,0,unroll=unroll)
    work(0,True)

def attn_bwd_kernel(BQ,G,NW,HP,unroll,NB,nblk_ref,qkv_ref,do_ref,o_ref,aux_ref,bias_ref,sig_ref,out_ref,dk_ref,dv_ref,gp_ref,ls_ref):
    step=pl.program_id(0)
    i=NB-1-step
    D=HP*128
    @pl.when(step==0)
    def _():
        dk_ref[...]=jnp.zeros_like(dk_ref)
        dv_ref[...]=jnp.zeros_like(dv_ref)
        ls_ref[...]=jnp.zeros_like(ls_ref)
    row0=pl.multiple_of(i*BQ,BQ)
    for n in range(1,NW+1):
        @pl.when(nblk_ref[i]==n)
        def _(n=n):
            bwd_block(row0,n,BQ,G,HP,unroll,qkv_ref,do_ref,o_ref,aux_ref,bias_ref.at[0],sig_ref.at[0],out_ref,dk_ref,dv_ref,gp_ref,ls_ref)
    @pl.when(step==NB-1)
    def _():
        out_ref[:,D:2*D]=dk_ref[...].astype(BF)
        out_ref[:,2*D:]=dv_ref[...].astype(BF)

def attn_bwd(qkv,do,o,aux,bias,sig,nblk,BQ=128,G=128,unroll=5):
    T,D3=qkv.shape; D=D3//3; HP=D//128
    NW=bias.shape[2]//G
    NB=T//BQ
    whole=lambda shape: pl.BlockSpec(shape,lambda i,*_:(0,0),pipeline_mode=pl.Buffered(1))
    rb=lambda w: pl.BlockSpec((BQ,w),lambda i,*_:(NB-1-i,0))
    r3=pl.BlockSpec((1,BQ,NW*G),lambda i,*_:(NB-1-i,0,0))
    gs=pltpu.PrefetchScalarGridSpec(num_scalar_prefetch=1,grid=(NB,),
      in_specs=[whole((T,D3)),rb(D),rb(D),rb(128),r3,r3],
      out_specs=whole((T,D3)),
      scratch_shapes=[pltpu.VMEM((T,D),F32),pltpu.VMEM((T,D),F32),pltpu.VMEM((BQ,NW*G),F32),pltpu.VMEM((1,T),F32)])
    return pl.pallas_call(functools.partial(attn_bwd_kernel,BQ,G,NW,HP,unroll,NB),grid_spec=gs,
      out_shape=jax.ShapeDtypeStruct((T,D3),BF),
      compiler_params=pltpu.CompilerParams(vmem_limit_bytes=50<<20),name="attn_bwd")(nblk,qkv,do,o,aux,bias,sig)

def prep(seg,BQ=128,G=128):
    T=seg.shape[0]
    NB=T//BQ
    at=seg[::BQ]
    first=jnp.sum((seg[None,:]<at[:,None]).astype(jnp.int32),axis=1)
    ends=(jnp.arange(NB,dtype=jnp.int32)+1)*BQ
    nblk=(ends-(first//G)*G)//G
    starts=jnp.concatenate([jnp.ones((1,),bool),seg[1:]!=seg[:-1]])
    nst=jnp.logical_not(starts).astype(jnp.int32)[None,:]
    return seg[:,None],seg[None,:],nst,nblk

EPS=1e-5
GC=0.7978845608028654; GA=0.044715
def rowmean(x): return jnp.mean(x,axis=-1,keepdims=True)
def ln_unit(x):
    m=rowmean(x); c=x-m; v=rowmean(c*c); r=lax.rsqrt(v+EPS)
    return c*r, r

def qkv_kernel(tok_ref,w_ref,vec_ref,n_ref,o_ref):
    u,_=ln_unit(tok_ref[...].astype(F32))
    n=(u*vec_ref[0:1,:]+vec_ref[1:2,:]).astype(BF)
    n_ref[...]=n
    o_ref[...]=nt(n,w_ref[...]).astype(BF)
def qkv_proj(tok,wT,vec,R=256):
    T,D=tok.shape; E=wT.shape[0]
    c=lambda s: pl.BlockSpec(s,lambda i:(0,0),pipeline_mode=pl.Buffered(1))
    return pl.pallas_call(qkv_kernel,grid=(T//R,),in_specs=[pl.BlockSpec((R,D),lambda i:(i,0)),c((E,D)),c(vec.shape)],
      out_specs=[pl.BlockSpec((R,D),lambda i:(i,0)),pl.BlockSpec((R,E),lambda i:(i,0))],
      out_shape=[jax.ShapeDtypeStruct((T,D),BF),jax.ShapeDtypeStruct((T,E),BF)],
      compiler_params=pltpu.CompilerParams(vmem_limit_bytes=40<<20),name="qkv_proj")(tok,wT,vec)

def mlp_kernel(NC,C,tok_ref,att_ref,cot_ref,ow_ref,up_ref,dn_ref,vec_ref,
    out_ref,gres_ref,gatt_ref,act_ref,gh_ref,n2_ref,gb_ref,vg_ref):
    i=pl.program_id(0)
    gain=vec_ref[2:3,:]; shift=vec_ref[3:4,:]
    res=tok_ref[...].astype(F32)+nn(att_ref[...],ow_ref[...])
    u,rstd=ln_unit(res)
    n2=(u*gain+shift).astype(BF)
    n2_ref[...]=n2
    cot=cot_ref[...]
    out_acc=res
    g_acc=jnp.zeros_like(res)
    for c in range(NC):
        cs=slice(c*C,(c+1)*C)
        h=nt(n2,up_ref[cs,:])
        h2=h*h
        t=jnp.tanh(h*(GC+GC*GA*h2))
        half=0.5*(1.0+t)
        act=(h*half).astype(BF)
        act_ref[:,cs]=act
        ga=nt(cot,dn_ref[cs,:])
        dg=half+(0.5*h)*(1.0-t*t)*(GC+3.0*GC*GA*h2)
        gh=(ga*dg).astype(BF)
        gh_ref[:,cs]=gh
        out_acc=out_acc+nn(act,dn_ref[cs,:])
        g_acc=g_acc+nn(gh,up_ref[cs,:])
    out_ref[...]=out_acc.astype(BF)
    @pl.when(i==0)
    def _():
        vg_ref[...]=jnp.zeros_like(vg_ref)
    vg_ref[2:3,:]+=jnp.sum(g_acc*u,axis=0,keepdims=True)
    vg_ref[3:4,:]+=jnp.sum(g_acc,axis=0,keepdims=True)
    g=g_acc*gain
    gr=cot.astype(F32)+rstd*(g-rowmean(g)-u*rowmean(g*u))
    gres_ref[...]=gr
    gb=gr.astype(BF)
    gb_ref[...]=gb
    gatt_ref[...]=nt(gb,ow_ref[...]).astype(BF)
def mlp(tok,att,cot,ow,upT,dn,vec,R=256,C=768):
    T,D=tok.shape; F=upT.shape[0]
    c=lambda s: pl.BlockSpec(s,lambda i:(0,0),pipeline_mode=pl.Buffered(1))
    rb=lambda w: pl.BlockSpec((R,w),lambda i:(i,0))
    sd=jax.ShapeDtypeStruct
    return pl.pallas_call(functools.partial(mlp_kernel,F//C,C),grid=(T//R,),
      in_specs=[rb(D),rb(D),rb(D),c((D,D)),c((F,D)),c((F,D)),c(vec.shape)],
      out_specs=[rb(D),rb(D),rb(D),rb(F),rb(F),rb(D),rb(D),c((8,D))],
      out_shape=[sd((T,D),BF),sd((T,D),F32),sd((T,D),BF),sd((T,F),BF),sd((T,F),BF),sd((T,D),BF),sd((T,D),BF),sd((8,D),F32)],
      compiler_params=pltpu.CompilerParams(vmem_limit_bytes=56<<20),name="mlp")(tok,att,cot,ow,upT,dn,vec)

def wg_kernel(gp_ref,n_ref,o_ref):
    o_ref[...]=tn(gp_ref[...],n_ref[...]).astype(BF)
def weight_grad(gp,n1,WC=384):
    T,E=gp.shape; D=n1.shape[1]
    return pl.pallas_call(wg_kernel,grid=(E//WC,),in_specs=[pl.BlockSpec((T,WC),lambda i:(0,i)),pl.BlockSpec((T,D),lambda i:(0,0),pipeline_mode=pl.Buffered(1))],
      out_specs=pl.BlockSpec((WC,D),lambda i:(i,0)),out_shape=jax.ShapeDtypeStruct((E,D),BF),
      compiler_params=pltpu.CompilerParams(vmem_limit_bytes=40<<20),name="weight_grad")(gp,n1)
def dg_kernel(gp_ref,w_ref,tok_ref,gres_ref,vec_ref,o_ref,vg_ref):
    i=pl.program_id(0)
    gn=nn(gp_ref[...],w_ref[...])
    u,rstd=ln_unit(tok_ref[...].astype(F32))
    @pl.when(i==0)
    def _():
        vg_ref[...]=jnp.zeros_like(vg_ref)
    vg_ref[0:1,:]+=jnp.sum(gn*u,axis=0,keepdims=True)
    vg_ref[1:2,:]+=jnp.sum(gn,axis=0,keepdims=True)
    g=gn*vec_ref[0:1,:]
    o_ref[...]=(gres_ref[...]+rstd*(g-rowmean(g)-u*rowmean(g*u))).astype(BF)
def qkv_dgrad(gp,wT,tok,gres,vec,R=256):
    T,E=gp.shape; D=tok.shape[1]
    c=lambda s: pl.BlockSpec(s,lambda i:(0,0),pipeline_mode=pl.Buffered(1))
    rb=lambda w: pl.BlockSpec((R,w),lambda i:(i,0))
    return pl.pallas_call(dg_kernel,grid=(T//R,),in_specs=[rb(E),c((E,D)),rb(D),rb(D),c(vec.shape)],out_specs=[rb(D),c((8,D))],
      out_shape=[jax.ShapeDtypeStruct((T,D),BF),jax.ShapeDtypeStruct((8,D),F32)],
      compiler_params=pltpu.CompilerParams(vmem_limit_bytes=40<<20),name="qkv_dgrad")(gp,wT,tok,gres,vec)

MESH=pl.DeviceIdType.MESH

def place():
    r=lax.axis_index("rep"); s=lax.axis_index("shard")
    y=r//2; x=r%2; z=s//2; c=s%2
    return dict(r=r,s=s,y=y,x=x,z=z,c=c,rx=y*2+(1-x),ry=(1-y)*2+x,rd=(1-y)*2+(1-x),mate=z*2+(1-c))
def zpeer(p,dz):
    return (p["z"]+dz)%4
def greet(p):
    bar=pltpu.get_barrier_semaphore()
    for dev in ((p["r"],p["mate"]),(p["rx"],p["s"]),(p["ry"],p["s"]))+tuple((p["r"],zpeer(p,dz)*2+p["c"]) for dz in (1,2,3)):
        pl.semaphore_signal(bar,inc=1,device_id=dev,device_id_type=MESH)
    pl.semaphore_wait(bar,6)
def rcopy(src,dst,ss,rs,dev):
    return pltpu.make_async_remote_copy(src_ref=src,dst_ref=dst,send_sem=ss,recv_sem=rs,device_id=dev,device_id_type=MESH)


def forward_kernel(BQ,G,NW,HP,unroll,q_ref,o_ref,u_ref,d_ref,v_ref,tok_ref,segc,segr,nst,
    of,uf,df,qf,vf,nf,pf,af,lf,bf_,sf,
    qv,nrm,prj,attv,lsev,biasv,sigv,cs,vz,vp,vm,lsem,osem,qsem,c0s,c0r,ss,rs,vs,vr):
    p=place()
    greet(p)
    r,s,c,z=p["r"],p["s"],p["c"],p["z"]
    mate=(r,p["mate"]); xm=(p["rx"],s); ym=(p["ry"],s)
    sets=(q_ref,o_ref,u_ref,d_ref)
    fulls=(qf,of,uf,df)
    T,D=nrm.shape
    H=D//2
    done=[]; outs=[]
    def go(cp):
        cp.start(); done.append(cp); return cp
    def local_copy(src,dst):
        cp=pltpu.make_async_copy(src,dst,osem.at[len(outs)]); cp.start(); outs.append(cp)
    def view(w,shard,first,count,cols=None):
        rows=pl.ds(pl.multiple_of(first,8),count)
        return fulls[w].at[shard,rows] if cols is None else fulls[w].at[shard,rows,cols]
    locs=[]
    for w in range(4):
        cp=pltpu.make_async_copy(sets[w],view(w,s,0,sets[w].shape[0]),lsem.at[w]); cp.start(); locs.append(cp)
    vcs=[go(rcopy(v_ref,vz.at[dz-1],vs.at[dz-1],vr.at[dz-1],(r,zpeer(p,dz)*2+c))) for dz in (1,2,3)]
    def zsend(w):
        Q=sets[w].shape[0]//4
        rows=pl.ds(pl.multiple_of(r*Q,8),Q)
        return [go(rcopy(sets[w].at[rows],view(w,s,r*Q,Q),ss.at[w,0,dz-1],rs.at[w,0,dz-1],(r,zpeer(p,dz)*2+c))) for dz in (1,2,3)]
    def core0(w):
        return go(rcopy(sets[w],view(w,s,0,sets[w].shape[0]),c0s.at[w],c0r.at[w],mate))
    def piece(w,dz,quarter,cols=None):
        Q=sets[w].shape[0]//4
        return view(w,((z+4-dz)%4)*2+c,quarter*Q,Q,cols)
    def fwd(w,dz,kind,quarter,dev,cols=None):
        ref=piece(w,dz,quarter,cols)
        return go(rcopy(ref,ref,ss.at[w,kind,dz-1],rs.at[w,kind,dz-1],dev))
    zc={};xc={};yc={};rc={};cores={}
    def send(w):
        zc[w]=zsend(w); cores[w]=core0(w)
    def stage_z(w):
        for dz in (1,2,3):
            zc[w][dz-1].wait_recv()
            xc[w,dz]=fwd(w,dz,1,r,xm)
            yc[w,dz]=fwd(w,dz,2,r,ym)
            fwd(w,dz,3,r,mate)
    def stage_xy(w):
        for dz in (1,2,3):
            xc[w,dz].wait_recv()
            rc[w,dz,0]=fwd(w,dz,6,p["rx"],ym,pl.ds(H,H))
            fwd(w,dz,4,p["rx"],mate)
            yc[w,dz].wait_recv()
            rc[w,dz,1]=fwd(w,dz,7,p["ry"],xm,pl.ds(0,H))
            fwd(w,dz,5,p["ry"],mate)
    def stage_r(w):
        for dz in (1,2,3):
            rc[w,dz,0].wait_recv()
            rc[w,dz,1].wait_recv()
            fwd(w,dz,8,p["rd"],mate)
    def from_mate(w):
        cores[w].wait_recv()
        for dz in (1,2,3):
            for kind,quarter in ((3,r),(4,p["rx"]),(5,p["ry"]),(8,p["rd"])):
                ref=piece(w,dz,quarter)
                rcopy(ref,ref,ss.at[w,kind,dz-1],rs.at[w,kind,dz-1],mate).wait_recv()
    send(0)
    for cp in vcs: cp.wait_recv()
    vp[...]=v_ref[...]+vz[0]+vz[1]+vz[2]
    vc=go(rcopy(vp,vm,vs.at[3],vr.at[3],mate))
    vc.wait_recv()
    vf[...]=vp[...]+vm[...]
    R=256
    gain=vf[0:1,:]; shift=vf[1:2,:]
    def norm(i,t):
        rows=pl.ds(pl.multiple_of(i*R,R),R)
        u,_=ln_unit(tok_ref[rows,:].astype(F32))
        nrm[rows,:]=(u*gain+shift).astype(BF)
        return t
    stage_z(0); send(1)
    lax.fori_loop(0,T//R,norm,0)
    local_copy(nrm,nf)
    cs[...]=jnp.zeros_like(cs)
    stage_xy(0); stage_z(1); send(2)
    stage_r(0)
    from_mate(0)
    locs[0].wait()
    S=qf.shape[0]; B=qf.shape[1]
    loads=[pltpu.make_async_copy(qf.at[t],qv.at[pl.ds(t*B,B)],qsem.at[t]) for t in range(S)]
    for cp in loads: cp.start()
    for cp in loads: cp.wait()
    def project(i,t):
        rows=pl.ds(pl.multiple_of(i*R,R),R)
        prj[rows,:]=nt(nrm[rows,:],qv[...]).astype(BF)
        return t
    half=T//R//2
    lax.fori_loop(0,half,project,0)
    stage_xy(1)
    lax.fori_loop(half,T//R,project,0)
    local_copy(prj,pf)
    stage_z(2); send(3); stage_r(1)
    def block(i,n):
        row0=i*BQ if isinstance(i,int) else pl.multiple_of(i*BQ,BQ)
        rows=pl.ds(row0,BQ)
        def put_out(off,val):
            attv[rows,pl.ds(off,128)]=val
        def put_aux(val):
            lsev[rows,:]=val
        fwd_block(row0,n,BQ,G,HP,unroll,prj,segc,segr,nst,biasv.at[i],sigv.at[i],cs,put_out,put_aux)
    def run(i,t):
        block(i,NW)
        return t
    NB=T//BQ
    first=min(NW-1,NB)
    events=[lambda: stage_xy(2), lambda: None, lambda: (stage_z(3),stage_r(2)), lambda: None]
    for i in range(first):
        block(i,i+1)
        events[i]()
    mid=(first+NB)//2
    lax.fori_loop(first,mid,run,0)
    stage_xy(3)
    lax.fori_loop(mid,NB,run,0)
    local_copy(attv,af); local_copy(lsev,lf); local_copy(biasv,bf_); local_copy(sigv,sf)
    stage_r(3)
    for w in (1,2,3): from_mate(w)
    for cp in done: cp.wait_send()
    for cp in locs[1:]: cp.wait()
    for cp in outs: cp.wait()

def forward_all(q,o,u,d,v,tok,segc,segr,nst,BQ=128,G=128,unroll=6):
    S=8
    T,D=tok.shape; NW=windows(T,BQ,G); NB=T//BQ
    any_=pl.BlockSpec(memory_space=pl.ANY); vm_=pl.BlockSpec(memory_space=pltpu.VMEM)
    full=lambda a: jax.ShapeDtypeStruct((S,)+a.shape,a.dtype)
    sd=jax.ShapeDtypeStruct
    dma=pltpu.SemaphoreType.DMA
    V=pltpu.VMEM
    E=S*q.shape[0]
    outs=pl.pallas_call(functools.partial(forward_kernel,BQ,G,NW,D//128,unroll),in_specs=[any_]*4+[vm_]*5,out_specs=[any_]*4+[vm_]+[any_]*6,
      out_shape=[full(o),full(u),full(d),full(q),sd(v.shape,F32),sd((T,D),BF),sd((T,E),BF),sd((T,D),BF),sd((T,128),F32),sd((NB,BQ,NW*G),F32),sd((NB,BQ,NW*G),BF)],
      scratch_shapes=[V((E,D),BF),V((T,D),BF),V((T,E),BF),V((T,D),BF),V((T,128),F32),V((NB,BQ,NW*G),F32),V((NB,BQ,NW*G),BF),V((1,T),F32),
        V((3,)+v.shape,F32),V(v.shape,F32),V(v.shape,F32),
        dma((4,)),dma((8,)),dma((8,)),dma((4,)),dma((4,)),dma((4,9,3)),dma((4,9,3)),dma((4,)),dma((4,))],
      compiler_params=pltpu.CompilerParams(collective_id=1,has_side_effects=True,vmem_limit_bytes=56<<20),name="forward_all")(q,o,u,d,v,tok,segc,segr,nst)
    return [a.reshape(-1,D) for a in outs[:4]]+list(outs[4:])

def backward_kernel(BQ,G,NW,HP,unroll,NK,
    act_h,gh_h,n2_h,cot_h,gb_h,att_h,prj_h,gatt_h,lse_h,bias_h,sig_h,nrm_h,qw_h,tok_h,gres_h,vec_ref,vg_ref,
    od,ou,oo,oq,tg_h,vo,
    gd,gu,go_,gq,cd,cu,co,cq,a1d,a1u,a1o,a1q,b1d,b1u,b1o,b1q,a2d,a2u,a2o,a2q,b2d,b2u,b2o,b2q,zd,zu,zo,zq,fd,fu,fo,fq,
    chunk,n2,cot,gb,att,prj,gatt,lse,bias,sig,qw,dk,dv,gp,ls,vb,
    csem,isem,ss,rs,cs_,cr_,vs,vr,osem):
    p=place()
    greet(p)
    r,s,c,z,x,y=p["r"],p["s"],p["c"],p["z"],p["x"],p["y"]
    mate=(r,p["mate"]); xm=(p["rx"],s); ym=(p["ry"],s)
    zdev=[(r,zpeer(p,dz)*2+c) for dz in (1,2,3)]
    T,D=n2.shape; H=D//2
    g=(gd,gu,go_,gq); cb=(cd,cu,co,cq); a1=(a1d,a1u,a1o,a1q); b1=(b1d,b1u,b1o,b1q)
    a2=(a2d,a2u,a2o,a2q); b2=(b2d,b2u,b2o,b2q); zb=(zd,zu,zo,zq); fin=(fd,fu,fo,fq); outs=(od,ou,oo,oq)
    lo=pl.ds(0,H); hi=pl.ds(H,H)
    done=[]
    def go(cp):
        cp.start(); done.append(cp); return cp
    ins={}
    def load(name,src,dst):
        ins[name]=pltpu.make_async_copy(src,dst,isem.at[len(ins)]); ins[name].start()
    cp_={}
    loc={}
    def acc(k): return g[k].at[:,c]
    def C(k,zz):
        cp_[k,"c",zz]=go(rcopy(g[k].at[zz,1-c],cb[k].at[zz],cs_.at[k,zz],cr_.at[k,zz],mate))
    def X(k):
        a=acc(k)
        for zz in range(4): cp_[k,"c",zz].wait_recv()
        def add(i,t):
            a[i]=a[i]+cb[k][i]
            return t
        lax.fori_loop(0,4,add,0)
        for yy in range(2):
            cp_[k,1+yy]=go(rcopy(a.at[:,yy*2+1-x,:,lo],a1[k].at[:,yy],ss.at[k,1+yy],rs.at[k,1+yy],xm))
        cp_[k,3]=go(rcopy(a.at[:,pl.ds((1-y)*2,2),:,hi],b1[k],ss.at[k,3],rs.at[k,3],ym))
    def Y(k):
        a=acc(k)
        cp_[k,1].wait_recv(); cp_[k,2].wait_recv(); cp_[k,3].wait_recv()
        def add(i,t):
            for yy in range(2):
                a[i,yy*2+x,:,lo]=a[i,yy*2+x,:,lo]+a1[k][i,yy]
            for xx in range(2):
                a[i,y*2+xx,:,hi]=a[i,y*2+xx,:,hi]+b1[k][i,xx]
            return t
        lax.fori_loop(0,4,add,0)
        cp_[k,4]=go(rcopy(a.at[:,(1-y)*2+x,:,lo],a2[k],ss.at[k,4],rs.at[k,4],ym))
        cp_[k,5]=go(rcopy(a.at[:,y*2+1-x,:,hi],b2[k],ss.at[k,5],rs.at[k,5],xm))
    def Z(k):
        a=acc(k)
        cp_[k,4].wait_recv(); cp_[k,5].wait_recv()
        def add(i,t):
            a[i,r,:,lo]=a[i,r,:,lo]+a2[k][i]
            a[i,r,:,hi]=a[i,r,:,hi]+b2[k][i]
            return t
        lax.fori_loop(0,4,add,0)
        for dz in (1,2,3):
            cp_[k,5+dz]=go(rcopy(a.at[zpeer(p,dz),r],zb[k].at[dz-1],ss.at[k,5+dz],rs.at[k,5+dz],zdev[dz-1]))
    def Fn(k):
        for dz in (1,2,3): cp_[k,5+dz].wait_recv()
        t=acc(k)[z,r].astype(F32)
        for dz in range(3): t=t+zb[k][dz].astype(F32)
        fin[k][r]=t.astype(BF)
        cp_[k,9]=go(rcopy(fin[k].at[r],fin[k].at[r],ss.at[k,9],rs.at[k,9],xm))
        cp_[k,10]=go(rcopy(fin[k].at[r],fin[k].at[r],ss.at[k,10],rs.at[k,10],ym))
    def Gn(k):
        cp_[k,9].wait_recv()
        cp_[k,11]=go(rcopy(fin[k].at[p["rx"],:,hi],fin[k].at[p["rx"],:,hi],ss.at[k,11],rs.at[k,11],ym))
        cp_[k,10].wait_recv()
        cp_[k,12]=go(rcopy(fin[k].at[p["ry"],:,lo],fin[k].at[p["ry"],:,lo],ss.at[k,12],rs.at[k,12],xm))
    def Hn(k):
        cp_[k,11].wait_recv(); cp_[k,12].wait_recv()
        loc[k]=pltpu.make_async_copy(fin[k],outs[k],osem.at[k]); loc[k].start()
    zz0=(z//2)*2
    vdev=[mate,xm,ym,(r,(zz0+1-z%2)*2+c),(r,((z+2)%4)*2+c)]
    def V(n):
        if n>0:
            cp_["v",n-1].wait_recv()
            vb[2*n]=vb[2*n-2]+vb[2*n-1]
        if n<5:
            cp_["v",n]=go(rcopy(vb.at[2*n],vb.at[2*n+1],vs.at[n],vr.at[n],vdev[n]))
        else:
            vo[...]=vb[10]
    load("cot",cot_h,cot)
    WC=chunk.shape[2]
    order=[(w,half,zz) for w in range(2) for half in range(2) for zz in range(4)]
    def fetch(n):
        w,half,zz=order[n]
        cc=(1-c) if half==0 else c
        src=(act_h,gh_h)[w].at[:,pl.ds(pl.multiple_of((zz*2+cc)*WC,128),WC)]
        return pltpu.make_async_copy(src,chunk.at[n%2],csem.at[n%2])
    fetch(0).start()
    fetch(1).start()
    load("n2",n2_h,n2); load("gb",gb_h,gb); load("att",att_h,att); load("prj",prj_h,prj); load("gatt",gatt_h,gatt)
    load("lse",lse_h,lse); load("bias",bias_h,bias); load("sig",sig_h,sig); load("qw",qw_h,qw)
    ins["cot"].wait()
    for n,(w,half,zz) in enumerate(order):
        fetch(n).wait()
        if n==8: ins["n2"].wait()
        cc=(1-c) if half==0 else c
        res=tn(chunk[n%2],(cot,n2)[w][...])
        q4=WC//4
        for k in range(4):
            g[w][zz,cc,k]=res[k*q4:(k+1)*q4].astype(BF)
        if n+2<len(order): fetch(n+2).start()
        if half==0: C(w,zz)
        if n==7: X(0)
    X(1)
    ins["gb"].wait(); ins["att"].wait()
    res=tn(att[...],gb[...])
    q4=D//32
    for sh in range(8):
        for k in range(4):
            at=sh*(D//8)+k*q4
            go_[sh//2,sh%2,k]=res[at:at+q4].astype(BF)
    for zz in range(4): C(2,zz)
    for name in ("prj","gatt","lse","bias","sig"): ins[name].wait()
    load("nrm",nrm_h,n2); load("tok",tok_h,cot)
    dk[...]=jnp.zeros_like(dk)
    dv[...]=jnp.zeros_like(dv)
    ls[...]=jnp.zeros_like(ls)
    X(2)
    def block(i,n):
        row0=i*BQ if isinstance(i,int) else pl.multiple_of(i*BQ,BQ)
        rows=pl.ds(row0,BQ)
        bwd_block(row0,n,BQ,G,HP,unroll,prj,gatt.at[rows],att.at[rows],lse.at[rows],bias.at[i],sig.at[i],prj,dk,dv,gp,ls)
    NB=T//BQ
    first=min(NW-1,NB)
    def run(t,u):
        block(NB-1-t,NW)
        return u
    mid=(NB-first)//2
    lax.fori_loop(0,mid,run,0)
    Y(0)
    lax.fori_loop(mid,NB-first,run,0)
    Y(1)
    events=[lambda: Y(2), lambda: None, lambda: None, lambda: Z(0)]
    for t,i in enumerate(range(first-1,-1,-1)):
        block(i,i+1)
        events[t]()
    prj[:,D:2*D]=dk[...].astype(BF)
    prj[:,2*D:]=dv[...].astype(BF)
    load("gres",gres_h,dk)
    ins["nrm"].wait()
    E2=prj.shape[1]//2; q4=gq.shape[3]
    for part in range(2):
        for h in range(2):
            res=tn(prj[:,part*E2:(part+1)*E2],n2[:,h*H:(h+1)*H])
            for blk in range(E2//q4):
                sh=part*4+blk//4
                gq[sh//2,sh%2,blk%4,:,h*H:(h+1)*H]=res[blk*q4:(blk+1)*q4].astype(BF)
        for zz in (part*2,part*2+1): C(3,zz)
        if part==0: Z(1)
    Z(2)
    X(3)
    ins["tok"].wait(); ins["qw"].wait(); ins["gres"].wait()
    vb[0]=vg_ref[...]
    R=256
    gain=vec_ref[0:1,:]
    def dgrad(i,t):
        rows=pl.ds(pl.multiple_of(i*R,R),R)
        gn=nn(prj[rows,:],qw[...])
        u,rstd=ln_unit(cot[rows,:].astype(F32))
        vb[0,0:1,:]=vb[0,0:1,:]+jnp.sum(gn*u,axis=0,keepdims=True)
        vb[0,1:2,:]=vb[0,1:2,:]+jnp.sum(gn,axis=0,keepdims=True)
        gg=gn*gain
        gb[rows,:]=(dk[rows,:]+rstd*(gg-rowmean(gg)-u*rowmean(gg*u))).astype(BF)
        return t
    lax.fori_loop(0,T//R//2,dgrad,0)
    Fn(0)
    lax.fori_loop(T//R//2,T//R,dgrad,0)
    out_cp=pltpu.make_async_copy(gb,tg_h,osem.at[4]); out_cp.start()
    V(0)
    Fn(1); Y(3); V(1); Fn(2); Gn(0); V(2); Gn(1); Gn(2); V(3); Z(3); Hn(0); Hn(1); Hn(2); V(4)
    Fn(3); V(5); Gn(3); Hn(3)
    for cp in done: cp.wait_send()
    for k in range(4): loc[k].wait()
    out_cp.wait()

def backward_all(act,gh,n2,cot,gb,att,prj,gatt,lse,bias,sig,nrm,qw,tok,gres,vec,vg,BQ=128,G=128,unroll=5):
    T,D=tok.shape; F=act.shape[1]; E=prj.shape[1]; NB=T//BQ; NW=bias.shape[2]//G
    any_=pl.BlockSpec(memory_space=pl.ANY); vm_=pl.BlockSpec(memory_space=pltpu.VMEM)
    dma=pltpu.SemaphoreType.DMA; V=pltpu.VMEM; sd=jax.ShapeDtypeStruct
    Qs=[F//32,F//32,D//32,E//32]; H=D//2
    scr=[V((4,2,4,q,D),BF) for q in Qs]+[V((4,4,q,D),BF) for q in Qs]+[V((4,2,q,H),BF) for q in Qs]+[V((4,2,q,H),BF) for q in Qs]
    scr+=[V((4,q,H),BF) for q in Qs]+[V((4,q,H),BF) for q in Qs]+[V((3,q,D),BF) for q in Qs]+[V((4,q,D),BF) for q in Qs]
    scr+=[V((2,T,F//8),BF)]+[V((T,D),BF)]*4+[V((T,E),BF),V((T,D),BF),V((T,128),F32),V(bias.shape,F32),V(sig.shape,BF),V((E,D),BF)]
    scr+=[V((T,D),F32)]*2+[V((BQ,NW*G),F32),V((1,T),F32),V((11,8,D),F32)]
    scr+=[dma((2,)),dma((14,)),dma((4,13)),dma((4,13)),dma((4,4)),dma((4,4)),dma((5,)),dma((5,)),dma((5,))]
    outs=pl.pallas_call(functools.partial(backward_kernel,BQ,G,NW,D//128,unroll,0),in_specs=[any_]*15+[vm_]*2,out_specs=[any_]*5+[vm_],
      out_shape=[sd((4,q,D),BF) for q in Qs]+[sd((T,D),BF),sd((8,D),F32)],scratch_shapes=scr,
      compiler_params=pltpu.CompilerParams(collective_id=2,has_side_effects=True,vmem_limit_bytes=63<<20),name="backward_all")(act,gh,n2,cot,gb,att,prj,gatt,lse,bias,sig,nrm,qw,tok,gres,vec,vg)
    return [a.reshape(-1,D) for a in outs[:4]],outs[4],outs[5]


def gather(x):
    return lax.all_gather(x, "shard", axis=0, tiled=True)


def forward_plain(q, o, u, d, v, tok, segc, segr, nst, nblk):
    q, o, u, d = gather(q), gather(o), gather(u), gather(d)
    vec = lax.psum(v, "shard")
    normed, projected = qkv_proj(tok, q, vec)
    return [o, u, d, q, vec, normed, projected] + list(attn_fwd(projected, segc, segr, nst, nblk))


def backward_plain(act, gh, n2, cot, gb, att, prj, gatt, lse, bias, sig, nrm, qw, tok, gres, vec, vg, nblk):
    def one(g):
        part = lax.psum_scatter(g, "shard", scatter_dimension=0, tiled=True)
        return lax.psum(part, "rep")

    gproj = attn_bwd(prj, gatt, att, lse, bias, sig, nblk)
    tgrad, vec1 = qkv_dgrad(gproj, qw, tok, gres, vec)
    gs = [weight_grad(act, cot), weight_grad(gh, n2), weight_grad(att, gb), weight_grad(gproj, nrm)]
    total = jnp.concatenate([vec1[:2], vg[2:]], axis=0)
    return [one(g) for g in gs], tgrad, lax.psum(total, ("rep", "shard"))


def local(tokens, segment_ids, qkv_weight, out_weight, up_weight, down_weight,
          norm1_gain, norm1_shift, norm2_gain, norm2_shift, cotangent):
    tok = tokens[0]
    cot = cotangent[0]
    seg = segment_ids[0]
    model = tok.shape[1]
    known = lax.axis_size("rep") == 4 and lax.axis_size("shard") == 8
    piece = norm1_gain.shape[0]
    at = lax.axis_index("shard") * piece
    vec_part = jnp.stack([norm1_gain, norm1_shift, norm2_gain, norm2_shift]).astype(F32)
    vec_mine = lax.dynamic_update_slice(jnp.zeros((8, model), F32), vec_part, (0, at))
    segc, segr, nst, nblk = prep(seg)
    parts = (qkv_weight.T, out_weight, up_weight.T, down_weight, vec_mine, tok, segc, segr, nst)
    held = forward_all(*parts) if known else forward_plain(*parts, nblk)
    out_full, up_t, down_full, qkv_t, vec, normed, projected, attended, lse, bias, sig = held
    output, gres, gatt, act, gh, n2, gb, vg = mlp(tok, attended, cot, out_full, up_t, down_full, vec)
    parts = (act, gh, n2, cot, gb, attended, projected, gatt, lse, bias, sig, normed, qkv_t, tok, gres, vec, vg)
    grads, tgrad, vec_sum = backward_all(*parts) if known else backward_plain(*parts, nblk)
    down_grad, up_grad, out_grad, qkv_grad = [g.astype(F32) for g in grads]
    mine = lax.dynamic_slice_in_dim(vec_sum, at, piece, 1)
    return (output[None], tgrad[None], qkv_grad.T, out_grad, up_grad.T, down_grad,
            mine[0], mine[1], mine[2], mine[3])


def solution(mesh):
    seq = P(("rep", "shard"), None, None)
    cols, rows, vecs = P(None, "shard"), P("shard", None), P("shard")
    return jax.shard_map(
        local,
        mesh=mesh,
        in_specs=(seq, P(("rep", "shard"), None), cols, rows, cols, rows, vecs, vecs, vecs, vecs, seq),
        out_specs=(seq, seq, cols, rows, cols, rows, vecs, vecs, vecs, vecs),
        check_vma=False,
    )
```

```python
import functools

import jax
import jax.numpy as jnp
from jax import lax
from jax.experimental import pallas as pl
from jax.experimental.pallas import tpu as pltpu
from jax.sharding import PartitionSpec as P

F32 = jnp.float32
BF = jnp.bfloat16
NEG=-1e30
WIN=512
def nt(a,b):
    return lax.dot_general(a,b,(((1,),(1,)),((),())),preferred_element_type=F32)
def nn(a,b):
    return lax.dot_general(a,b,(((1,),(0,)),((),())),preferred_element_type=F32)
def tn(a,b):
    return lax.dot_general(a,b,(((0,),(0,)),((),())),preferred_element_type=F32)
def split2(x):
    hi=x.astype(BF)
    lo=(x-hi.astype(F32)).astype(BF)
    return hi,lo
def eighth(x):
    return x*jnp.asarray(0.125,BF)

def fwd_block(row0,n,BQ,G,HP,unroll,qkv,segr,nst,bias,sig,cs,put_out,put_aux):
    D=HP*128
    W=n*G
    k0=row0+BQ-W
    if not isinstance(k0,int): k0=pl.multiple_of(k0,G)
    kw=pl.ds(k0,W); rows=pl.ds(row0,BQ)
    lane=lax.broadcasted_iota(jnp.int32,(BQ,128),1)
    left=lane<64
    same=jnp.broadcast_to(segr[:,rows],(128,BQ)).T[:,:1]==segr[:,kw]
    qi=lax.broadcasted_iota(jnp.int32,(BQ,W),0)+(W-BQ)
    ki=lax.broadcasted_iota(jnp.int32,(BQ,W),1)
    allowed=same&(ki<=qi)
    chosen=same&(ki<qi)&(nst[:,kw]>0)
    q=eighth(qkv[rows,pl.ds(0,128)])
    k=qkv[kw,pl.ds(D,128)]
    s0=nt(jnp.where(left,q,jnp.zeros_like(q)),k)
    e=jnp.exp(-jnp.abs(s0))
    sp=jnp.maximum(s0,0.0)+jnp.log1p(e)
    sg=jnp.where(s0>=0,1.0,e)/(1.0+e)
    sel=jnp.where(chosen,sp,0.0)
    sig[:,sig.shape[1]-W:]=jnp.where(chosen,sg,0.0).astype(BF)
    hi,lo=split2(sel)
    ri=lax.broadcasted_iota(jnp.int32,(BQ,BQ),0); ci=lax.broadcasted_iota(jnp.int32,(BQ,BQ),1)
    L=(ri>ci).astype(BF)
    pen=nn(L,hi)+nn(L,lo)+cs[:,kw]
    cs[:,kw]=cs[:,kw]+jnp.sum(sel,axis=0,keepdims=True)
    bias[:,bias.shape[1]-W:]=jnp.where(allowed,-pen,NEG)
    ones=jnp.ones((W,128),BF)
    def pair(j,acc):
        off=pl.multiple_of(j*128,128)
        q=eighth(qkv[rows,pl.ds(off,128)])
        z=jnp.zeros_like(q)
        k=qkv[kw,pl.ds(D+off,128)]
        v1=jnp.concatenate([qkv[kw,pl.ds(2*D+off,128)],ones],axis=1)
        b=bias[:,bias.shape[1]-W:]
        outs=[]
        for hh in range(2):
            qm=jnp.where(left,q,z) if hh==0 else jnp.where(left,z,q)
            s=nt(qm,k)+b
            m=jnp.max(s,axis=1,keepdims=True)
            p=jnp.exp(s-m)
            ol=nn(p.astype(BF),v1)
            l=ol[:,128:]
            outs.append(ol[:,:128]*(1.0/l))
            acc=jnp.where(lane==2*j+hh,m+jnp.log(l),acc)
        put_out(off,jnp.where(left,outs[0],outs[1]).astype(BF))
        return acc
    lse=lax.fori_loop(0,HP,pair,jnp.zeros((BQ,128),F32),unroll=unroll)
    put_aux(lse)

def attn_fwd_kernel(BQ,G,NW,HP,unroll,nblk_ref,qkv_ref,segr_ref,nst_ref,o_ref,aux_ref,bias_ref,sig_ref,cs_ref):
    i=pl.program_id(0)
    @pl.when(i==0)
    def _():
        cs_ref[...]=jnp.zeros_like(cs_ref)
    row0=pl.multiple_of(i*BQ,BQ)
    def put_out(off,val):
        o_ref[:,pl.ds(off,128)]=val
    def put_aux(val):
        aux_ref[...]=val
    for n in range(1,NW+1):
        @pl.when(nblk_ref[i]==n)
        def _(n=n):
            fwd_block(row0,n,BQ,G,HP,unroll,qkv_ref,segr_ref,nst_ref,bias_ref.at[0],sig_ref.at[0],cs_ref,put_out,put_aux)

def windows(T,BQ,G):
    return min(T//G,-(-(WIN-1+BQ)//G))

def attn_fwd(qkv,segr,nst,nblk,BQ=128,G=128,unroll=6):
    T,D3=qkv.shape; D=D3//3; HP=D//128
    NW=windows(T,BQ,G)
    NB=T//BQ
    whole=lambda shape: pl.BlockSpec(shape,lambda i,*_:(0,0),pipeline_mode=pl.Buffered(1))
    gs=pltpu.PrefetchScalarGridSpec(num_scalar_prefetch=1,grid=(NB,),
      in_specs=[whole((T,D3)),whole((1,T)),whole((1,T))],
      out_specs=[pl.BlockSpec((BQ,D),lambda i,*_:(i,0)),pl.BlockSpec((BQ,128),lambda i,*_:(i,0)),
        pl.BlockSpec((1,BQ,NW*G),lambda i,*_:(i,0,0)),pl.BlockSpec((1,BQ,NW*G),lambda i,*_:(i,0,0))],
      scratch_shapes=[pltpu.VMEM((1,T),F32)])
    return pl.pallas_call(functools.partial(attn_fwd_kernel,BQ,G,NW,HP,unroll),grid_spec=gs,
      out_shape=[jax.ShapeDtypeStruct((T,D),BF),jax.ShapeDtypeStruct((T,128),F32),
        jax.ShapeDtypeStruct((NB,BQ,NW*G),F32),jax.ShapeDtypeStruct((NB,BQ,NW*G),BF)],
      compiler_params=pltpu.CompilerParams(vmem_limit_bytes=40<<20),name="attn_fwd")(nblk,qkv,segr,nst)

def bwd_block(row0,n,BQ,G,HP,unroll,qkv,do_ref,o_ref,aux_ref,bias,sig,dq_ref,dk_ref,dv_ref,gp_ref,ls_ref):
    D=HP*128
    W=n*G
    k0=row0+BQ-W
    if not isinstance(k0,int): k0=pl.multiple_of(k0,G)
    kw=pl.ds(k0,W); rows=pl.ds(row0,BQ)
    lane=lax.broadcasted_iota(jnp.int32,(BQ,128),1)
    left=lane<64
    gp_ref[:,:W]=jnp.zeros((BQ,W),F32)
    lse=aux_ref[...]
    def stack(t):
        z=jnp.zeros_like(t)
        return jnp.concatenate([jnp.where(left,t,z),jnp.where(left,z,t)],axis=0)
    def work(j,first):
        off=j*128 if isinstance(j,int) else pl.multiple_of(j*128,128)
        k=qkv[kw,pl.ds(D+off,128)]
        v=qkv[kw,pl.ds(2*D+off,128)]
        do=do_ref[:,pl.ds(off,128)]
        prod=do.astype(F32)*o_ref[:,pl.ds(off,128)].astype(F32)
        b=bias[:,bias.shape[1]-W:]
        q2=stack(eighth(qkv[rows,pl.ds(off,128)]))
        do2=stack(do)
        def row(t0,t1):
            return jnp.sum(t0,axis=1,keepdims=True),jnp.sum(t1,axis=1,keepdims=True)
        l0,l1=row(jnp.where(lane==2*j,lse,0.0),jnp.where(lane==2*j+1,lse,0.0))
        e0,e1=row(jnp.where(left,prod,0.0),jnp.where(left,0.0,prod))
        s2=nt(q2,k)
        dp2=nt(do2,v)
        p0=jnp.exp(s2[:BQ]+b-l0); p1=jnp.exp(s2[BQ:]+b-l1)
        ds0=p0*(dp2[:BQ]-e0); ds1=p1*(dp2[BQ:]-e1)
        if not first:
            gp_ref[:,:W]=gp_ref[:,:W]+(ds0+ds1)
        else:
            gp=gp_ref[:,:W]+(ds0+ds1)
            hi,lo=split2(gp)
            ri=lax.broadcasted_iota(jnp.int32,(BQ,BQ),0); ci=lax.broadcasted_iota(jnp.int32,(BQ,BQ),1)
            U=(ci>ri).astype(BF)
            gsel=nn(U,hi)+nn(U,lo)+ls_ref[:,kw]
            ls_ref[:,kw]=ls_ref[:,kw]+jnp.sum(gp,axis=0,keepdims=True)
            ds0=ds0-gsel*sig[:,sig.shape[1]-W:].astype(F32)
        dsb=jnp.concatenate([ds0.astype(BF),ds1.astype(BF)],axis=0)
        pb=jnp.concatenate([p0.astype(BF),p1.astype(BF)],axis=0)
        dq2=nn(dsb,k)
        dq_ref[rows,pl.ds(off,128)]=(jnp.where(left,dq2[:BQ],dq2[BQ:])*0.125).astype(BF)
        dk_ref[kw,pl.ds(off,128)]+=tn(dsb,q2)
        dv_ref[kw,pl.ds(off,128)]+=tn(pb,do2)
    def body(j,c):
        work(j,False)
        return c
    lax.fori_loop(1,HP,body,0,unroll=unroll)
    work(0,True)

def attn_bwd_kernel(BQ,G,NW,HP,unroll,NB,nblk_ref,qkv_ref,do_ref,o_ref,aux_ref,bias_ref,sig_ref,out_ref,dk_ref,dv_ref,gp_ref,ls_ref):
    step=pl.program_id(0)
    i=NB-1-step
    D=HP*128
    @pl.when(step==0)
    def _():
        dk_ref[...]=jnp.zeros_like(dk_ref)
        dv_ref[...]=jnp.zeros_like(dv_ref)
        ls_ref[...]=jnp.zeros_like(ls_ref)
    row0=pl.multiple_of(i*BQ,BQ)
    for n in range(1,NW+1):
        @pl.when(nblk_ref[i]==n)
        def _(n=n):
            bwd_block(row0,n,BQ,G,HP,unroll,qkv_ref,do_ref,o_ref,aux_ref,bias_ref.at[0],sig_ref.at[0],out_ref,dk_ref,dv_ref,gp_ref,ls_ref)
    @pl.when(step==NB-1)
    def _():
        out_ref[:,D:2*D]=dk_ref[...].astype(BF)
        out_ref[:,2*D:]=dv_ref[...].astype(BF)

def attn_bwd(qkv,do,o,aux,bias,sig,nblk,BQ=128,G=128,unroll=5):
    T,D3=qkv.shape; D=D3//3; HP=D//128
    NW=bias.shape[2]//G
    NB=T//BQ
    whole=lambda shape: pl.BlockSpec(shape,lambda i,*_:(0,0),pipeline_mode=pl.Buffered(1))
    rb=lambda w: pl.BlockSpec((BQ,w),lambda i,*_:(NB-1-i,0))
    r3=pl.BlockSpec((1,BQ,NW*G),lambda i,*_:(NB-1-i,0,0))
    gs=pltpu.PrefetchScalarGridSpec(num_scalar_prefetch=1,grid=(NB,),
      in_specs=[whole((T,D3)),rb(D),rb(D),rb(128),r3,r3],
      out_specs=whole((T,D3)),
      scratch_shapes=[pltpu.VMEM((T,D),F32),pltpu.VMEM((T,D),F32),pltpu.VMEM((BQ,NW*G),F32),pltpu.VMEM((1,T),F32)])
    return pl.pallas_call(functools.partial(attn_bwd_kernel,BQ,G,NW,HP,unroll,NB),grid_spec=gs,
      out_shape=jax.ShapeDtypeStruct((T,D3),BF),
      compiler_params=pltpu.CompilerParams(vmem_limit_bytes=50<<20),name="attn_bwd")(nblk,qkv,do,o,aux,bias,sig)

def prep(seg,BQ=128,G=128):
    T=seg.shape[0]
    NB=T//BQ
    at=seg[::BQ]
    first=jnp.sum((seg[None,:]<at[:,None]).astype(jnp.int32),axis=1)
    ends=(jnp.arange(NB,dtype=jnp.int32)+1)*BQ
    nblk=(ends-(first//G)*G)//G
    starts=jnp.concatenate([jnp.ones((1,),bool),seg[1:]!=seg[:-1]])
    nst=jnp.logical_not(starts).astype(jnp.int32)[None,:]
    return seg[None,:].astype(F32),nst,nblk

EPS=1e-5
GC=0.7978845608028654; GA=0.044715
def rowmean(x): return jnp.mean(x,axis=-1,keepdims=True)
def ln_unit(x):
    m=rowmean(x); c=x-m; v=rowmean(c*c); r=lax.rsqrt(v+EPS)
    return c*r, r

def qkv_kernel(tok_ref,w_ref,vec_ref,n_ref,o_ref):
    u,_=ln_unit(tok_ref[...].astype(F32))
    n=(u*vec_ref[0:1,:]+vec_ref[1:2,:]).astype(BF)
    n_ref[...]=n
    o_ref[...]=nt(n,w_ref[...]).astype(BF)
def qkv_proj(tok,wT,vec,R=256):
    T,D=tok.shape; E=wT.shape[0]
    c=lambda s: pl.BlockSpec(s,lambda i:(0,0),pipeline_mode=pl.Buffered(1))
    return pl.pallas_call(qkv_kernel,grid=(T//R,),in_specs=[pl.BlockSpec((R,D),lambda i:(i,0)),c((E,D)),c(vec.shape)],
      out_specs=[pl.BlockSpec((R,D),lambda i:(i,0)),pl.BlockSpec((R,E),lambda i:(i,0))],
      out_shape=[jax.ShapeDtypeStruct((T,D),BF),jax.ShapeDtypeStruct((T,E),BF)],
      compiler_params=pltpu.CompilerParams(vmem_limit_bytes=40<<20),name="qkv_proj")(tok,wT,vec)

def mlp_kernel(NC,C,tok_ref,att_ref,cot_ref,ow_ref,up_ref,dn_ref,vec_ref,
    out_ref,gres_ref,gatt_ref,act_ref,gh_ref,n2_ref,gb_ref,vg_ref):
    i=pl.program_id(0)
    gain=vec_ref[2:3,:]; shift=vec_ref[3:4,:]
    res=tok_ref[...].astype(F32)+nn(att_ref[...],ow_ref[...])
    u,rstd=ln_unit(res)
    n2=(u*gain+shift).astype(BF)
    n2_ref[...]=n2
    cot=cot_ref[...]
    out_acc=res
    g_acc=jnp.zeros_like(res)
    for c in range(NC):
        cs=slice(c*C,(c+1)*C)
        h=nt(n2,up_ref[cs,:])
        h2=h*h
        t=jnp.tanh(h*(GC+GC*GA*h2))
        half=0.5*(1.0+t)
        act=(h*half).astype(BF)
        act_ref[:,cs]=act
        ga=nt(cot,dn_ref[cs,:])
        dg=half+(0.5*h)*(1.0-t*t)*(GC+3.0*GC*GA*h2)
        gh=(ga*dg).astype(BF)
        gh_ref[:,cs]=gh
        out_acc=out_acc+nn(act,dn_ref[cs,:])
        g_acc=g_acc+nn(gh,up_ref[cs,:])
    out_ref[...]=out_acc.astype(BF)
    @pl.when(i==0)
    def _():
        vg_ref[...]=jnp.zeros_like(vg_ref)
    vg_ref[2:3,:]+=jnp.sum(g_acc*u,axis=0,keepdims=True)
    vg_ref[3:4,:]+=jnp.sum(g_acc,axis=0,keepdims=True)
    g=g_acc*gain
    gr=cot.astype(F32)+rstd*(g-rowmean(g)-u*rowmean(g*u))
    gres_ref[...]=gr
    gb=gr.astype(BF)
    gb_ref[...]=gb
    gatt_ref[...]=nt(gb,ow_ref[...]).astype(BF)
def mlp(tok,att,cot,ow,upT,dn,vec,R=256,C=768):
    T,D=tok.shape; F=upT.shape[0]
    c=lambda s: pl.BlockSpec(s,lambda i:(0,0),pipeline_mode=pl.Buffered(1))
    rb=lambda w: pl.BlockSpec((R,w),lambda i:(i,0))
    sd=jax.ShapeDtypeStruct
    return pl.pallas_call(functools.partial(mlp_kernel,F//C,C),grid=(T//R,),
      in_specs=[rb(D),rb(D),rb(D),c((D,D)),c((F,D)),c((F,D)),c(vec.shape)],
      out_specs=[rb(D),rb(D),rb(D),rb(F),rb(F),rb(D),rb(D),c((8,D))],
      out_shape=[sd((T,D),BF),sd((T,D),F32),sd((T,D),BF),sd((T,F),BF),sd((T,F),BF),sd((T,D),BF),sd((T,D),BF),sd((8,D),F32)],
      compiler_params=pltpu.CompilerParams(vmem_limit_bytes=56<<20),name="mlp")(tok,att,cot,ow,upT,dn,vec)

def wg_kernel(gp_ref,n_ref,o_ref):
    o_ref[...]=tn(gp_ref[...],n_ref[...]).astype(BF)
def weight_grad(gp,n1,WC=384):
    T,E=gp.shape; D=n1.shape[1]
    return pl.pallas_call(wg_kernel,grid=(E//WC,),in_specs=[pl.BlockSpec((T,WC),lambda i:(0,i)),pl.BlockSpec((T,D),lambda i:(0,0),pipeline_mode=pl.Buffered(1))],
      out_specs=pl.BlockSpec((WC,D),lambda i:(i,0)),out_shape=jax.ShapeDtypeStruct((E,D),BF),
      compiler_params=pltpu.CompilerParams(vmem_limit_bytes=40<<20),name="weight_grad")(gp,n1)
def dg_kernel(gp_ref,w_ref,tok_ref,gres_ref,vec_ref,o_ref,vg_ref):
    i=pl.program_id(0)
    gn=nn(gp_ref[...],w_ref[...])
    u,rstd=ln_unit(tok_ref[...].astype(F32))
    @pl.when(i==0)
    def _():
        vg_ref[...]=jnp.zeros_like(vg_ref)
    vg_ref[0:1,:]+=jnp.sum(gn*u,axis=0,keepdims=True)
    vg_ref[1:2,:]+=jnp.sum(gn,axis=0,keepdims=True)
    g=gn*vec_ref[0:1,:]
    o_ref[...]=(gres_ref[...]+rstd*(g-rowmean(g)-u*rowmean(g*u))).astype(BF)
def qkv_dgrad(gp,wT,tok,gres,vec,R=256):
    T,E=gp.shape; D=tok.shape[1]
    c=lambda s: pl.BlockSpec(s,lambda i:(0,0),pipeline_mode=pl.Buffered(1))
    rb=lambda w: pl.BlockSpec((R,w),lambda i:(i,0))
    return pl.pallas_call(dg_kernel,grid=(T//R,),in_specs=[rb(E),c((E,D)),rb(D),rb(D),c(vec.shape)],out_specs=[rb(D),c((8,D))],
      out_shape=[jax.ShapeDtypeStruct((T,D),BF),jax.ShapeDtypeStruct((8,D),F32)],
      compiler_params=pltpu.CompilerParams(vmem_limit_bytes=40<<20),name="qkv_dgrad")(gp,wT,tok,gres,vec)

MESH=pl.DeviceIdType.MESH

def place():
    r=lax.axis_index("rep"); s=lax.axis_index("shard")
    y=r//2; x=r%2; z=s//2; c=s%2
    return dict(r=r,s=s,y=y,x=x,z=z,c=c,rx=y*2+(1-x),ry=(1-y)*2+x,rd=(1-y)*2+(1-x),mate=z*2+(1-c))
def zpeer(p,dz):
    return (p["z"]+dz)%4
def greet(p):
    bar=pltpu.get_barrier_semaphore()
    for dev in ((p["r"],p["mate"]),(p["rx"],p["s"]),(p["ry"],p["s"]))+tuple((p["r"],zpeer(p,dz)*2+p["c"]) for dz in (1,2,3)):
        pl.semaphore_signal(bar,inc=1,device_id=dev,device_id_type=MESH)
    pl.semaphore_wait(bar,6)
def rcopy(src,dst,ss,rs,dev):
    return pltpu.make_async_remote_copy(src_ref=src,dst_ref=dst,send_sem=ss,recv_sem=rs,device_id=dev,device_id_type=MESH)


def forward_kernel(BQ,G,NW,HP,unroll,q_ref,o_ref,u_ref,d_ref,v_ref,tok_ref,segr,nst,
    of,uf,df,qf,vf,nf,pf,af,lf,bf_,sf,
    qv,nrm,prj,attv,lsev,biasv,sigv,cs,vz,vp,vm,h0,h1,h2,h3,lsem,wsem,osem,qsem,c0s,c0r,ss,rs,vs,vr):
    p=place()
    greet(p)
    r,s,c,z=p["r"],p["s"],p["c"],p["z"]
    mate=(r,p["mate"]); xm=(p["rx"],s); ym=(p["ry"],s)
    sets=(q_ref,o_ref,u_ref,d_ref)
    fulls=(qf,of,uf,df)
    held=(h0,h1,h2,h3)
    T,D=nrm.shape
    H=D//2
    done=[]; outs=[]
    def go(cp):
        cp.start(); done.append(cp); return cp
    def local_copy(src,dst):
        cp=pltpu.make_async_copy(src,dst,osem.at[len(outs)]); cp.start(); outs.append(cp)
    def view(w,shard,first,count,cols=None):
        rows=pl.ds(pl.multiple_of(first,8),count)
        return fulls[w].at[shard,rows] if cols is None else fulls[w].at[shard,rows,cols]
    locs=[]
    for w in range(4):
        cp=pltpu.make_async_copy(sets[w],held[w],lsem.at[w]); cp.start(); locs.append(cp)
    vcs=[go(rcopy(v_ref,vz.at[dz-1],vs.at[dz-1],vr.at[dz-1],(r,zpeer(p,dz)*2+c))) for dz in (1,2,3)]
    def zsend(w):
        Q=sets[w].shape[0]//4
        rows=pl.ds(pl.multiple_of(r*Q,8),Q)
        return [go(rcopy(sets[w].at[rows],view(w,s,r*Q,Q),ss.at[w,0,dz-1],rs.at[w,0,dz-1],(r,zpeer(p,dz)*2+c))) for dz in (1,2,3)]
    def core0(w):
        return go(rcopy(sets[w],view(w,s,0,sets[w].shape[0]),c0s.at[w],c0r.at[w],mate))
    def piece(w,dz,quarter,cols=None):
        Q=sets[w].shape[0]//4
        return view(w,((z+4-dz)%4)*2+c,quarter*Q,Q,cols)
    def fwd(w,dz,kind,quarter,dev,cols=None):
        ref=piece(w,dz,quarter,cols)
        return go(rcopy(ref,ref,ss.at[w,kind,dz-1],rs.at[w,kind,dz-1],dev))
    zc={};xc={};yc={};rc={};cores={}
    def send(w):
        zc[w]=zsend(w); cores[w]=core0(w)
    def stage_z(w):
        for dz in (1,2,3):
            zc[w][dz-1].wait_recv()
            xc[w,dz]=fwd(w,dz,1,r,xm)
            yc[w,dz]=fwd(w,dz,2,r,ym)
            fwd(w,dz,3,r,mate)
    def stage_xy(w):
        for dz in (1,2,3):
            xc[w,dz].wait_recv()
            rc[w,dz,0]=fwd(w,dz,6,p["rx"],ym,pl.ds(H,H))
            fwd(w,dz,4,p["rx"],mate)
            yc[w,dz].wait_recv()
            rc[w,dz,1]=fwd(w,dz,7,p["ry"],xm,pl.ds(0,H))
            fwd(w,dz,5,p["ry"],mate)
    def stage_r(w):
        for dz in (1,2,3):
            rc[w,dz,0].wait_recv()
            rc[w,dz,1].wait_recv()
            fwd(w,dz,8,p["rd"],mate)
    def from_mate(w):
        cores[w].wait_recv()
        for dz in (1,2,3):
            for kind,quarter in ((3,r),(4,p["rx"]),(5,p["ry"]),(8,p["rd"])):
                ref=piece(w,dz,quarter)
                rcopy(ref,ref,ss.at[w,kind,dz-1],rs.at[w,kind,dz-1],mate).wait_recv()
    send(0)
    owns=[]
    for w in range(4):
        locs[w].wait()
        cp=pltpu.make_async_copy(held[w],fulls[w].at[s],wsem.at[w]); cp.start(); owns.append(cp)
    for cp in vcs: cp.wait_recv()
    vp[...]=v_ref[...]+vz[0]+vz[1]+vz[2]
    vc=go(rcopy(vp,vm,vs.at[3],vr.at[3],mate))
    vc.wait_recv()
    vf[...]=vp[...]+vm[...]
    R=256
    gain=vf[0:1,:]; shift=vf[1:2,:]
    def norm(i,t):
        rows=pl.ds(pl.multiple_of(i*R,R),R)
        u,_=ln_unit(tok_ref[rows,:].astype(F32))
        nrm[rows,:]=(u*gain+shift).astype(BF)
        return t
    stage_z(0); send(1); send(2)
    lax.fori_loop(0,T//R,norm,0)
    local_copy(nrm,nf)
    cs[...]=jnp.zeros_like(cs)
    stage_xy(0); stage_z(1); send(3)
    stage_r(0)
    from_mate(0)
    owns[0].wait()
    S=qf.shape[0]; B=qf.shape[1]
    loads=[pltpu.make_async_copy(qf.at[t],qv.at[pl.ds(t*B,B)],qsem.at[t]) for t in range(S)]
    for cp in loads: cp.start()
    for cp in loads: cp.wait()
    def project(i,t):
        rows=pl.ds(pl.multiple_of(i*R,R),R)
        prj[rows,:]=nt(nrm[rows,:],qv[...]).astype(BF)
        return t
    half=T//R//2
    lax.fori_loop(0,half,project,0)
    stage_xy(1); stage_z(2)
    lax.fori_loop(half,T//R,project,0)
    local_copy(prj,pf)
    stage_r(1)
    def block(i,n):
        row0=i*BQ if isinstance(i,int) else pl.multiple_of(i*BQ,BQ)
        rows=pl.ds(row0,BQ)
        def put_out(off,val):
            attv[rows,pl.ds(off,128)]=val
        def put_aux(val):
            lsev[rows,:]=val
        fwd_block(row0,n,BQ,G,HP,unroll,prj,segr,nst,biasv.at[i],sigv.at[i],cs,put_out,put_aux)
    def run(i,t):
        block(i,NW)
        return t
    NB=T//BQ
    first=min(NW,NB)
    for i in range(first):
        block(i,i+1)
    stage_xy(2); stage_z(3)
    lax.fori_loop(first,NB,run,0)
    stage_r(2)
    local_copy(attv,af); local_copy(lsev,lf); local_copy(biasv,bf_); local_copy(sigv,sf)
    stage_xy(3); stage_r(3)
    for w in (1,2,3): from_mate(w)
    for cp in done: cp.wait_send()
    for cp in owns[1:]: cp.wait()
    for cp in outs: cp.wait()

def forward_all(q,o,u,d,v,tok,segr,nst,BQ=128,G=128,unroll=6):
    S=8
    T,D=tok.shape; NW=windows(T,BQ,G); NB=T//BQ
    any_=pl.BlockSpec(memory_space=pl.ANY); vm_=pl.BlockSpec(memory_space=pltpu.VMEM)
    full=lambda a: jax.ShapeDtypeStruct((S,)+a.shape,a.dtype)
    sd=jax.ShapeDtypeStruct
    dma=pltpu.SemaphoreType.DMA
    V=pltpu.VMEM
    E=S*q.shape[0]
    outs=pl.pallas_call(functools.partial(forward_kernel,BQ,G,NW,D//128,unroll),in_specs=[any_]*4+[vm_]*4,out_specs=[any_]*4+[vm_]+[any_]*6,
      out_shape=[full(o),full(u),full(d),full(q),sd(v.shape,F32),sd((T,D),BF),sd((T,E),BF),sd((T,D),BF),sd((T,128),F32),sd((NB,BQ,NW*G),F32),sd((NB,BQ,NW*G),BF)],
      scratch_shapes=[V((E,D),BF),V((T,D),BF),V((T,E),BF),V((T,D),BF),V((T,128),F32),V((NB,BQ,NW*G),F32),V((NB,BQ,NW*G),BF),V((1,T),F32),
        V((3,)+v.shape,F32),V(v.shape,F32),V(v.shape,F32),V(q.shape,BF),V(o.shape,BF),V(u.shape,BF),V(d.shape,BF),
        dma((4,)),dma((4,)),dma((8,)),dma((8,)),dma((4,)),dma((4,)),dma((4,9,3)),dma((4,9,3)),dma((4,)),dma((4,))],
      compiler_params=pltpu.CompilerParams(collective_id=1,has_side_effects=True,vmem_limit_bytes=56<<20),name="forward_all")(q,o,u,d,v,tok,segr,nst)
    return [a.reshape(-1,D) for a in outs[:4]]+list(outs[4:])

def backward_kernel(BQ,G,NW,HP,unroll,NK,
    act_h,gh_h,n2_h,cot_h,gb_h,att_h,prj_h,gatt_h,lse_h,bias_h,sig_h,nrm_h,qw_h,tok_h,gres_h,vec_ref,vg_ref,
    od,ou,oo,oq,tg_h,vo,
    gd,gu,go_,gq,cd,cu,co,cq,a1d,a1u,a1o,a1q,b1d,b1u,b1o,b1q,a2d,a2u,a2o,a2q,b2d,b2u,b2o,b2q,zd,zu,zo,zq,fd,fu,fo,fq,
    chunk,n2,cot,gb,att,prj,gatt,lse,bias,sig,qw,dk,dv,gp,ls,vb,
    csem,isem,ss,rs,cs_,cr_,vs,vr,osem):
    p=place()
    greet(p)
    r,s,c,z,x,y=p["r"],p["s"],p["c"],p["z"],p["x"],p["y"]
    mate=(r,p["mate"]); xm=(p["rx"],s); ym=(p["ry"],s)
    zdev=[(r,zpeer(p,dz)*2+c) for dz in (1,2,3)]
    T,D=n2.shape; H=D//2
    g=(gd,gu,go_,gq); cb=(cd,cu,co,cq); a1=(a1d,a1u,a1o,a1q); b1=(b1d,b1u,b1o,b1q)
    a2=(a2d,a2u,a2o,a2q); b2=(b2d,b2u,b2o,b2q); zb=(zd,zu,zo,zq); fin=(fd,fu,fo,fq); outs=(od,ou,oo,oq)
    lo=pl.ds(0,H); hi=pl.ds(H,H)
    done=[]
    def go(cp):
        cp.start(); done.append(cp); return cp
    ins={}
    def load(name,src,dst):
        ins[name]=pltpu.make_async_copy(src,dst,isem.at[len(ins)]); ins[name].start()
    cp_={}
    loc={}
    def acc(k): return g[k].at[:,c]
    def C(k,zz):
        cp_[k,"c",zz]=go(rcopy(g[k].at[zz,1-c],cb[k].at[zz],cs_.at[k,zz],cr_.at[k,zz],mate))
    def X(k):
        a=acc(k)
        for zz in range(4): cp_[k,"c",zz].wait_recv()
        def add(i,t):
            a[i]=a[i]+cb[k][i]
            return t
        lax.fori_loop(0,4,add,0)
        for yy in range(2):
            cp_[k,1+yy]=go(rcopy(a.at[:,yy*2+1-x,:,lo],a1[k].at[:,yy],ss.at[k,1+yy],rs.at[k,1+yy],xm))
        cp_[k,3]=go(rcopy(a.at[:,pl.ds((1-y)*2,2),:,hi],b1[k],ss.at[k,3],rs.at[k,3],ym))
    def Y(k):
        a=acc(k)
        cp_[k,1].wait_recv(); cp_[k,2].wait_recv(); cp_[k,3].wait_recv()
        def add(i,t):
            for yy in range(2):
                a[i,yy*2+x,:,lo]=a[i,yy*2+x,:,lo]+a1[k][i,yy]
            for xx in range(2):
                a[i,y*2+xx,:,hi]=a[i,y*2+xx,:,hi]+b1[k][i,xx]
            return t
        lax.fori_loop(0,4,add,0)
        cp_[k,4]=go(rcopy(a.at[:,(1-y)*2+x,:,lo],a2[k],ss.at[k,4],rs.at[k,4],ym))
        cp_[k,5]=go(rcopy(a.at[:,y*2+1-x,:,hi],b2[k],ss.at[k,5],rs.at[k,5],xm))
    def Z(k):
        a=acc(k)
        cp_[k,4].wait_recv(); cp_[k,5].wait_recv()
        def add(i,t):
            a[i,r,:,lo]=a[i,r,:,lo]+a2[k][i]
            a[i,r,:,hi]=a[i,r,:,hi]+b2[k][i]
            return t
        lax.fori_loop(0,4,add,0)
        for dz in (1,2,3):
            cp_[k,5+dz]=go(rcopy(a.at[zpeer(p,dz),r],zb[k].at[dz-1],ss.at[k,5+dz],rs.at[k,5+dz],zdev[dz-1]))
    def Fn(k):
        for dz in (1,2,3): cp_[k,5+dz].wait_recv()
        t=acc(k)[z,r].astype(F32)
        for dz in range(3): t=t+zb[k][dz].astype(F32)
        fin[k][r]=t.astype(BF)
        cp_[k,9]=go(rcopy(fin[k].at[r],fin[k].at[r],ss.at[k,9],rs.at[k,9],xm))
        cp_[k,10]=go(rcopy(fin[k].at[r],fin[k].at[r],ss.at[k,10],rs.at[k,10],ym))
    def Gn(k):
        cp_[k,9].wait_recv()
        cp_[k,11]=go(rcopy(fin[k].at[p["rx"],:,hi],fin[k].at[p["rx"],:,hi],ss.at[k,11],rs.at[k,11],ym))
        cp_[k,10].wait_recv()
        cp_[k,12]=go(rcopy(fin[k].at[p["ry"],:,lo],fin[k].at[p["ry"],:,lo],ss.at[k,12],rs.at[k,12],xm))
    def Hn(k):
        cp_[k,11].wait_recv(); cp_[k,12].wait_recv()
        loc[k]=pltpu.make_async_copy(fin[k],outs[k],osem.at[k]); loc[k].start()
    zz0=(z//2)*2
    vdev=[mate,xm,ym,(r,(zz0+1-z%2)*2+c),(r,((z+2)%4)*2+c)]
    def V(n):
        if n>0:
            cp_["v",n-1].wait_recv()
            vb[2*n]=vb[2*n-2]+vb[2*n-1]
        if n<5:
            cp_["v",n]=go(rcopy(vb.at[2*n],vb.at[2*n+1],vs.at[n],vr.at[n],vdev[n]))
        else:
            vo[...]=vb[10]
    load("cot",cot_h,cot)
    WC=chunk.shape[2]
    order=[(w,half,zz) for w in range(2) for half in range(2) for zz in range(4)]
    def fetch(n):
        w,half,zz=order[n]
        cc=(1-c) if half==0 else c
        src=(act_h,gh_h)[w].at[:,pl.ds(pl.multiple_of((zz*2+cc)*WC,128),WC)]
        return pltpu.make_async_copy(src,chunk.at[n%2],csem.at[n%2])
    fetch(0).start()
    fetch(1).start()
    load("n2",n2_h,n2); load("gb",gb_h,gb); load("att",att_h,att); load("prj",prj_h,prj); load("gatt",gatt_h,gatt)
    load("lse",lse_h,lse); load("bias",bias_h,bias); load("sig",sig_h,sig); load("qw",qw_h,qw)
    ins["cot"].wait()
    for n,(w,half,zz) in enumerate(order):
        fetch(n).wait()
        if n==8: ins["n2"].wait()
        cc=(1-c) if half==0 else c
        res=tn(chunk[n%2],(cot,n2)[w][...])
        q4=WC//4
        for k in range(4):
            g[w][zz,cc,k]=res[k*q4:(k+1)*q4].astype(BF)
        if n+2<len(order): fetch(n+2).start()
        if half==0: C(w,zz)
        if n==7: X(0)
    ins["gb"].wait(); ins["att"].wait()
    res=tn(att[...],gb[...])
    q4=D//32
    for sh in range(8):
        for k in range(4):
            at=sh*(D//8)+k*q4
            go_[sh//2,sh%2,k]=res[at:at+q4].astype(BF)
    for zz in range(4): C(2,zz)
    for name in ("prj","gatt","lse","bias","sig"): ins[name].wait()
    load("nrm",nrm_h,n2); load("tok",tok_h,cot)
    dk[...]=jnp.zeros_like(dk)
    dv[...]=jnp.zeros_like(dv)
    ls[...]=jnp.zeros_like(ls)
    def block(i,n):
        row0=i*BQ if isinstance(i,int) else pl.multiple_of(i*BQ,BQ)
        rows=pl.ds(row0,BQ)
        bwd_block(row0,n,BQ,G,HP,unroll,prj,gatt.at[rows],att.at[rows],lse.at[rows],bias.at[i],sig.at[i],prj,dk,dv,gp,ls)
    NB=T//BQ
    first=min(NW-1,NB)
    def run(t,u):
        block(NB-1-t,NW)
        return u
    block(NB-1,NW)
    Y(0); X(1); X(2)
    lax.fori_loop(1,NB-1-first,run,0)
    Z(0)
    block(first,NW)
    events=[lambda: None, lambda: (Y(1),Y(2)), lambda: None, lambda: None]
    for t,i in enumerate(range(first-1,-1,-1)):
        block(i,i+1)
        events[t]()
    prj[:,D:2*D]=dk[...].astype(BF)
    prj[:,2*D:]=dv[...].astype(BF)
    load("gres",gres_h,dk)
    ins["nrm"].wait()
    E2=prj.shape[1]//2; q4=gq.shape[3]
    for part in range(2):
        for h in range(2):
            res=tn(prj[:,part*E2:(part+1)*E2],n2[:,h*H:(h+1)*H])
            for blk in range(E2//q4):
                sh=part*4+blk//4
                gq[sh//2,sh%2,blk%4,:,h*H:(h+1)*H]=res[blk*q4:(blk+1)*q4].astype(BF)
        for zz in (part*2,part*2+1): C(3,zz)
        if part==0: Fn(0)
    Z(1); Z(2)
    X(3)
    ins["tok"].wait(); ins["qw"].wait(); ins["gres"].wait()
    vb[0]=vg_ref[...]
    R=256
    gain=vec_ref[0:1,:]
    def dgrad(i,t):
        rows=pl.ds(pl.multiple_of(i*R,R),R)
        gn=nn(prj[rows,:],qw[...])
        u,rstd=ln_unit(cot[rows,:].astype(F32))
        vb[0,0:1,:]=vb[0,0:1,:]+jnp.sum(gn*u,axis=0,keepdims=True)
        vb[0,1:2,:]=vb[0,1:2,:]+jnp.sum(gn,axis=0,keepdims=True)
        gg=gn*gain
        gb[rows,:]=(dk[rows,:]+rstd*(gg-rowmean(gg)-u*rowmean(gg*u))).astype(BF)
        return t
    lax.fori_loop(0,T//R//2,dgrad,0)
    Gn(0)
    lax.fori_loop(T//R//2,T//R,dgrad,0)
    out_cp=pltpu.make_async_copy(gb,tg_h,osem.at[4]); out_cp.start()
    Y(3); V(0); Z(3); V(1); Fn(1); V(2); Fn(2); Hn(0); V(3); Gn(1); V(4); Gn(2)
    V(5); Fn(3); Hn(1); Hn(2); Gn(3); Hn(3)
    for cp in done: cp.wait_send()
    for k in range(4): loc[k].wait()
    out_cp.wait()

def backward_all(act,gh,n2,cot,gb,att,prj,gatt,lse,bias,sig,nrm,qw,tok,gres,vec,vg,BQ=128,G=128,unroll=5):
    T,D=tok.shape; F=act.shape[1]; E=prj.shape[1]; NB=T//BQ; NW=bias.shape[2]//G
    any_=pl.BlockSpec(memory_space=pl.ANY); vm_=pl.BlockSpec(memory_space=pltpu.VMEM)
    dma=pltpu.SemaphoreType.DMA; V=pltpu.VMEM; sd=jax.ShapeDtypeStruct
    Qs=[F//32,F//32,D//32,E//32]; H=D//2
    scr=[V((4,2,4,q,D),BF) for q in Qs]+[V((4,4,q,D),BF) for q in Qs]+[V((4,2,q,H),BF) for q in Qs]+[V((4,2,q,H),BF) for q in Qs]
    scr+=[V((4,q,H),BF) for q in Qs]+[V((4,q,H),BF) for q in Qs]+[V((3,q,D),BF) for q in Qs]+[V((4,q,D),BF) for q in Qs]
    scr+=[V((2,T,F//8),BF)]+[V((T,D),BF)]*4+[V((T,E),BF),V((T,D),BF),V((T,128),F32),V(bias.shape,F32),V(sig.shape,BF),V((E,D),BF)]
    scr+=[V((T,D),F32)]*2+[V((BQ,NW*G),F32),V((1,T),F32),V((11,8,D),F32)]
    scr+=[dma((2,)),dma((14,)),dma((4,13)),dma((4,13)),dma((4,4)),dma((4,4)),dma((5,)),dma((5,)),dma((5,))]
    outs=pl.pallas_call(functools.partial(backward_kernel,BQ,G,NW,D//128,unroll,0),in_specs=[any_]*15+[vm_]*2,out_specs=[any_]*5+[vm_],
      out_shape=[sd((4,q,D),BF) for q in Qs]+[sd((T,D),BF),sd((8,D),F32)],scratch_shapes=scr,
      compiler_params=pltpu.CompilerParams(collective_id=2,has_side_effects=True,vmem_limit_bytes=63<<20),name="backward_all")(act,gh,n2,cot,gb,att,prj,gatt,lse,bias,sig,nrm,qw,tok,gres,vec,vg)
    return [a.reshape(-1,D) for a in outs[:4]],outs[4],outs[5]


def gather(x):
    return lax.all_gather(x, "shard", axis=0, tiled=True)


def forward_plain(q, o, u, d, v, tok, segr, nst, nblk):
    q, o, u, d = gather(q), gather(o), gather(u), gather(d)
    vec = lax.psum(v, "shard")
    normed, projected = qkv_proj(tok, q, vec)
    return [o, u, d, q, vec, normed, projected] + list(attn_fwd(projected, segr, nst, nblk))


def backward_plain(act, gh, n2, cot, gb, att, prj, gatt, lse, bias, sig, nrm, qw, tok, gres, vec, vg, nblk):
    def one(g):
        part = lax.psum_scatter(g, "shard", scatter_dimension=0, tiled=True)
        return lax.psum(part, "rep")

    gproj = attn_bwd(prj, gatt, att, lse, bias, sig, nblk)
    tgrad, vec1 = qkv_dgrad(gproj, qw, tok, gres, vec)
    gs = [weight_grad(act, cot), weight_grad(gh, n2), weight_grad(att, gb), weight_grad(gproj, nrm)]
    total = jnp.concatenate([vec1[:2], vg[2:]], axis=0)
    return [one(g) for g in gs], tgrad, lax.psum(total, ("rep", "shard"))


def local(tokens, segment_ids, qkv_weight, out_weight, up_weight, down_weight,
          norm1_gain, norm1_shift, norm2_gain, norm2_shift, cotangent):
    tok = tokens[0]
    cot = cotangent[0]
    seg = segment_ids[0]
    model = tok.shape[1]
    known = lax.axis_size("rep") == 4 and lax.axis_size("shard") == 8
    piece = norm1_gain.shape[0]
    at = lax.axis_index("shard") * piece
    vec_part = jnp.stack([norm1_gain, norm1_shift, norm2_gain, norm2_shift]).astype(F32)
    vec_mine = lax.dynamic_update_slice(jnp.zeros((8, model), F32), vec_part, (0, at))
    segr, nst, nblk = prep(seg)
    parts = (qkv_weight.T, out_weight, up_weight.T, down_weight, vec_mine, tok, segr, nst)
    held = forward_all(*parts) if known else forward_plain(*parts, nblk)
    out_full, up_t, down_full, qkv_t, vec, normed, projected, attended, lse, bias, sig = held
    output, gres, gatt, act, gh, n2, gb, vg = mlp(tok, attended, cot, out_full, up_t, down_full, vec)
    parts = (act, gh, n2, cot, gb, attended, projected, gatt, lse, bias, sig, normed, qkv_t, tok, gres, vec, vg)
    grads, tgrad, vec_sum = backward_all(*parts) if known else backward_plain(*parts, nblk)
    down_grad, up_grad, out_grad, qkv_grad = [g.astype(F32) for g in grads]
    mine = lax.dynamic_slice_in_dim(vec_sum, at, piece, 1)
    return (output[None], tgrad[None], qkv_grad.T, out_grad, up_grad.T, down_grad,
            mine[0], mine[1], mine[2], mine[3])


def solution(mesh):
    seq = P(("rep", "shard"), None, None)
    cols, rows, vecs = P(None, "shard"), P("shard", None), P("shard")
    return jax.shard_map(
        local,
        mesh=mesh,
        in_specs=(seq, P(("rep", "shard"), None), cols, rows, cols, rows, vecs, vecs, vecs, vecs, seq),
        out_specs=(seq, seq, cols, rows, cols, rows, vecs, vecs, vecs, vecs),
        check_vma=False,
    )
```

```python
import functools

import jax
import jax.numpy as jnp
from jax import lax
from jax.experimental import pallas as pl
from jax.experimental.pallas import tpu as pltpu
from jax.sharding import PartitionSpec as P

F32 = jnp.float32
BF = jnp.bfloat16
NEG=-1e30
WIN=512
def nt(a,b):
    return lax.dot_general(a,b,(((1,),(1,)),((),())),preferred_element_type=F32)
def nn(a,b):
    return lax.dot_general(a,b,(((1,),(0,)),((),())),preferred_element_type=F32)
def tn(a,b):
    return lax.dot_general(a,b,(((0,),(0,)),((),())),preferred_element_type=F32)
def split2(x):
    hi=x.astype(BF)
    lo=(x-hi.astype(F32)).astype(BF)
    return hi,lo
def eighth(x):
    return x*jnp.asarray(0.125,BF)

def fwd_block(row0,n,BQ,G,HP,unroll,qkv,segr,nst,bias,sig,cs,put_out,put_aux):
    D=HP*128
    W=n*G
    k0=row0+BQ-W
    if not isinstance(k0,int): k0=pl.multiple_of(k0,G)
    kw=pl.ds(k0,W); rows=pl.ds(row0,BQ)
    lane=lax.broadcasted_iota(jnp.int32,(BQ,128),1)
    left=lane<64
    same=jnp.broadcast_to(segr[:,rows],(128,BQ)).T[:,:1]==segr[:,kw]
    qi=lax.broadcasted_iota(jnp.int32,(BQ,W),0)+(W-BQ)
    ki=lax.broadcasted_iota(jnp.int32,(BQ,W),1)
    allowed=same&(ki<=qi)
    chosen=same&(ki<qi)&(nst[:,kw]>0)
    q=eighth(qkv[rows,pl.ds(0,128)])
    k=qkv[kw,pl.ds(D,128)]
    s0=nt(jnp.where(left,q,jnp.zeros_like(q)),k)
    e=jnp.exp(-jnp.abs(s0))
    sp=jnp.maximum(s0,0.0)+jnp.log1p(e)
    sg=jnp.where(s0>=0,1.0,e)/(1.0+e)
    sel=jnp.where(chosen,sp,0.0)
    sig[:,sig.shape[1]-W:]=jnp.where(chosen,sg,0.0).astype(BF)
    hi,lo=split2(sel)
    ri=lax.broadcasted_iota(jnp.int32,(BQ,BQ),0); ci=lax.broadcasted_iota(jnp.int32,(BQ,BQ),1)
    L=(ri>ci).astype(BF)
    pen=nn(L,hi)+nn(L,lo)+cs[:,kw]
    cs[:,kw]=cs[:,kw]+jnp.sum(sel,axis=0,keepdims=True)
    bias[:,bias.shape[1]-W:]=jnp.where(allowed,-pen,NEG)
    ones=jnp.ones((W,128),BF)
    def pair(j,acc):
        off=pl.multiple_of(j*128,128)
        q=eighth(qkv[rows,pl.ds(off,128)])
        z=jnp.zeros_like(q)
        k=qkv[kw,pl.ds(D+off,128)]
        v1=jnp.concatenate([qkv[kw,pl.ds(2*D+off,128)],ones],axis=1)
        b=bias[:,bias.shape[1]-W:]
        outs=[]
        for hh in range(2):
            qm=jnp.where(left,q,z) if hh==0 else jnp.where(left,z,q)
            s=nt(qm,k)+b
            m=jnp.max(s,axis=1,keepdims=True)
            p=jnp.exp(s-m)
            ol=nn(p.astype(BF),v1)
            l=ol[:,128:]
            outs.append(ol[:,:128]*(1.0/l))
            acc=jnp.where(lane==2*j+hh,m+jnp.log(l),acc)
        put_out(off,jnp.where(left,outs[0],outs[1]).astype(BF))
        return acc
    lse=lax.fori_loop(0,HP,pair,jnp.zeros((BQ,128),F32),unroll=unroll)
    put_aux(lse)

def attn_fwd_kernel(BQ,G,NW,HP,unroll,nblk_ref,qkv_ref,segr_ref,nst_ref,o_ref,aux_ref,bias_ref,sig_ref,cs_ref):
    i=pl.program_id(0)
    @pl.when(i==0)
    def _():
        cs_ref[...]=jnp.zeros_like(cs_ref)
    row0=pl.multiple_of(i*BQ,BQ)
    def put_out(off,val):
        o_ref[:,pl.ds(off,128)]=val
    def put_aux(val):
        aux_ref[...]=val
    for n in range(1,NW+1):
        @pl.when(nblk_ref[i]==n)
        def _(n=n):
            fwd_block(row0,n,BQ,G,HP,unroll,qkv_ref,segr_ref,nst_ref,bias_ref.at[0],sig_ref.at[0],cs_ref,put_out,put_aux)

def windows(T,BQ,G):
    return min(T//G,-(-(WIN-1+BQ)//G))

def attn_fwd(qkv,segr,nst,nblk,BQ=128,G=128,unroll=6):
    T,D3=qkv.shape; D=D3//3; HP=D//128
    NW=windows(T,BQ,G)
    NB=T//BQ
    whole=lambda shape: pl.BlockSpec(shape,lambda i,*_:(0,0),pipeline_mode=pl.Buffered(1))
    gs=pltpu.PrefetchScalarGridSpec(num_scalar_prefetch=1,grid=(NB,),
      in_specs=[whole((T,D3)),whole((1,T)),whole((1,T))],
      out_specs=[pl.BlockSpec((BQ,D),lambda i,*_:(i,0)),pl.BlockSpec((BQ,128),lambda i,*_:(i,0)),
        pl.BlockSpec((1,BQ,NW*G),lambda i,*_:(i,0,0)),pl.BlockSpec((1,BQ,NW*G),lambda i,*_:(i,0,0))],
      scratch_shapes=[pltpu.VMEM((1,T),F32)])
    return pl.pallas_call(functools.partial(attn_fwd_kernel,BQ,G,NW,HP,unroll),grid_spec=gs,
      out_shape=[jax.ShapeDtypeStruct((T,D),BF),jax.ShapeDtypeStruct((T,128),F32),
        jax.ShapeDtypeStruct((NB,BQ,NW*G),F32),jax.ShapeDtypeStruct((NB,BQ,NW*G),BF)],
      compiler_params=pltpu.CompilerParams(vmem_limit_bytes=40<<20),name="attn_fwd")(nblk,qkv,segr,nst)

def bwd_block(row0,n,BQ,G,HP,unroll,qkv,do_ref,o_ref,aux_ref,bias,sig,dq_ref,dk_ref,dv_ref,gp_ref,ls_ref):
    D=HP*128
    W=n*G
    k0=row0+BQ-W
    if not isinstance(k0,int): k0=pl.multiple_of(k0,G)
    kw=pl.ds(k0,W); rows=pl.ds(row0,BQ)
    lane=lax.broadcasted_iota(jnp.int32,(BQ,128),1)
    left=lane<64
    gp_ref[:,:W]=jnp.zeros((BQ,W),F32)
    lse=aux_ref[...]
    def stack(t):
        z=jnp.zeros_like(t)
        return jnp.concatenate([jnp.where(left,t,z),jnp.where(left,z,t)],axis=0)
    def work(j,first):
        off=j*128 if isinstance(j,int) else pl.multiple_of(j*128,128)
        k=qkv[kw,pl.ds(D+off,128)]
        v=qkv[kw,pl.ds(2*D+off,128)]
        do=do_ref[:,pl.ds(off,128)]
        prod=do.astype(F32)*o_ref[:,pl.ds(off,128)].astype(F32)
        b=bias[:,bias.shape[1]-W:]
        q2=stack(eighth(qkv[rows,pl.ds(off,128)]))
        do2=stack(do)
        def row(t0,t1):
            return jnp.sum(t0,axis=1,keepdims=True),jnp.sum(t1,axis=1,keepdims=True)
        l0,l1=row(jnp.where(lane==2*j,lse,0.0),jnp.where(lane==2*j+1,lse,0.0))
        e0,e1=row(jnp.where(left,prod,0.0),jnp.where(left,0.0,prod))
        s2=nt(q2,k)
        dp2=nt(do2,v)
        p0=jnp.exp(s2[:BQ]+b-l0); p1=jnp.exp(s2[BQ:]+b-l1)
        ds0=p0*(dp2[:BQ]-e0); ds1=p1*(dp2[BQ:]-e1)
        if not first:
            gp_ref[:,:W]=gp_ref[:,:W]+(ds0+ds1)
        else:
            gp=gp_ref[:,:W]+(ds0+ds1)
            hi,lo=split2(gp)
            ri=lax.broadcasted_iota(jnp.int32,(BQ,BQ),0); ci=lax.broadcasted_iota(jnp.int32,(BQ,BQ),1)
            U=(ci>ri).astype(BF)
            gsel=nn(U,hi)+nn(U,lo)+ls_ref[:,kw]
            ls_ref[:,kw]=ls_ref[:,kw]+jnp.sum(gp,axis=0,keepdims=True)
            ds0=ds0-gsel*sig[:,sig.shape[1]-W:].astype(F32)
        dsb=jnp.concatenate([ds0.astype(BF),ds1.astype(BF)],axis=0)
        pb=jnp.concatenate([p0.astype(BF),p1.astype(BF)],axis=0)
        dq2=nn(dsb,k)
        dq_ref[rows,pl.ds(off,128)]=(jnp.where(left,dq2[:BQ],dq2[BQ:])*0.125).astype(BF)
        dk_ref[kw,pl.ds(off,128)]+=tn(dsb,q2)
        dv_ref[kw,pl.ds(off,128)]+=tn(pb,do2)
    def body(j,c):
        work(j,False)
        return c
    lax.fori_loop(1,HP,body,0,unroll=unroll)
    work(0,True)

def attn_bwd_kernel(BQ,G,NW,HP,unroll,NB,nblk_ref,qkv_ref,do_ref,o_ref,aux_ref,bias_ref,sig_ref,out_ref,dk_ref,dv_ref,gp_ref,ls_ref):
    step=pl.program_id(0)
    i=NB-1-step
    D=HP*128
    @pl.when(step==0)
    def _():
        dk_ref[...]=jnp.zeros_like(dk_ref)
        dv_ref[...]=jnp.zeros_like(dv_ref)
        ls_ref[...]=jnp.zeros_like(ls_ref)
    row0=pl.multiple_of(i*BQ,BQ)
    for n in range(1,NW+1):
        @pl.when(nblk_ref[i]==n)
        def _(n=n):
            bwd_block(row0,n,BQ,G,HP,unroll,qkv_ref,do_ref,o_ref,aux_ref,bias_ref.at[0],sig_ref.at[0],out_ref,dk_ref,dv_ref,gp_ref,ls_ref)
    @pl.when(step==NB-1)
    def _():
        out_ref[:,D:2*D]=dk_ref[...].astype(BF)
        out_ref[:,2*D:]=dv_ref[...].astype(BF)

def attn_bwd(qkv,do,o,aux,bias,sig,nblk,BQ=128,G=128,unroll=5):
    T,D3=qkv.shape; D=D3//3; HP=D//128
    NW=bias.shape[2]//G
    NB=T//BQ
    whole=lambda shape: pl.BlockSpec(shape,lambda i,*_:(0,0),pipeline_mode=pl.Buffered(1))
    rb=lambda w: pl.BlockSpec((BQ,w),lambda i,*_:(NB-1-i,0))
    r3=pl.BlockSpec((1,BQ,NW*G),lambda i,*_:(NB-1-i,0,0))
    gs=pltpu.PrefetchScalarGridSpec(num_scalar_prefetch=1,grid=(NB,),
      in_specs=[whole((T,D3)),rb(D),rb(D),rb(128),r3,r3],
      out_specs=whole((T,D3)),
      scratch_shapes=[pltpu.VMEM((T,D),F32),pltpu.VMEM((T,D),F32),pltpu.VMEM((BQ,NW*G),F32),pltpu.VMEM((1,T),F32)])
    return pl.pallas_call(functools.partial(attn_bwd_kernel,BQ,G,NW,HP,unroll,NB),grid_spec=gs,
      out_shape=jax.ShapeDtypeStruct((T,D3),BF),
      compiler_params=pltpu.CompilerParams(vmem_limit_bytes=50<<20),name="attn_bwd")(nblk,qkv,do,o,aux,bias,sig)

def prep(seg,BQ=128,G=128):
    T=seg.shape[0]
    NB=T//BQ
    at=seg[::BQ]
    first=jnp.sum((seg[None,:]<at[:,None]).astype(jnp.int32),axis=1)
    ends=(jnp.arange(NB,dtype=jnp.int32)+1)*BQ
    nblk=(ends-(first//G)*G)//G
    starts=jnp.concatenate([jnp.ones((1,),bool),seg[1:]!=seg[:-1]])
    nst=jnp.logical_not(starts).astype(jnp.int32)[None,:]
    return seg[None,:].astype(F32),nst,nblk

EPS=1e-5
GC=0.7978845608028654; GA=0.044715
def rowmean(x): return jnp.mean(x,axis=-1,keepdims=True)
def ln_unit(x):
    m=rowmean(x); c=x-m; v=rowmean(c*c); r=lax.rsqrt(v+EPS)
    return c*r, r

def qkv_kernel(tok_ref,w_ref,vec_ref,n_ref,o_ref):
    u,_=ln_unit(tok_ref[...].astype(F32))
    n=(u*vec_ref[0:1,:]+vec_ref[1:2,:]).astype(BF)
    n_ref[...]=n
    o_ref[...]=nt(n,w_ref[...]).astype(BF)
def qkv_proj(tok,wT,vec,R=256):
    T,D=tok.shape; E=wT.shape[0]
    c=lambda s: pl.BlockSpec(s,lambda i:(0,0),pipeline_mode=pl.Buffered(1))
    return pl.pallas_call(qkv_kernel,grid=(T//R,),in_specs=[pl.BlockSpec((R,D),lambda i:(i,0)),c((E,D)),c(vec.shape)],
      out_specs=[pl.BlockSpec((R,D),lambda i:(i,0)),pl.BlockSpec((R,E),lambda i:(i,0))],
      out_shape=[jax.ShapeDtypeStruct((T,D),BF),jax.ShapeDtypeStruct((T,E),BF)],
      compiler_params=pltpu.CompilerParams(vmem_limit_bytes=40<<20),name="qkv_proj")(tok,wT,vec)

def mlp_kernel(NC,C,tok_ref,att_ref,cot_ref,ow_ref,up_ref,dn_ref,vec_ref,
    out_ref,gres_ref,gatt_ref,act_ref,gh_ref,n2_ref,gb_ref,vg_ref):
    i=pl.program_id(0)
    gain=vec_ref[2:3,:]; shift=vec_ref[3:4,:]
    res=tok_ref[...].astype(F32)+nn(att_ref[...],ow_ref[...])
    u,rstd=ln_unit(res)
    n2=(u*gain+shift).astype(BF)
    n2_ref[...]=n2
    cot=cot_ref[...]
    out_acc=res
    g_acc=jnp.zeros_like(res)
    for c in range(NC):
        cs=slice(c*C,(c+1)*C)
        h=nt(n2,up_ref[cs,:])
        h2=h*h
        t=jnp.tanh(h*(GC+GC*GA*h2))
        half=0.5*(1.0+t)
        act=(h*half).astype(BF)
        act_ref[:,cs]=act
        ga=nt(cot,dn_ref[cs,:])
        dg=half+(0.5*h)*(1.0-t*t)*(GC+3.0*GC*GA*h2)
        gh=(ga*dg).astype(BF)
        gh_ref[:,cs]=gh
        out_acc=out_acc+nn(act,dn_ref[cs,:])
        g_acc=g_acc+nn(gh,up_ref[cs,:])
    out_ref[...]=out_acc.astype(BF)
    @pl.when(i==0)
    def _():
        vg_ref[...]=jnp.zeros_like(vg_ref)
    vg_ref[2:3,:]+=jnp.sum(g_acc*u,axis=0,keepdims=True)
    vg_ref[3:4,:]+=jnp.sum(g_acc,axis=0,keepdims=True)
    g=g_acc*gain
    gr=cot.astype(F32)+rstd*(g-rowmean(g)-u*rowmean(g*u))
    gres_ref[...]=gr
    gb=gr.astype(BF)
    gb_ref[...]=gb
    gatt_ref[...]=nt(gb,ow_ref[...]).astype(BF)
def mlp(tok,att,cot,ow,upT,dn,vec,R=256,C=768):
    T,D=tok.shape; F=upT.shape[0]
    c=lambda s: pl.BlockSpec(s,lambda i:(0,0),pipeline_mode=pl.Buffered(1))
    rb=lambda w: pl.BlockSpec((R,w),lambda i:(i,0))
    sd=jax.ShapeDtypeStruct
    return pl.pallas_call(functools.partial(mlp_kernel,F//C,C),grid=(T//R,),
      in_specs=[rb(D),rb(D),rb(D),c((D,D)),c((F,D)),c((F,D)),c(vec.shape)],
      out_specs=[rb(D),rb(D),rb(D),rb(F),rb(F),rb(D),rb(D),c((8,D))],
      out_shape=[sd((T,D),BF),sd((T,D),F32),sd((T,D),BF),sd((T,F),BF),sd((T,F),BF),sd((T,D),BF),sd((T,D),BF),sd((8,D),F32)],
      compiler_params=pltpu.CompilerParams(vmem_limit_bytes=56<<20),name="mlp")(tok,att,cot,ow,upT,dn,vec)

def wg_kernel(gp_ref,n_ref,o_ref):
    o_ref[...]=tn(gp_ref[...],n_ref[...]).astype(BF)
def weight_grad(gp,n1,WC=384):
    T,E=gp.shape; D=n1.shape[1]
    return pl.pallas_call(wg_kernel,grid=(E//WC,),in_specs=[pl.BlockSpec((T,WC),lambda i:(0,i)),pl.BlockSpec((T,D),lambda i:(0,0),pipeline_mode=pl.Buffered(1))],
      out_specs=pl.BlockSpec((WC,D),lambda i:(i,0)),out_shape=jax.ShapeDtypeStruct((E,D),BF),
      compiler_params=pltpu.CompilerParams(vmem_limit_bytes=40<<20),name="weight_grad")(gp,n1)
def dg_kernel(gp_ref,w_ref,tok_ref,gres_ref,vec_ref,o_ref,vg_ref):
    i=pl.program_id(0)
    gn=nn(gp_ref[...],w_ref[...])
    u,rstd=ln_unit(tok_ref[...].astype(F32))
    @pl.when(i==0)
    def _():
        vg_ref[...]=jnp.zeros_like(vg_ref)
    vg_ref[0:1,:]+=jnp.sum(gn*u,axis=0,keepdims=True)
    vg_ref[1:2,:]+=jnp.sum(gn,axis=0,keepdims=True)
    g=gn*vec_ref[0:1,:]
    o_ref[...]=(gres_ref[...]+rstd*(g-rowmean(g)-u*rowmean(g*u))).astype(BF)
def qkv_dgrad(gp,wT,tok,gres,vec,R=256):
    T,E=gp.shape; D=tok.shape[1]
    c=lambda s: pl.BlockSpec(s,lambda i:(0,0),pipeline_mode=pl.Buffered(1))
    rb=lambda w: pl.BlockSpec((R,w),lambda i:(i,0))
    return pl.pallas_call(dg_kernel,grid=(T//R,),in_specs=[rb(E),c((E,D)),rb(D),rb(D),c(vec.shape)],out_specs=[rb(D),c((8,D))],
      out_shape=[jax.ShapeDtypeStruct((T,D),BF),jax.ShapeDtypeStruct((8,D),F32)],
      compiler_params=pltpu.CompilerParams(vmem_limit_bytes=40<<20),name="qkv_dgrad")(gp,wT,tok,gres,vec)

MESH=pl.DeviceIdType.MESH

def place():
    r=lax.axis_index("rep"); s=lax.axis_index("shard")
    y=r//2; x=r%2; z=s//2; c=s%2
    return dict(r=r,s=s,y=y,x=x,z=z,c=c,rx=y*2+(1-x),ry=(1-y)*2+x,rd=(1-y)*2+(1-x),mate=z*2+(1-c))
def zpeer(p,dz):
    return (p["z"]+dz)%4
def greet(p):
    bar=pltpu.get_barrier_semaphore()
    for dev in ((p["r"],p["mate"]),(p["rx"],p["s"]),(p["ry"],p["s"]))+tuple((p["r"],zpeer(p,dz)*2+p["c"]) for dz in (1,2,3)):
        pl.semaphore_signal(bar,inc=1,device_id=dev,device_id_type=MESH)
    pl.semaphore_wait(bar,6)
def rcopy(src,dst,ss,rs,dev):
    return pltpu.make_async_remote_copy(src_ref=src,dst_ref=dst,send_sem=ss,recv_sem=rs,device_id=dev,device_id_type=MESH)


def forward_kernel(BQ,G,NW,HP,unroll,q_ref,o_ref,u_ref,d_ref,v_ref,tok_ref,seg_ref,
    of,uf,df,qf,vf,nf,pf,af,lf,bf_,sf,
    qv,nrm,prj,attv,lsev,biasv,sigv,cs,vz,vp,vm,h0,h1,h2,h3,segr,nst,lsem,wsem,osem,qsem,c0s,c0r,ss,rs,vs,vr):
    p=place()
    greet(p)
    r,s,c,z=p["r"],p["s"],p["c"],p["z"]
    mate=(r,p["mate"]); xm=(p["rx"],s); ym=(p["ry"],s)
    sets=(q_ref,o_ref,u_ref,d_ref)
    fulls=(qf,of,uf,df)
    held=(h0,h1,h2,h3)
    T,D=nrm.shape
    H=D//2
    done=[]; outs=[]
    def go(cp):
        cp.start(); done.append(cp); return cp
    def local_copy(src,dst):
        cp=pltpu.make_async_copy(src,dst,osem.at[len(outs)]); cp.start(); outs.append(cp)
    def view(w,shard,first,count,cols=None):
        rows=pl.ds(pl.multiple_of(first,8),count)
        return fulls[w].at[shard,rows] if cols is None else fulls[w].at[shard,rows,cols]
    locs=[]
    for w in range(4):
        cp=pltpu.make_async_copy(sets[w],held[w],lsem.at[w]); cp.start(); locs.append(cp)
    vcs=[go(rcopy(v_ref,vz.at[dz-1],vs.at[dz-1],vr.at[dz-1],(r,zpeer(p,dz)*2+c))) for dz in (1,2,3)]
    def zsend(w):
        Q=sets[w].shape[0]//4
        rows=pl.ds(pl.multiple_of(r*Q,8),Q)
        return [go(rcopy(sets[w].at[rows],view(w,s,r*Q,Q),ss.at[w,0,dz-1],rs.at[w,0,dz-1],(r,zpeer(p,dz)*2+c))) for dz in (1,2,3)]
    def core0(w):
        return go(rcopy(sets[w],view(w,s,0,sets[w].shape[0]),c0s.at[w],c0r.at[w],mate))
    def piece(w,dz,quarter,cols=None):
        Q=sets[w].shape[0]//4
        return view(w,((z+4-dz)%4)*2+c,quarter*Q,Q,cols)
    def fwd(w,dz,kind,quarter,dev,cols=None):
        ref=piece(w,dz,quarter,cols)
        return go(rcopy(ref,ref,ss.at[w,kind,dz-1],rs.at[w,kind,dz-1],dev))
    zc={};xc={};yc={};rc={};cores={}
    def send(w):
        zc[w]=zsend(w); cores[w]=core0(w)
    def stage_z(w):
        for dz in (1,2,3):
            zc[w][dz-1].wait_recv()
            xc[w,dz]=fwd(w,dz,1,r,xm)
            yc[w,dz]=fwd(w,dz,2,r,ym)
            fwd(w,dz,3,r,mate)
    def stage_xy(w):
        for dz in (1,2,3):
            xc[w,dz].wait_recv()
            rc[w,dz,0]=fwd(w,dz,6,p["rx"],ym,pl.ds(H,H))
            fwd(w,dz,4,p["rx"],mate)
            yc[w,dz].wait_recv()
            rc[w,dz,1]=fwd(w,dz,7,p["ry"],xm,pl.ds(0,H))
            fwd(w,dz,5,p["ry"],mate)
    def stage_r(w):
        for dz in (1,2,3):
            rc[w,dz,0].wait_recv()
            rc[w,dz,1].wait_recv()
            fwd(w,dz,8,p["rd"],mate)
    def from_mate(w):
        cores[w].wait_recv()
        for dz in (1,2,3):
            for kind,quarter in ((3,r),(4,p["rx"]),(5,p["ry"]),(8,p["rd"])):
                ref=piece(w,dz,quarter)
                rcopy(ref,ref,ss.at[w,kind,dz-1],rs.at[w,kind,dz-1],mate).wait_recv()
    send(0)
    ids=jnp.broadcast_to(seg_ref[...],(8,T)).astype(F32)
    segr[...]=ids[:1]
    inner=(ids==pltpu.roll(ids,1,1))&(lax.broadcasted_iota(jnp.int32,(8,T),1)>0)
    nst[...]=jnp.where(inner,1.0,0.0)[:1]
    owns=[]
    for w in range(4):
        locs[w].wait()
        cp=pltpu.make_async_copy(held[w],fulls[w].at[s],wsem.at[w]); cp.start(); owns.append(cp)
    for cp in vcs: cp.wait_recv()
    vp[...]=v_ref[...]+vz[0]+vz[1]+vz[2]
    vc=go(rcopy(vp,vm,vs.at[3],vr.at[3],mate))
    vc.wait_recv()
    vf[...]=vp[...]+vm[...]
    R=256
    gain=vf[0:1,:]; shift=vf[1:2,:]
    def norm(i,t):
        rows=pl.ds(pl.multiple_of(i*R,R),R)
        u,_=ln_unit(tok_ref[rows,:].astype(F32))
        nrm[rows,:]=(u*gain+shift).astype(BF)
        return t
    stage_z(0); send(1); send(2)
    lax.fori_loop(0,T//R,norm,0)
    local_copy(nrm,nf)
    cs[...]=jnp.zeros_like(cs)
    stage_xy(0); stage_z(1); send(3)
    stage_r(0)
    from_mate(0)
    owns[0].wait()
    S=qf.shape[0]; B=qf.shape[1]
    loads=[pltpu.make_async_copy(qf.at[t],qv.at[pl.ds(t*B,B)],qsem.at[t]) for t in range(S)]
    for cp in loads: cp.start()
    for cp in loads: cp.wait()
    def project(i,t):
        rows=pl.ds(pl.multiple_of(i*R,R),R)
        prj[rows,:]=nt(nrm[rows,:],qv[...]).astype(BF)
        return t
    half=T//R//2
    lax.fori_loop(0,half,project,0)
    stage_xy(1); stage_z(2)
    lax.fori_loop(half,T//R,project,0)
    local_copy(prj,pf)
    stage_r(1)
    def block(i,n):
        row0=i*BQ if isinstance(i,int) else pl.multiple_of(i*BQ,BQ)
        rows=pl.ds(row0,BQ)
        def put_out(off,val):
            attv[rows,pl.ds(off,128)]=val
        def put_aux(val):
            lsev[rows,:]=val
        fwd_block(row0,n,BQ,G,HP,unroll,prj,segr,nst,biasv.at[i],sigv.at[i],cs,put_out,put_aux)
    def run(i,t):
        block(i,NW)
        return t
    NB=T//BQ
    first=min(NW,NB)
    for i in range(first):
        block(i,i+1)
    stage_xy(2); stage_z(3)
    lax.fori_loop(first,NB,run,0)
    stage_r(2)
    local_copy(attv,af); local_copy(lsev,lf); local_copy(biasv,bf_); local_copy(sigv,sf)
    stage_xy(3); stage_r(3)
    for w in (1,2,3): from_mate(w)
    for cp in done: cp.wait_send()
    for cp in owns[1:]: cp.wait()
    for cp in outs: cp.wait()

def forward_all(q,o,u,d,v,tok,seg,BQ=128,G=128,unroll=6):
    S=8
    T,D=tok.shape; NW=windows(T,BQ,G); NB=T//BQ
    any_=pl.BlockSpec(memory_space=pl.ANY); vm_=pl.BlockSpec(memory_space=pltpu.VMEM)
    full=lambda a: jax.ShapeDtypeStruct((S,)+a.shape,a.dtype)
    sd=jax.ShapeDtypeStruct
    dma=pltpu.SemaphoreType.DMA
    V=pltpu.VMEM
    E=S*q.shape[0]
    outs=pl.pallas_call(functools.partial(forward_kernel,BQ,G,NW,D//128,unroll),in_specs=[any_]*4+[vm_]*3,out_specs=[any_]*4+[vm_]+[any_]*6,
      out_shape=[full(o),full(u),full(d),full(q),sd(v.shape,F32),sd((T,D),BF),sd((T,E),BF),sd((T,D),BF),sd((T,128),F32),sd((NB,BQ,NW*G),F32),sd((NB,BQ,NW*G),BF)],
      scratch_shapes=[V((E,D),BF),V((T,D),BF),V((T,E),BF),V((T,D),BF),V((T,128),F32),V((NB,BQ,NW*G),F32),V((NB,BQ,NW*G),BF),V((1,T),F32),
        V((3,)+v.shape,F32),V(v.shape,F32),V(v.shape,F32),V(q.shape,BF),V(o.shape,BF),V(u.shape,BF),V(d.shape,BF),V((1,T),F32),V((1,T),F32),
        dma((4,)),dma((4,)),dma((8,)),dma((8,)),dma((4,)),dma((4,)),dma((4,9,3)),dma((4,9,3)),dma((4,)),dma((4,))],
      compiler_params=pltpu.CompilerParams(collective_id=1,has_side_effects=True,vmem_limit_bytes=56<<20),name="forward_all")(q,o,u,d,v,tok,seg)
    return [a.reshape(-1,D) for a in outs[:4]]+list(outs[4:])

def backward_kernel(BQ,G,NW,HP,unroll,NK,
    act_h,gh_h,n2_h,cot_h,gb_h,att_h,prj_h,gatt_h,lse_h,bias_h,sig_h,nrm_h,qw_h,tok_h,gres_h,vec_ref,vg_ref,
    od,ou,oo,oq,tg_h,vo,
    gd,gu,go_,gq,cd,cu,co,cq,a1d,a1u,a1o,a1q,b1d,b1u,b1o,b1q,a2d,a2u,a2o,a2q,b2d,b2u,b2o,b2q,zd,zu,zo,zq,fd,fu,fo,fq,
    chunk,n2,cot,gb,att,prj,gatt,lse,bias,sig,qw,dk,dv,gp,ls,vb,
    csem,isem,ss,rs,cs_,cr_,vs,vr,osem):
    p=place()
    greet(p)
    r,s,c,z,x,y=p["r"],p["s"],p["c"],p["z"],p["x"],p["y"]
    mate=(r,p["mate"]); xm=(p["rx"],s); ym=(p["ry"],s)
    zdev=[(r,zpeer(p,dz)*2+c) for dz in (1,2,3)]
    T,D=n2.shape; H=D//2
    g=(gd,gu,go_,gq); cb=(cd,cu,co,cq); a1=(a1d,a1u,a1o,a1q); b1=(b1d,b1u,b1o,b1q)
    a2=(a2d,a2u,a2o,a2q); b2=(b2d,b2u,b2o,b2q); zb=(zd,zu,zo,zq); fin=(fd,fu,fo,fq); outs=(od,ou,oo,oq)
    lo=pl.ds(0,H); hi=pl.ds(H,H)
    done=[]
    def go(cp):
        cp.start(); done.append(cp); return cp
    ins={}
    def load(name,src,dst):
        ins[name]=pltpu.make_async_copy(src,dst,isem.at[len(ins)]); ins[name].start()
    cp_={}
    loc={}
    def acc(k): return g[k].at[:,c]
    def C(k,zz):
        cp_[k,"c",zz]=go(rcopy(g[k].at[zz,1-c],cb[k].at[zz],cs_.at[k,zz],cr_.at[k,zz],mate))
    def X(k):
        a=acc(k)
        for zz in range(4): cp_[k,"c",zz].wait_recv()
        def add(i,t):
            a[i]=a[i]+cb[k][i]
            return t
        lax.fori_loop(0,4,add,0)
        for yy in range(2):
            cp_[k,1+yy]=go(rcopy(a.at[:,yy*2+1-x,:,lo],a1[k].at[:,yy],ss.at[k,1+yy],rs.at[k,1+yy],xm))
        cp_[k,3]=go(rcopy(a.at[:,pl.ds((1-y)*2,2),:,hi],b1[k],ss.at[k,3],rs.at[k,3],ym))
    def Y(k):
        a=acc(k)
        cp_[k,1].wait_recv(); cp_[k,2].wait_recv(); cp_[k,3].wait_recv()
        def add(i,t):
            for yy in range(2):
                a[i,yy*2+x,:,lo]=a[i,yy*2+x,:,lo]+a1[k][i,yy]
            for xx in range(2):
                a[i,y*2+xx,:,hi]=a[i,y*2+xx,:,hi]+b1[k][i,xx]
            return t
        lax.fori_loop(0,4,add,0)
        cp_[k,4]=go(rcopy(a.at[:,(1-y)*2+x,:,lo],a2[k],ss.at[k,4],rs.at[k,4],ym))
        cp_[k,5]=go(rcopy(a.at[:,y*2+1-x,:,hi],b2[k],ss.at[k,5],rs.at[k,5],xm))
    def Z(k):
        a=acc(k)
        cp_[k,4].wait_recv(); cp_[k,5].wait_recv()
        def add(i,t):
            a[i,r,:,lo]=a[i,r,:,lo]+a2[k][i]
            a[i,r,:,hi]=a[i,r,:,hi]+b2[k][i]
            return t
        lax.fori_loop(0,4,add,0)
        for dz in (1,2,3):
            cp_[k,5+dz]=go(rcopy(a.at[zpeer(p,dz),r],zb[k].at[dz-1],ss.at[k,5+dz],rs.at[k,5+dz],zdev[dz-1]))
    def Fn(k):
        for dz in (1,2,3): cp_[k,5+dz].wait_recv()
        t=acc(k)[z,r].astype(F32)
        for dz in range(3): t=t+zb[k][dz].astype(F32)
        fin[k][r]=t.astype(BF)
        cp_[k,9]=go(rcopy(fin[k].at[r],fin[k].at[r],ss.at[k,9],rs.at[k,9],xm))
        cp_[k,10]=go(rcopy(fin[k].at[r],fin[k].at[r],ss.at[k,10],rs.at[k,10],ym))
    def Gn(k):
        cp_[k,9].wait_recv()
        cp_[k,11]=go(rcopy(fin[k].at[p["rx"],:,hi],fin[k].at[p["rx"],:,hi],ss.at[k,11],rs.at[k,11],ym))
        cp_[k,10].wait_recv()
        cp_[k,12]=go(rcopy(fin[k].at[p["ry"],:,lo],fin[k].at[p["ry"],:,lo],ss.at[k,12],rs.at[k,12],xm))
    def Hn(k):
        cp_[k,11].wait_recv(); cp_[k,12].wait_recv()
        loc[k]=pltpu.make_async_copy(fin[k],outs[k],osem.at[k]); loc[k].start()
    zz0=(z//2)*2
    vdev=[mate,xm,ym,(r,(zz0+1-z%2)*2+c),(r,((z+2)%4)*2+c)]
    def V(n):
        if n>0:
            cp_["v",n-1].wait_recv()
            vb[2*n]=vb[2*n-2]+vb[2*n-1]
        if n<5:
            cp_["v",n]=go(rcopy(vb.at[2*n],vb.at[2*n+1],vs.at[n],vr.at[n],vdev[n]))
        else:
            vo[...]=vb[10]
    load("cot",cot_h,cot)
    WC=chunk.shape[2]
    order=[(w,half,zz) for w in range(2) for half in range(2) for zz in range(4)]
    def fetch(n):
        w,half,zz=order[n]
        cc=(1-c) if half==0 else c
        src=(act_h,gh_h)[w].at[:,pl.ds(pl.multiple_of((zz*2+cc)*WC,128),WC)]
        return pltpu.make_async_copy(src,chunk.at[n%2],csem.at[n%2])
    fetch(0).start()
    fetch(1).start()
    load("n2",n2_h,n2); load("gb",gb_h,gb); load("att",att_h,att); load("prj",prj_h,prj); load("gatt",gatt_h,gatt)
    load("lse",lse_h,lse); load("bias",bias_h,bias); load("sig",sig_h,sig); load("qw",qw_h,qw)
    ins["cot"].wait()
    for n,(w,half,zz) in enumerate(order):
        fetch(n).wait()
        if n==8: ins["n2"].wait()
        cc=(1-c) if half==0 else c
        res=tn(chunk[n%2],(cot,n2)[w][...])
        q4=WC//4
        for k in range(4):
            g[w][zz,cc,k]=res[k*q4:(k+1)*q4].astype(BF)
        if n+2<len(order): fetch(n+2).start()
        if half==0: C(w,zz)
        if n==7: X(0)
    ins["gb"].wait(); ins["att"].wait()
    res=tn(att[...],gb[...])
    q4=D//32
    for sh in range(8):
        for k in range(4):
            at=sh*(D//8)+k*q4
            go_[sh//2,sh%2,k]=res[at:at+q4].astype(BF)
    for zz in range(4): C(2,zz)
    for name in ("prj","gatt","lse","bias","sig"): ins[name].wait()
    load("nrm",nrm_h,n2); load("tok",tok_h,cot)
    dk[...]=jnp.zeros_like(dk)
    dv[...]=jnp.zeros_like(dv)
    ls[...]=jnp.zeros_like(ls)
    def block(i,n):
        row0=i*BQ if isinstance(i,int) else pl.multiple_of(i*BQ,BQ)
        rows=pl.ds(row0,BQ)
        bwd_block(row0,n,BQ,G,HP,unroll,prj,gatt.at[rows],att.at[rows],lse.at[rows],bias.at[i],sig.at[i],prj,dk,dv,gp,ls)
    NB=T//BQ
    first=min(NW-1,NB)
    def run(t,u):
        block(NB-1-t,NW)
        return u
    block(NB-1,NW)
    Y(0); X(1); X(2)
    lax.fori_loop(1,NB-1-first,run,0)
    Z(0)
    block(first,NW)
    events=[lambda: None, lambda: (Y(1),Y(2)), lambda: None, lambda: None]
    for t,i in enumerate(range(first-1,-1,-1)):
        block(i,i+1)
        events[t]()
    prj[:,D:2*D]=dk[...].astype(BF)
    prj[:,2*D:]=dv[...].astype(BF)
    load("gres",gres_h,dk)
    ins["nrm"].wait()
    E2=prj.shape[1]//2; q4=gq.shape[3]
    for part in range(2):
        for h in range(2):
            res=tn(prj[:,part*E2:(part+1)*E2],n2[:,h*H:(h+1)*H])
            for blk in range(E2//q4):
                sh=part*4+blk//4
                gq[sh//2,sh%2,blk%4,:,h*H:(h+1)*H]=res[blk*q4:(blk+1)*q4].astype(BF)
        for zz in (part*2,part*2+1): C(3,zz)
        if part==0: Fn(0)
    Z(1); Z(2)
    X(3)
    ins["tok"].wait(); ins["qw"].wait(); ins["gres"].wait()
    vb[0]=vg_ref[...]
    R=256
    gain=vec_ref[0:1,:]
    def dgrad(i,t):
        rows=pl.ds(pl.multiple_of(i*R,R),R)
        gn=nn(prj[rows,:],qw[...])
        u,rstd=ln_unit(cot[rows,:].astype(F32))
        vb[0,0:1,:]=vb[0,0:1,:]+jnp.sum(gn*u,axis=0,keepdims=True)
        vb[0,1:2,:]=vb[0,1:2,:]+jnp.sum(gn,axis=0,keepdims=True)
        gg=gn*gain
        gb[rows,:]=(dk[rows,:]+rstd*(gg-rowmean(gg)-u*rowmean(gg*u))).astype(BF)
        return t
    lax.fori_loop(0,T//R//2,dgrad,0)
    Gn(0)
    lax.fori_loop(T//R//2,T//R,dgrad,0)
    out_cp=pltpu.make_async_copy(gb,tg_h,osem.at[4]); out_cp.start()
    Y(3); V(0); Z(3); V(1); Fn(1); V(2); Fn(2); Hn(0); V(3); Gn(1); V(4); Gn(2)
    V(5); Fn(3); Hn(1); Hn(2); Gn(3); Hn(3)
    for cp in done: cp.wait_send()
    for k in range(4): loc[k].wait()
    out_cp.wait()

def backward_all(act,gh,n2,cot,gb,att,prj,gatt,lse,bias,sig,nrm,qw,tok,gres,vec,vg,BQ=128,G=128,unroll=5):
    T,D=tok.shape; F=act.shape[1]; E=prj.shape[1]; NB=T//BQ; NW=bias.shape[2]//G
    any_=pl.BlockSpec(memory_space=pl.ANY); vm_=pl.BlockSpec(memory_space=pltpu.VMEM)
    dma=pltpu.SemaphoreType.DMA; V=pltpu.VMEM; sd=jax.ShapeDtypeStruct
    Qs=[F//32,F//32,D//32,E//32]; H=D//2
    scr=[V((4,2,4,q,D),BF) for q in Qs]+[V((4,4,q,D),BF) for q in Qs]+[V((4,2,q,H),BF) for q in Qs]+[V((4,2,q,H),BF) for q in Qs]
    scr+=[V((4,q,H),BF) for q in Qs]+[V((4,q,H),BF) for q in Qs]+[V((3,q,D),BF) for q in Qs]+[V((4,q,D),BF) for q in Qs]
    scr+=[V((2,T,F//8),BF)]+[V((T,D),BF)]*4+[V((T,E),BF),V((T,D),BF),V((T,128),F32),V(bias.shape,F32),V(sig.shape,BF),V((E,D),BF)]
    scr+=[V((T,D),F32)]*2+[V((BQ,NW*G),F32),V((1,T),F32),V((11,8,D),F32)]
    scr+=[dma((2,)),dma((14,)),dma((4,13)),dma((4,13)),dma((4,4)),dma((4,4)),dma((5,)),dma((5,)),dma((5,))]
    outs=pl.pallas_call(functools.partial(backward_kernel,BQ,G,NW,D//128,unroll,0),in_specs=[any_]*15+[vm_]*2,out_specs=[any_]*5+[vm_],
      out_shape=[sd((4,q,D),BF) for q in Qs]+[sd((T,D),BF),sd((8,D),F32)],scratch_shapes=scr,
      compiler_params=pltpu.CompilerParams(collective_id=2,has_side_effects=True,vmem_limit_bytes=63<<20),name="backward_all")(act,gh,n2,cot,gb,att,prj,gatt,lse,bias,sig,nrm,qw,tok,gres,vec,vg)
    return [a.reshape(-1,D) for a in outs[:4]],outs[4],outs[5]


def gather(x):
    return lax.all_gather(x, "shard", axis=0, tiled=True)


def forward_plain(q, o, u, d, v, tok, segr, nst, nblk):
    q, o, u, d = gather(q), gather(o), gather(u), gather(d)
    vec = lax.psum(v, "shard")
    normed, projected = qkv_proj(tok, q, vec)
    return [o, u, d, q, vec, normed, projected] + list(attn_fwd(projected, segr, nst, nblk))


def backward_plain(act, gh, n2, cot, gb, att, prj, gatt, lse, bias, sig, nrm, qw, tok, gres, vec, vg, nblk):
    def one(g):
        part = lax.psum_scatter(g, "shard", scatter_dimension=0, tiled=True)
        return lax.psum(part, "rep")

    gproj = attn_bwd(prj, gatt, att, lse, bias, sig, nblk)
    tgrad, vec1 = qkv_dgrad(gproj, qw, tok, gres, vec)
    gs = [weight_grad(act, cot), weight_grad(gh, n2), weight_grad(att, gb), weight_grad(gproj, nrm)]
    total = jnp.concatenate([vec1[:2], vg[2:]], axis=0)
    return [one(g) for g in gs], tgrad, lax.psum(total, ("rep", "shard"))


def local(tokens, segment_ids, qkv_weight, out_weight, up_weight, down_weight,
          norm1_gain, norm1_shift, norm2_gain, norm2_shift, cotangent):
    tok = tokens[0]
    cot = cotangent[0]
    seg = segment_ids[0]
    model = tok.shape[1]
    known = lax.axis_size("rep") == 4 and lax.axis_size("shard") == 8
    piece = norm1_gain.shape[0]
    at = lax.axis_index("shard") * piece
    vec_part = jnp.stack([norm1_gain, norm1_shift, norm2_gain, norm2_shift]).astype(F32)
    vec_mine = lax.dynamic_update_slice(jnp.zeros((8, model), F32), vec_part, (0, at))
    segr, nst, nblk = prep(seg)
    parts = (qkv_weight.T, out_weight, up_weight.T, down_weight, vec_mine, tok)
    held = forward_all(*parts, segment_ids) if known else forward_plain(*parts, segr, nst, nblk)
    out_full, up_t, down_full, qkv_t, vec, normed, projected, attended, lse, bias, sig = held
    output, gres, gatt, act, gh, n2, gb, vg = mlp(tok, attended, cot, out_full, up_t, down_full, vec)
    parts = (act, gh, n2, cot, gb, attended, projected, gatt, lse, bias, sig, normed, qkv_t, tok, gres, vec, vg)
    grads, tgrad, vec_sum = backward_all(*parts) if known else backward_plain(*parts, nblk)
    down_grad, up_grad, out_grad, qkv_grad = [g.astype(F32) for g in grads]
    mine = lax.dynamic_slice_in_dim(vec_sum, at, piece, 1)
    return (output[None], tgrad[None], qkv_grad.T, out_grad, up_grad.T, down_grad,
            mine[0], mine[1], mine[2], mine[3])


def solution(mesh):
    seq = P(("rep", "shard"), None, None)
    cols, rows, vecs = P(None, "shard"), P("shard", None), P("shard")
    return jax.shard_map(
        local,
        mesh=mesh,
        in_specs=(seq, P(("rep", "shard"), None), cols, rows, cols, rows, vecs, vecs, vecs, vecs, seq),
        out_specs=(seq, seq, cols, rows, cols, rows, vecs, vecs, vecs, vecs),
        check_vma=False,
    )
```

```python
import functools

import jax
import jax.numpy as jnp
from jax import lax
from jax.experimental import pallas as pl
from jax.experimental.pallas import tpu as pltpu
from jax.sharding import PartitionSpec as P

F32 = jnp.float32
BF = jnp.bfloat16
NEG=-1e30
WIN=512
def nt(a,b):
    return lax.dot_general(a,b,(((1,),(1,)),((),())),preferred_element_type=F32)
def nn(a,b):
    return lax.dot_general(a,b,(((1,),(0,)),((),())),preferred_element_type=F32)
def tn(a,b):
    return lax.dot_general(a,b,(((0,),(0,)),((),())),preferred_element_type=F32)
def split2(x):
    hi=x.astype(BF)
    lo=(x-hi.astype(F32)).astype(BF)
    return hi,lo
def eighth(x):
    return x*jnp.asarray(0.125,BF)

def fwd_block(row0,n,BQ,G,HP,unroll,qkv,segr,nst,bias,sig,cs,put_out,put_aux):
    D=HP*128
    W=n*G
    k0=row0+BQ-W
    if not isinstance(k0,int): k0=pl.multiple_of(k0,G)
    kw=pl.ds(k0,W); rows=pl.ds(row0,BQ)
    lane=lax.broadcasted_iota(jnp.int32,(BQ,128),1)
    left=lane<64
    same=jnp.broadcast_to(segr[:,rows],(128,BQ)).T[:,:1]==segr[:,kw]
    qi=lax.broadcasted_iota(jnp.int32,(BQ,W),0)+(W-BQ)
    ki=lax.broadcasted_iota(jnp.int32,(BQ,W),1)
    allowed=same&(ki<=qi)
    chosen=same&(ki<qi)&(nst[:,kw]>0)
    q=eighth(qkv[rows,pl.ds(0,128)])
    k=qkv[kw,pl.ds(D,128)]
    s0=nt(jnp.where(left,q,jnp.zeros_like(q)),k)
    e=jnp.exp(-jnp.abs(s0))
    sp=jnp.maximum(s0,0.0)+jnp.log1p(e)
    sg=jnp.where(s0>=0,1.0,e)/(1.0+e)
    sel=jnp.where(chosen,sp,0.0)
    sig[:,sig.shape[1]-W:]=jnp.where(chosen,sg,0.0).astype(BF)
    hi,lo=split2(sel)
    ri=lax.broadcasted_iota(jnp.int32,(BQ,BQ),0); ci=lax.broadcasted_iota(jnp.int32,(BQ,BQ),1)
    L=(ri>ci).astype(BF)
    pen=nn(L,hi)+nn(L,lo)+cs[:,kw]
    cs[:,kw]=cs[:,kw]+jnp.sum(sel,axis=0,keepdims=True)
    bias[:,bias.shape[1]-W:]=jnp.where(allowed,-pen,NEG)
    ones=jnp.ones((W,128),BF)
    def pair(j,acc):
        off=pl.multiple_of(j*128,128)
        q=eighth(qkv[rows,pl.ds(off,128)])
        z=jnp.zeros_like(q)
        k=qkv[kw,pl.ds(D+off,128)]
        v1=jnp.concatenate([qkv[kw,pl.ds(2*D+off,128)],ones],axis=1)
        b=bias[:,bias.shape[1]-W:]
        outs=[]
        for hh in range(2):
            qm=jnp.where(left,q,z) if hh==0 else jnp.where(left,z,q)
            s=nt(qm,k)+b
            m=jnp.max(s,axis=1,keepdims=True)
            p=jnp.exp(s-m)
            ol=nn(p.astype(BF),v1)
            l=ol[:,128:]
            outs.append(ol[:,:128]*(1.0/l))
            acc=jnp.where(lane==2*j+hh,m+jnp.log(l),acc)
        put_out(off,jnp.where(left,outs[0],outs[1]).astype(BF))
        return acc
    lse=lax.fori_loop(0,HP,pair,jnp.zeros((BQ,128),F32),unroll=unroll)
    put_aux(lse)

def attn_fwd_kernel(BQ,G,NW,HP,unroll,nblk_ref,qkv_ref,segr_ref,nst_ref,o_ref,aux_ref,bias_ref,sig_ref,cs_ref):
    i=pl.program_id(0)
    @pl.when(i==0)
    def _():
        cs_ref[...]=jnp.zeros_like(cs_ref)
    row0=pl.multiple_of(i*BQ,BQ)
    def put_out(off,val):
        o_ref[:,pl.ds(off,128)]=val
    def put_aux(val):
        aux_ref[...]=val
    for n in range(1,NW+1):
        @pl.when(nblk_ref[i]==n)
        def _(n=n):
            fwd_block(row0,n,BQ,G,HP,unroll,qkv_ref,segr_ref,nst_ref,bias_ref.at[0],sig_ref.at[0],cs_ref,put_out,put_aux)

def windows(T,BQ,G):
    return min(T//G,-(-(WIN-1+BQ)//G))

def attn_fwd(qkv,segr,nst,nblk,BQ=128,G=128,unroll=6):
    T,D3=qkv.shape; D=D3//3; HP=D//128
    NW=windows(T,BQ,G)
    NB=T//BQ
    whole=lambda shape: pl.BlockSpec(shape,lambda i,*_:(0,0),pipeline_mode=pl.Buffered(1))
    gs=pltpu.PrefetchScalarGridSpec(num_scalar_prefetch=1,grid=(NB,),
      in_specs=[whole((T,D3)),whole((1,T)),whole((1,T))],
      out_specs=[pl.BlockSpec((BQ,D),lambda i,*_:(i,0)),pl.BlockSpec((BQ,128),lambda i,*_:(i,0)),
        pl.BlockSpec((1,BQ,NW*G),lambda i,*_:(i,0,0)),pl.BlockSpec((1,BQ,NW*G),lambda i,*_:(i,0,0))],
      scratch_shapes=[pltpu.VMEM((1,T),F32)])
    return pl.pallas_call(functools.partial(attn_fwd_kernel,BQ,G,NW,HP,unroll),grid_spec=gs,
      out_shape=[jax.ShapeDtypeStruct((T,D),BF),jax.ShapeDtypeStruct((T,128),F32),
        jax.ShapeDtypeStruct((NB,BQ,NW*G),F32),jax.ShapeDtypeStruct((NB,BQ,NW*G),BF)],
      compiler_params=pltpu.CompilerParams(vmem_limit_bytes=40<<20),name="attn_fwd")(nblk,qkv,segr,nst)

def bwd_block(row0,n,BQ,G,HP,unroll,qkv,do_ref,o_ref,aux_ref,bias,sig,dq_ref,dk_ref,dv_ref,gp_ref,ls_ref):
    D=HP*128
    W=n*G
    k0=row0+BQ-W
    if not isinstance(k0,int): k0=pl.multiple_of(k0,G)
    kw=pl.ds(k0,W); rows=pl.ds(row0,BQ)
    lane=lax.broadcasted_iota(jnp.int32,(BQ,128),1)
    left=lane<64
    gp_ref[:,:W]=jnp.zeros((BQ,W),F32)
    lse=aux_ref[...]
    def stack(t):
        z=jnp.zeros_like(t)
        return jnp.concatenate([jnp.where(left,t,z),jnp.where(left,z,t)],axis=0)
    def work(j,first):
        off=j*128 if isinstance(j,int) else pl.multiple_of(j*128,128)
        k=qkv[kw,pl.ds(D+off,128)]
        v=qkv[kw,pl.ds(2*D+off,128)]
        do=do_ref[:,pl.ds(off,128)]
        prod=do.astype(F32)*o_ref[:,pl.ds(off,128)].astype(F32)
        b=bias[:,bias.shape[1]-W:]
        q2=stack(eighth(qkv[rows,pl.ds(off,128)]))
        do2=stack(do)
        def row(t0,t1):
            return jnp.sum(t0,axis=1,keepdims=True),jnp.sum(t1,axis=1,keepdims=True)
        l0,l1=row(jnp.where(lane==2*j,lse,0.0),jnp.where(lane==2*j+1,lse,0.0))
        e0,e1=row(jnp.where(left,prod,0.0),jnp.where(left,0.0,prod))
        s2=nt(q2,k)
        dp2=nt(do2,v)
        p0=jnp.exp(s2[:BQ]+b-l0); p1=jnp.exp(s2[BQ:]+b-l1)
        ds0=p0*(dp2[:BQ]-e0); ds1=p1*(dp2[BQ:]-e1)
        if not first:
            gp_ref[:,:W]=gp_ref[:,:W]+(ds0+ds1)
        else:
            gp=gp_ref[:,:W]+(ds0+ds1)
            hi,lo=split2(gp)
            ri=lax.broadcasted_iota(jnp.int32,(BQ,BQ),0); ci=lax.broadcasted_iota(jnp.int32,(BQ,BQ),1)
            U=(ci>ri).astype(BF)
            gsel=nn(U,hi)+nn(U,lo)+ls_ref[:,kw]
            ls_ref[:,kw]=ls_ref[:,kw]+jnp.sum(gp,axis=0,keepdims=True)
            ds0=ds0-gsel*sig[:,sig.shape[1]-W:].astype(F32)
        dsb=jnp.concatenate([ds0.astype(BF),ds1.astype(BF)],axis=0)
        pb=jnp.concatenate([p0.astype(BF),p1.astype(BF)],axis=0)
        dq2=nn(dsb,k)
        dq_ref[rows,pl.ds(off,128)]=(jnp.where(left,dq2[:BQ],dq2[BQ:])*0.125).astype(BF)
        dk_ref[kw,pl.ds(off,128)]+=tn(dsb,q2)
        dv_ref[kw,pl.ds(off,128)]+=tn(pb,do2)
    def body(j,c):
        work(j,False)
        return c
    lax.fori_loop(1,HP,body,0,unroll=unroll)
    work(0,True)

def attn_bwd_kernel(BQ,G,NW,HP,unroll,NB,nblk_ref,qkv_ref,do_ref,o_ref,aux_ref,bias_ref,sig_ref,out_ref,dk_ref,dv_ref,gp_ref,ls_ref):
    step=pl.program_id(0)
    i=NB-1-step
    D=HP*128
    @pl.when(step==0)
    def _():
        dk_ref[...]=jnp.zeros_like(dk_ref)
        dv_ref[...]=jnp.zeros_like(dv_ref)
        ls_ref[...]=jnp.zeros_like(ls_ref)
    row0=pl.multiple_of(i*BQ,BQ)
    for n in range(1,NW+1):
        @pl.when(nblk_ref[i]==n)
        def _(n=n):
            bwd_block(row0,n,BQ,G,HP,unroll,qkv_ref,do_ref,o_ref,aux_ref,bias_ref.at[0],sig_ref.at[0],out_ref,dk_ref,dv_ref,gp_ref,ls_ref)
    @pl.when(step==NB-1)
    def _():
        out_ref[:,D:2*D]=dk_ref[...].astype(BF)
        out_ref[:,2*D:]=dv_ref[...].astype(BF)

def attn_bwd(qkv,do,o,aux,bias,sig,nblk,BQ=128,G=128,unroll=5):
    T,D3=qkv.shape; D=D3//3; HP=D//128
    NW=bias.shape[2]//G
    NB=T//BQ
    whole=lambda shape: pl.BlockSpec(shape,lambda i,*_:(0,0),pipeline_mode=pl.Buffered(1))
    rb=lambda w: pl.BlockSpec((BQ,w),lambda i,*_:(NB-1-i,0))
    r3=pl.BlockSpec((1,BQ,NW*G),lambda i,*_:(NB-1-i,0,0))
    gs=pltpu.PrefetchScalarGridSpec(num_scalar_prefetch=1,grid=(NB,),
      in_specs=[whole((T,D3)),rb(D),rb(D),rb(128),r3,r3],
      out_specs=whole((T,D3)),
      scratch_shapes=[pltpu.VMEM((T,D),F32),pltpu.VMEM((T,D),F32),pltpu.VMEM((BQ,NW*G),F32),pltpu.VMEM((1,T),F32)])
    return pl.pallas_call(functools.partial(attn_bwd_kernel,BQ,G,NW,HP,unroll,NB),grid_spec=gs,
      out_shape=jax.ShapeDtypeStruct((T,D3),BF),
      compiler_params=pltpu.CompilerParams(vmem_limit_bytes=50<<20),name="attn_bwd")(nblk,qkv,do,o,aux,bias,sig)

def prep(seg,BQ=128,G=128):
    T=seg.shape[0]
    NB=T//BQ
    at=seg[::BQ]
    first=jnp.sum((seg[None,:]<at[:,None]).astype(jnp.int32),axis=1)
    ends=(jnp.arange(NB,dtype=jnp.int32)+1)*BQ
    nblk=(ends-(first//G)*G)//G
    starts=jnp.concatenate([jnp.ones((1,),bool),seg[1:]!=seg[:-1]])
    nst=jnp.logical_not(starts).astype(jnp.int32)[None,:]
    return seg[None,:].astype(F32),nst,nblk

EPS=1e-5
GC=0.7978845608028654; GA=0.044715
def rowmean(x): return jnp.mean(x,axis=-1,keepdims=True)
def ln_unit(x):
    m=rowmean(x); c=x-m; v=rowmean(c*c); r=lax.rsqrt(v+EPS)
    return c*r, r

def qkv_kernel(tok_ref,w_ref,vec_ref,n_ref,o_ref):
    u,_=ln_unit(tok_ref[...].astype(F32))
    n=(u*vec_ref[0:1,:]+vec_ref[1:2,:]).astype(BF)
    n_ref[...]=n
    o_ref[...]=nt(n,w_ref[...]).astype(BF)
def qkv_proj(tok,wT,vec,R=256):
    T,D=tok.shape; E=wT.shape[0]
    c=lambda s: pl.BlockSpec(s,lambda i:(0,0),pipeline_mode=pl.Buffered(1))
    return pl.pallas_call(qkv_kernel,grid=(T//R,),in_specs=[pl.BlockSpec((R,D),lambda i:(i,0)),c((E,D)),c(vec.shape)],
      out_specs=[pl.BlockSpec((R,D),lambda i:(i,0)),pl.BlockSpec((R,E),lambda i:(i,0))],
      out_shape=[jax.ShapeDtypeStruct((T,D),BF),jax.ShapeDtypeStruct((T,E),BF)],
      compiler_params=pltpu.CompilerParams(vmem_limit_bytes=40<<20),name="qkv_proj")(tok,wT,vec)

def mlp_kernel(NC,C,tok_ref,att_ref,cot_ref,ow_ref,up_ref,dn_ref,vec_ref,
    out_ref,gres_ref,gatt_ref,act_ref,gh_ref,n2_ref,gb_ref,vg_ref):
    i=pl.program_id(0)
    gain=vec_ref[2:3,:]; shift=vec_ref[3:4,:]
    res=tok_ref[...].astype(F32)+nn(att_ref[...],ow_ref[...])
    u,rstd=ln_unit(res)
    n2=(u*gain+shift).astype(BF)
    n2_ref[...]=n2
    cot=cot_ref[...]
    out_acc=res
    g_acc=jnp.zeros_like(res)
    for c in range(NC):
        cs=slice(c*C,(c+1)*C)
        h=nt(n2,up_ref[cs,:])
        h2=h*h
        t=jnp.tanh(h*(GC+GC*GA*h2))
        half=0.5*(1.0+t)
        act=(h*half).astype(BF)
        act_ref[:,cs]=act
        ga=nt(cot,dn_ref[cs,:])
        dg=half+(0.5*h)*(1.0-t*t)*(GC+3.0*GC*GA*h2)
        gh=(ga*dg).astype(BF)
        gh_ref[:,cs]=gh
        out_acc=out_acc+nn(act,dn_ref[cs,:])
        g_acc=g_acc+nn(gh,up_ref[cs,:])
    out_ref[...]=out_acc.astype(BF)
    @pl.when(i==0)
    def _():
        vg_ref[...]=jnp.zeros_like(vg_ref)
    vg_ref[2:3,:]+=jnp.sum(g_acc*u,axis=0,keepdims=True)
    vg_ref[3:4,:]+=jnp.sum(g_acc,axis=0,keepdims=True)
    g=g_acc*gain
    gr=cot.astype(F32)+rstd*(g-rowmean(g)-u*rowmean(g*u))
    gres_ref[...]=gr
    gb=gr.astype(BF)
    gb_ref[...]=gb
    gatt_ref[...]=nt(gb,ow_ref[...]).astype(BF)
def mlp(tok,att,cot,ow,upT,dn,vec,R=256,C=768):
    T,D=tok.shape; F=upT.shape[0]
    c=lambda s: pl.BlockSpec(s,lambda i:(0,0),pipeline_mode=pl.Buffered(1))
    rb=lambda w: pl.BlockSpec((R,w),lambda i:(i,0))
    sd=jax.ShapeDtypeStruct
    return pl.pallas_call(functools.partial(mlp_kernel,F//C,C),grid=(T//R,),
      in_specs=[rb(D),rb(D),rb(D),c((D,D)),c((F,D)),c((F,D)),c(vec.shape)],
      out_specs=[rb(D),rb(D),rb(D),rb(F),rb(F),rb(D),rb(D),c((8,D))],
      out_shape=[sd((T,D),BF),sd((T,D),F32),sd((T,D),BF),sd((T,F),BF),sd((T,F),BF),sd((T,D),BF),sd((T,D),BF),sd((8,D),F32)],
      compiler_params=pltpu.CompilerParams(vmem_limit_bytes=56<<20),name="mlp")(tok,att,cot,ow,upT,dn,vec)

def wg_kernel(gp_ref,n_ref,o_ref):
    o_ref[...]=tn(gp_ref[...],n_ref[...]).astype(BF)
def weight_grad(gp,n1,WC=384):
    T,E=gp.shape; D=n1.shape[1]
    return pl.pallas_call(wg_kernel,grid=(E//WC,),in_specs=[pl.BlockSpec((T,WC),lambda i:(0,i)),pl.BlockSpec((T,D),lambda i:(0,0),pipeline_mode=pl.Buffered(1))],
      out_specs=pl.BlockSpec((WC,D),lambda i:(i,0)),out_shape=jax.ShapeDtypeStruct((E,D),BF),
      compiler_params=pltpu.CompilerParams(vmem_limit_bytes=40<<20),name="weight_grad")(gp,n1)
def dg_kernel(gp_ref,w_ref,tok_ref,gres_ref,vec_ref,o_ref,vg_ref):
    i=pl.program_id(0)
    gn=nn(gp_ref[...],w_ref[...])
    u,rstd=ln_unit(tok_ref[...].astype(F32))
    @pl.when(i==0)
    def _():
        vg_ref[...]=jnp.zeros_like(vg_ref)
    vg_ref[0:1,:]+=jnp.sum(gn*u,axis=0,keepdims=True)
    vg_ref[1:2,:]+=jnp.sum(gn,axis=0,keepdims=True)
    g=gn*vec_ref[0:1,:]
    o_ref[...]=(gres_ref[...]+rstd*(g-rowmean(g)-u*rowmean(g*u))).astype(BF)
def qkv_dgrad(gp,wT,tok,gres,vec,R=256):
    T,E=gp.shape; D=tok.shape[1]
    c=lambda s: pl.BlockSpec(s,lambda i:(0,0),pipeline_mode=pl.Buffered(1))
    rb=lambda w: pl.BlockSpec((R,w),lambda i:(i,0))
    return pl.pallas_call(dg_kernel,grid=(T//R,),in_specs=[rb(E),c((E,D)),rb(D),rb(D),c(vec.shape)],out_specs=[rb(D),c((8,D))],
      out_shape=[jax.ShapeDtypeStruct((T,D),BF),jax.ShapeDtypeStruct((8,D),F32)],
      compiler_params=pltpu.CompilerParams(vmem_limit_bytes=40<<20),name="qkv_dgrad")(gp,wT,tok,gres,vec)

MESH=pl.DeviceIdType.MESH

def place():
    r=lax.axis_index("rep"); s=lax.axis_index("shard")
    y=r//2; x=r%2; z=s//2; c=s%2
    return dict(r=r,s=s,y=y,x=x,z=z,c=c,rx=y*2+(1-x),ry=(1-y)*2+x,rd=(1-y)*2+(1-x),mate=z*2+(1-c))
def zpeer(p,dz):
    return (p["z"]+dz)%4
def greet(p):
    bar=pltpu.get_barrier_semaphore()
    for dev in ((p["r"],p["mate"]),(p["rx"],p["s"]),(p["ry"],p["s"]))+tuple((p["r"],zpeer(p,dz)*2+p["c"]) for dz in (1,2,3)):
        pl.semaphore_signal(bar,inc=1,device_id=dev,device_id_type=MESH)
    pl.semaphore_wait(bar,6)
def rcopy(src,dst,ss,rs,dev):
    return pltpu.make_async_remote_copy(src_ref=src,dst_ref=dst,send_sem=ss,recv_sem=rs,device_id=dev,device_id_type=MESH)


def forward_kernel(BQ,G,NW,HP,unroll,q_ref,o_ref,u_ref,d_ref,v_ref,tok_ref,seg_ref,
    of,uf,df,qf,vf,nf,pf,af,lf,bf_,sf,
    qv,nrm,prj,attv,lsev,biasv,sigv,cs,vz,vp,vm,h0,h1,h2,h3,segr,nst,lsem,wsem,osem,qsem,c0s,c0r,ss,rs,vs,vr):
    p=place()
    greet(p)
    r,s,c,z=p["r"],p["s"],p["c"],p["z"]
    mate=(r,p["mate"]); xm=(p["rx"],s); ym=(p["ry"],s)
    sets=(q_ref,o_ref,u_ref,d_ref)
    fulls=(qf,of,uf,df)
    held=(h0,h1,h2,h3)
    T,D=nrm.shape
    H=D//2
    done=[]; outs=[]
    def go(cp):
        cp.start(); done.append(cp); return cp
    def local_copy(src,dst):
        cp=pltpu.make_async_copy(src,dst,osem.at[len(outs)]); cp.start(); outs.append(cp)
    def view(w,shard,first,count,cols=None):
        rows=pl.ds(pl.multiple_of(first,8),count)
        return fulls[w].at[shard,rows] if cols is None else fulls[w].at[shard,rows,cols]
    locs=[]
    for w in range(4):
        cp=pltpu.make_async_copy(sets[w],held[w],lsem.at[w]); cp.start(); locs.append(cp)
    vcs=[go(rcopy(v_ref,vz.at[dz-1],vs.at[dz-1],vr.at[dz-1],(r,zpeer(p,dz)*2+c))) for dz in (1,2,3)]
    def zsend(w):
        Q=sets[w].shape[0]//4
        rows=pl.ds(pl.multiple_of(r*Q,8),Q)
        return [go(rcopy(sets[w].at[rows],view(w,s,r*Q,Q),ss.at[w,0,dz-1],rs.at[w,0,dz-1],(r,zpeer(p,dz)*2+c))) for dz in (1,2,3)]
    def core0(w):
        return go(rcopy(sets[w],view(w,s,0,sets[w].shape[0]),c0s.at[w],c0r.at[w],mate))
    def piece(w,dz,quarter,cols=None):
        Q=sets[w].shape[0]//4
        return view(w,((z+4-dz)%4)*2+c,quarter*Q,Q,cols)
    def fwd(w,dz,kind,quarter,dev,cols=None):
        ref=piece(w,dz,quarter,cols)
        return go(rcopy(ref,ref,ss.at[w,kind,dz-1],rs.at[w,kind,dz-1],dev))
    zc={};xc={};yc={};rc={};cores={}
    def send(w):
        zc[w]=zsend(w); cores[w]=core0(w)
    def stage_z(w):
        for dz in (1,2,3):
            zc[w][dz-1].wait_recv()
            xc[w,dz]=fwd(w,dz,1,r,xm)
            yc[w,dz]=fwd(w,dz,2,r,ym)
            fwd(w,dz,3,r,mate)
    def stage_xy(w):
        for dz in (1,2,3):
            xc[w,dz].wait_recv()
            rc[w,dz,0]=fwd(w,dz,6,p["rx"],ym,pl.ds(H,H))
            fwd(w,dz,4,p["rx"],mate)
            yc[w,dz].wait_recv()
            rc[w,dz,1]=fwd(w,dz,7,p["ry"],xm,pl.ds(0,H))
            fwd(w,dz,5,p["ry"],mate)
    def stage_r(w):
        for dz in (1,2,3):
            rc[w,dz,0].wait_recv()
            rc[w,dz,1].wait_recv()
            fwd(w,dz,8,p["rd"],mate)
    def from_mate(w):
        cores[w].wait_recv()
        for dz in (1,2,3):
            for kind,quarter in ((3,r),(4,p["rx"]),(5,p["ry"]),(8,p["rd"])):
                ref=piece(w,dz,quarter)
                rcopy(ref,ref,ss.at[w,kind,dz-1],rs.at[w,kind,dz-1],mate).wait_recv()
    send(0)
    ids=jnp.broadcast_to(seg_ref[...],(8,T)).astype(F32)
    segr[...]=ids[:1]
    inner=(ids==pltpu.roll(ids,1,1))&(lax.broadcasted_iota(jnp.int32,(8,T),1)>0)
    nst[...]=jnp.where(inner,1.0,0.0)[:1]
    owns=[]
    for w in range(4):
        locs[w].wait()
        cp=pltpu.make_async_copy(held[w],fulls[w].at[s],wsem.at[w]); cp.start(); owns.append(cp)
    for cp in vcs: cp.wait_recv()
    vp[...]=v_ref[...]+vz[0]+vz[1]+vz[2]
    vc=go(rcopy(vp,vm,vs.at[3],vr.at[3],mate))
    vc.wait_recv()
    vf[...]=vp[...]+vm[...]
    R=256
    gain=vf[0:1,:]; shift=vf[1:2,:]
    def norm(i,t):
        rows=pl.ds(pl.multiple_of(i*R,R),R)
        u,_=ln_unit(tok_ref[rows,:].astype(F32))
        nrm[rows,:]=(u*gain+shift).astype(BF)
        return t
    stage_z(0); send(1); send(2)
    lax.fori_loop(0,T//R,norm,0)
    local_copy(nrm,nf)
    cs[...]=jnp.zeros_like(cs)
    stage_xy(0); stage_z(1); send(3)
    stage_r(0)
    from_mate(0)
    owns[0].wait()
    S=qf.shape[0]; B=qf.shape[1]
    loads=[pltpu.make_async_copy(qf.at[t],qv.at[pl.ds(t*B,B)],qsem.at[t]) for t in range(S)]
    for cp in loads: cp.start()
    for cp in loads: cp.wait()
    def project(i,t):
        rows=pl.ds(pl.multiple_of(i*R,R),R)
        prj[rows,:]=nt(nrm[rows,:],qv[...]).astype(BF)
        return t
    half=T//R//2
    lax.fori_loop(0,half,project,0)
    stage_xy(1); stage_z(2)
    lax.fori_loop(half,T//R,project,0)
    local_copy(prj,pf)
    stage_r(1)
    def block(i,n):
        row0=i*BQ if isinstance(i,int) else pl.multiple_of(i*BQ,BQ)
        rows=pl.ds(row0,BQ)
        def put_out(off,val):
            attv[rows,pl.ds(off,128)]=val
        def put_aux(val):
            lsev[rows,:]=val
        fwd_block(row0,n,BQ,G,HP,unroll,prj,segr,nst,biasv.at[i],sigv.at[i],cs,put_out,put_aux)
    def run(i,t):
        block(i,NW)
        return t
    NB=T//BQ
    first=min(NW,NB)
    for i in range(first):
        block(i,i+1)
    stage_xy(2); stage_z(3)
    lax.fori_loop(first,NB,run,0)
    stage_r(2)
    local_copy(attv,af); local_copy(lsev,lf); local_copy(biasv,bf_); local_copy(sigv,sf)
    stage_xy(3); stage_r(3)
    for w in (1,2,3): from_mate(w)
    for cp in done: cp.wait_send()
    for cp in owns[1:]: cp.wait()
    for cp in outs: cp.wait()

def forward_all(q,o,u,d,v,tok,seg,BQ=128,G=128,unroll=6):
    S=8
    T,D=tok.shape; NW=windows(T,BQ,G); NB=T//BQ
    any_=pl.BlockSpec(memory_space=pl.ANY); vm_=pl.BlockSpec(memory_space=pltpu.VMEM)
    full=lambda a: jax.ShapeDtypeStruct((S,)+a.shape,a.dtype)
    sd=jax.ShapeDtypeStruct
    dma=pltpu.SemaphoreType.DMA
    V=pltpu.VMEM
    E=S*q.shape[0]
    outs=pl.pallas_call(functools.partial(forward_kernel,BQ,G,NW,D//128,unroll),in_specs=[any_]*4+[vm_]*3,out_specs=[any_]*4+[vm_]+[any_]*6,
      out_shape=[full(o),full(u),full(d),full(q),sd(v.shape,F32),sd((T,D),BF),sd((T,E),BF),sd((T,D),BF),sd((T,128),F32),sd((NB,BQ,NW*G),F32),sd((NB,BQ,NW*G),BF)],
      scratch_shapes=[V((E,D),BF),V((T,D),BF),V((T,E),BF),V((T,D),BF),V((T,128),F32),V((NB,BQ,NW*G),F32),V((NB,BQ,NW*G),BF),V((1,T),F32),
        V((3,)+v.shape,F32),V(v.shape,F32),V(v.shape,F32),V(q.shape,BF),V(o.shape,BF),V(u.shape,BF),V(d.shape,BF),V((1,T),F32),V((1,T),F32),
        dma((4,)),dma((4,)),dma((8,)),dma((8,)),dma((4,)),dma((4,)),dma((4,9,3)),dma((4,9,3)),dma((4,)),dma((4,))],
      compiler_params=pltpu.CompilerParams(collective_id=1,has_side_effects=True,vmem_limit_bytes=56<<20),name="forward_all")(q,o,u,d,v,tok,seg)
    return [a.reshape(-1,D) for a in outs[:4]]+list(outs[4:])

def backward_kernel(BQ,G,NW,HP,unroll,NK,
    act_h,gh_h,n2_h,cot_h,gb_h,att_h,prj_h,gatt_h,lse_h,bias_h,sig_h,nrm_h,qw_h,tok_h,gres_h,vec_ref,vg_ref,
    od,ou,oo,oq,tg_h,vo,
    gd,gu,go_,gq,cd,cu,co,cq,a1d,a1u,a1o,a1q,b1d,b1u,b1o,b1q,a2d,a2u,a2o,a2q,b2d,b2u,b2o,b2q,zd,zu,zo,zq,fd,fu,fo,fq,
    chunk,n2,cot,gb,att,prj,gatt,lse,bias,sig,qw,dk,dv,gp,ls,vb,
    csem,isem,ss,rs,cs_,cr_,vs,vr,osem):
    p=place()
    greet(p)
    r,s,c,z,x,y=p["r"],p["s"],p["c"],p["z"],p["x"],p["y"]
    mate=(r,p["mate"]); xm=(p["rx"],s); ym=(p["ry"],s)
    zdev=[(r,zpeer(p,dz)*2+c) for dz in (1,2,3)]
    T,D=n2.shape; H=D//2
    g=(gd,gu,go_,gq); cb=(cd,cu,co,cq); a1=(a1d,a1u,a1o,a1q); b1=(b1d,b1u,b1o,b1q)
    a2=(a2d,a2u,a2o,a2q); b2=(b2d,b2u,b2o,b2q); zb=(zd,zu,zo,zq); fin=(fd,fu,fo,fq); outs=(od,ou,oo,oq)
    lo=pl.ds(0,H); hi=pl.ds(H,H)
    done=[]
    def go(cp):
        cp.start(); done.append(cp); return cp
    ins={}
    def load(name,src,dst):
        ins[name]=pltpu.make_async_copy(src,dst,isem.at[len(ins)]); ins[name].start()
    cp_={}
    loc={}
    def acc(k): return g[k].at[:,c]
    def C(k,zz):
        cp_[k,"c",zz]=go(rcopy(g[k].at[zz,1-c],cb[k].at[zz],cs_.at[k,zz],cr_.at[k,zz],mate))
    def X(k):
        a=acc(k)
        for zz in range(4):
            cp_[k,"c",zz].wait_recv()
            a[zz]=a[zz]+cb[k][zz]
        for yy in range(2):
            cp_[k,1+yy]=go(rcopy(a.at[:,yy*2+1-x,:,lo],a1[k].at[:,yy],ss.at[k,1+yy],rs.at[k,1+yy],xm))
        cp_[k,3]=go(rcopy(a.at[:,pl.ds((1-y)*2,2),:,hi],b1[k],ss.at[k,3],rs.at[k,3],ym))
    def Y(k):
        a=acc(k)
        cp_[k,1].wait_recv(); cp_[k,2].wait_recv(); cp_[k,3].wait_recv()
        def add(i,t):
            for yy in range(2):
                a[i,yy*2+x,:,lo]=a[i,yy*2+x,:,lo]+a1[k][i,yy]
            for xx in range(2):
                a[i,y*2+xx,:,hi]=a[i,y*2+xx,:,hi]+b1[k][i,xx]
            return t
        lax.fori_loop(0,4,add,0)
        cp_[k,4]=go(rcopy(a.at[:,(1-y)*2+x,:,lo],a2[k],ss.at[k,4],rs.at[k,4],ym))
        cp_[k,5]=go(rcopy(a.at[:,y*2+1-x,:,hi],b2[k],ss.at[k,5],rs.at[k,5],xm))
    def Z(k):
        a=acc(k)
        cp_[k,4].wait_recv(); cp_[k,5].wait_recv()
        def add(i,t):
            a[i,r,:,lo]=a[i,r,:,lo]+a2[k][i]
            a[i,r,:,hi]=a[i,r,:,hi]+b2[k][i]
            return t
        lax.fori_loop(0,4,add,0)
        for dz in (1,2,3):
            cp_[k,5+dz]=go(rcopy(a.at[zpeer(p,dz),r],zb[k].at[dz-1],ss.at[k,5+dz],rs.at[k,5+dz],zdev[dz-1]))
    def Fn(k):
        for dz in (1,2,3): cp_[k,5+dz].wait_recv()
        t=acc(k)[z,r].astype(F32)
        for dz in range(3): t=t+zb[k][dz].astype(F32)
        fin[k][r]=t.astype(BF)
        cp_[k,9]=go(rcopy(fin[k].at[r],fin[k].at[r],ss.at[k,9],rs.at[k,9],xm))
        cp_[k,10]=go(rcopy(fin[k].at[r],fin[k].at[r],ss.at[k,10],rs.at[k,10],ym))
    def Gn(k):
        cp_[k,9].wait_recv()
        cp_[k,11]=go(rcopy(fin[k].at[p["rx"],:,hi],fin[k].at[p["rx"],:,hi],ss.at[k,11],rs.at[k,11],ym))
        cp_[k,10].wait_recv()
        cp_[k,12]=go(rcopy(fin[k].at[p["ry"],:,lo],fin[k].at[p["ry"],:,lo],ss.at[k,12],rs.at[k,12],xm))
    def Hn(k):
        cp_[k,11].wait_recv(); cp_[k,12].wait_recv()
        loc[k]=pltpu.make_async_copy(fin[k],outs[k],osem.at[k]); loc[k].start()
    zz0=(z//2)*2
    vdev=[mate,xm,ym,(r,(zz0+1-z%2)*2+c),(r,((z+2)%4)*2+c)]
    def V(n):
        if n>0:
            cp_["v",n-1].wait_recv()
            vb[2*n]=vb[2*n-2]+vb[2*n-1]
        if n<5:
            cp_["v",n]=go(rcopy(vb.at[2*n],vb.at[2*n+1],vs.at[n],vr.at[n],vdev[n]))
        else:
            vo[...]=vb[10]
    load("cot",cot_h,cot)
    WC=chunk.shape[2]
    order=[(w,half,zz) for w in range(2) for half in range(2) for zz in range(4)]
    def fetch(n):
        w,half,zz=order[n]
        cc=(1-c) if half==0 else c
        src=(act_h,gh_h)[w].at[:,pl.ds(pl.multiple_of((zz*2+cc)*WC,128),WC)]
        return pltpu.make_async_copy(src,chunk.at[n%2],csem.at[n%2])
    fetch(0).start()
    fetch(1).start()
    load("n2",n2_h,n2); load("gb",gb_h,gb); load("att",att_h,att); load("prj",prj_h,prj); load("gatt",gatt_h,gatt)
    load("lse",lse_h,lse); load("bias",bias_h,bias); load("sig",sig_h,sig); load("qw",qw_h,qw)
    ins["cot"].wait()
    for n,(w,half,zz) in enumerate(order):
        fetch(n).wait()
        if n==8: ins["n2"].wait()
        cc=(1-c) if half==0 else c
        res=tn(chunk[n%2],(cot,n2)[w][...])
        q4=WC//4
        for k in range(4):
            g[w][zz,cc,k]=res[k*q4:(k+1)*q4].astype(BF)
        if n+2<len(order): fetch(n+2).start()
        if half==0: C(w,zz)
        if n==7: X(0)
    ins["gb"].wait(); ins["att"].wait()
    res=tn(att[...],gb[...])
    q4=D//32
    for sh in range(8):
        for k in range(4):
            at=sh*(D//8)+k*q4
            go_[sh//2,sh%2,k]=res[at:at+q4].astype(BF)
    for zz in range(4): C(2,zz)
    for name in ("prj","gatt","lse","bias","sig"): ins[name].wait()
    load("nrm",nrm_h,n2); load("tok",tok_h,cot)
    dk[...]=jnp.zeros_like(dk)
    dv[...]=jnp.zeros_like(dv)
    ls[...]=jnp.zeros_like(ls)
    def block(i,n):
        row0=i*BQ if isinstance(i,int) else pl.multiple_of(i*BQ,BQ)
        rows=pl.ds(row0,BQ)
        bwd_block(row0,n,BQ,G,HP,unroll,prj,gatt.at[rows],att.at[rows],lse.at[rows],bias.at[i],sig.at[i],prj,dk,dv,gp,ls)
    NB=T//BQ
    first=min(NW-1,NB)
    def run(t,u):
        block(NB-1-t,NW)
        return u
    block(NB-1,NW)
    Y(0); X(1); X(2)
    lax.fori_loop(1,NB-1-first,run,0)
    Z(0)
    block(first,NW)
    events=[lambda: None, lambda: (Y(1),Y(2)), lambda: None, lambda: None]
    for t,i in enumerate(range(first-1,-1,-1)):
        block(i,i+1)
        events[t]()
    prj[:,D:2*D]=dk[...].astype(BF)
    prj[:,2*D:]=dv[...].astype(BF)
    load("gres",gres_h,dk)
    ins["nrm"].wait()
    E2=prj.shape[1]//2; q4=gq.shape[3]
    for part in range(2):
        for h in range(2):
            res=tn(prj[:,part*E2:(part+1)*E2],n2[:,h*H:(h+1)*H])
            for blk in range(E2//q4):
                sh=part*4+blk//4
                gq[sh//2,sh%2,blk%4,:,h*H:(h+1)*H]=res[blk*q4:(blk+1)*q4].astype(BF)
        for zz in (part*2,part*2+1): C(3,zz)
        if part==0: Fn(0)
    Z(1); Z(2)
    X(3)
    ins["tok"].wait(); ins["qw"].wait(); ins["gres"].wait()
    vb[0]=vg_ref[...]
    R=256
    gain=vec_ref[0:1,:]
    def dgrad(i,t):
        rows=pl.ds(pl.multiple_of(i*R,R),R)
        gn=nn(prj[rows,:],qw[...])
        u,rstd=ln_unit(cot[rows,:].astype(F32))
        vb[0,0:1,:]=vb[0,0:1,:]+jnp.sum(gn*u,axis=0,keepdims=True)
        vb[0,1:2,:]=vb[0,1:2,:]+jnp.sum(gn,axis=0,keepdims=True)
        gg=gn*gain
        gb[rows,:]=(dk[rows,:]+rstd*(gg-rowmean(gg)-u*rowmean(gg*u))).astype(BF)
        return t
    lax.fori_loop(0,T//R//2,dgrad,0)
    Gn(0)
    lax.fori_loop(T//R//2,T//R,dgrad,0)
    out_cp=pltpu.make_async_copy(gb,tg_h,osem.at[4]); out_cp.start()
    Y(3); V(0); Z(3); V(1); Fn(1); V(2); Fn(2); Hn(0); V(3); Gn(1); V(4); Gn(2)
    V(5); Fn(3); Hn(1); Hn(2); Gn(3); Hn(3)
    for cp in done: cp.wait_send()
    for k in range(4): loc[k].wait()
    out_cp.wait()

def backward_all(act,gh,n2,cot,gb,att,prj,gatt,lse,bias,sig,nrm,qw,tok,gres,vec,vg,BQ=128,G=128,unroll=5):
    T,D=tok.shape; F=act.shape[1]; E=prj.shape[1]; NB=T//BQ; NW=bias.shape[2]//G
    any_=pl.BlockSpec(memory_space=pl.ANY); vm_=pl.BlockSpec(memory_space=pltpu.VMEM)
    dma=pltpu.SemaphoreType.DMA; V=pltpu.VMEM; sd=jax.ShapeDtypeStruct
    Qs=[F//32,F//32,D//32,E//32]; H=D//2
    scr=[V((4,2,4,q,D),BF) for q in Qs]+[V((4,4,q,D),BF) for q in Qs]+[V((4,2,q,H),BF) for q in Qs]+[V((4,2,q,H),BF) for q in Qs]
    scr+=[V((4,q,H),BF) for q in Qs]+[V((4,q,H),BF) for q in Qs]+[V((3,q,D),BF) for q in Qs]+[V((4,q,D),BF) for q in Qs]
    scr+=[V((2,T,F//8),BF)]+[V((T,D),BF)]*4+[V((T,E),BF),V((T,D),BF),V((T,128),F32),V(bias.shape,F32),V(sig.shape,BF),V((E,D),BF)]
    scr+=[V((T,D),F32)]*2+[V((BQ,NW*G),F32),V((1,T),F32),V((11,8,D),F32)]
    scr+=[dma((2,)),dma((14,)),dma((4,13)),dma((4,13)),dma((4,4)),dma((4,4)),dma((5,)),dma((5,)),dma((5,))]
    outs=pl.pallas_call(functools.partial(backward_kernel,BQ,G,NW,D//128,unroll,0),in_specs=[any_]*15+[vm_]*2,out_specs=[any_]*5+[vm_],
      out_shape=[sd((4,q,D),BF) for q in Qs]+[sd((T,D),BF),sd((8,D),F32)],scratch_shapes=scr,
      compiler_params=pltpu.CompilerParams(collective_id=2,has_side_effects=True,vmem_limit_bytes=63<<20),name="backward_all")(act,gh,n2,cot,gb,att,prj,gatt,lse,bias,sig,nrm,qw,tok,gres,vec,vg)
    return [a.reshape(-1,D) for a in outs[:4]],outs[4],outs[5]


def gather(x):
    return lax.all_gather(x, "shard", axis=0, tiled=True)


def forward_plain(q, o, u, d, v, tok, segr, nst, nblk):
    q, o, u, d = gather(q), gather(o), gather(u), gather(d)
    vec = lax.psum(v, "shard")
    normed, projected = qkv_proj(tok, q, vec)
    return [o, u, d, q, vec, normed, projected] + list(attn_fwd(projected, segr, nst, nblk))


def backward_plain(act, gh, n2, cot, gb, att, prj, gatt, lse, bias, sig, nrm, qw, tok, gres, vec, vg, nblk):
    def one(g):
        part = lax.psum_scatter(g, "shard", scatter_dimension=0, tiled=True)
        return lax.psum(part, "rep")

    gproj = attn_bwd(prj, gatt, att, lse, bias, sig, nblk)
    tgrad, vec1 = qkv_dgrad(gproj, qw, tok, gres, vec)
    gs = [weight_grad(act, cot), weight_grad(gh, n2), weight_grad(att, gb), weight_grad(gproj, nrm)]
    total = jnp.concatenate([vec1[:2], vg[2:]], axis=0)
    return [one(g) for g in gs], tgrad, lax.psum(total, ("rep", "shard"))


def local(tokens, segment_ids, qkv_weight, out_weight, up_weight, down_weight,
          norm1_gain, norm1_shift, norm2_gain, norm2_shift, cotangent):
    tok = tokens[0]
    cot = cotangent[0]
    seg = segment_ids[0]
    model = tok.shape[1]
    known = lax.axis_size("rep") == 4 and lax.axis_size("shard") == 8
    piece = norm1_gain.shape[0]
    at = lax.axis_index("shard") * piece
    vec_part = jnp.stack([norm1_gain, norm1_shift, norm2_gain, norm2_shift]).astype(F32)
    vec_mine = lax.dynamic_update_slice(jnp.zeros((8, model), F32), vec_part, (0, at))
    segr, nst, nblk = prep(seg)
    parts = (qkv_weight.T, out_weight, up_weight.T, down_weight, vec_mine, tok)
    held = forward_all(*parts, segment_ids) if known else forward_plain(*parts, segr, nst, nblk)
    out_full, up_t, down_full, qkv_t, vec, normed, projected, attended, lse, bias, sig = held
    output, gres, gatt, act, gh, n2, gb, vg = mlp(tok, attended, cot, out_full, up_t, down_full, vec)
    parts = (act, gh, n2, cot, gb, attended, projected, gatt, lse, bias, sig, normed, qkv_t, tok, gres, vec, vg)
    grads, tgrad, vec_sum = backward_all(*parts) if known else backward_plain(*parts, nblk)
    down_grad, up_grad, out_grad, qkv_grad = [g.astype(F32) for g in grads]
    mine = lax.dynamic_slice_in_dim(vec_sum, at, piece, 1)
    return (output[None], tgrad[None], qkv_grad.T, out_grad, up_grad.T, down_grad,
            mine[0], mine[1], mine[2], mine[3])


def solution(mesh):
    seq = P(("rep", "shard"), None, None)
    cols, rows, vecs = P(None, "shard"), P("shard", None), P("shard")
    return jax.shard_map(
        local,
        mesh=mesh,
        in_specs=(seq, P(("rep", "shard"), None), cols, rows, cols, rows, vecs, vecs, vecs, vecs, seq),
        out_specs=(seq, seq, cols, rows, cols, rows, vecs, vecs, vecs, vecs),
        check_vma=False,
    )
```
